32 devices in a mesh: seq: 32 (over z, y, x, core).
Axes of the slice: x: 2, y: 2, z: 4, core: 2. Of those that a mesh axis runs over, the one named last changes fastest.
Arguments:
- tokens: bfloat16 [2, 8192, 1024], P(None, 'seq'), may hold values from -6 to 6
- ln1_gain: bfloat16 [1024], P('seq'), may hold values from 0.5 to 1.5
- ln1_bias: bfloat16 [1024], P('seq'), may hold values from -1.75 to 1.75
- qkv_weight: bfloat16 [1024, 3072], P('seq'), may hold values from -0.1875 to 0.1875
- q_bias: bfloat16 [1024], P('seq'), may hold values from -1.75 to 1.75
- v_bias: bfloat16 [1024], P('seq'), may hold values from -1.75 to 1.75
- out_weight: bfloat16 [1024, 1024], P('seq'), may hold values from -4 to 4
- out_bias: bfloat16 [1024], P('seq'), may hold values from -1.75 to 1.75
- ln2_gain: bfloat16 [1024], P('seq'), may hold values from 0.5 to 1.5
- ln2_bias: bfloat16 [1024], P('seq'), may hold values from -1.75 to 1.75
- fc1_weight: bfloat16 [1024, 4096], P('seq'), may hold values from -0.1875 to 0.1875
- fc1_bias: bfloat16 [4096], P('seq'), may hold values from -3 to 3
- fc2_weight: bfloat16 [4096, 1024], P('seq'), may hold values from -0.125 to 0.125
- fc2_bias: bfloat16 [1024], P('seq'), may hold values from -1.75 to 1.75
- image_ids: int32 [2, 8192], P(None, 'seq'), may hold values from 0 to 14, as said below
- image_starts: int32 [2, 15], replicated, may hold values from 0 to 8191, as said below
- cotangent: bfloat16 [2, 8192, 1024], P(None, 'seq'), may hold values from -6 to 6
Outputs:
- out: bfloat16 [2, 8192, 1024], P(None, 'seq')
- input_grad: bfloat16 [2, 8192, 1024], P(None, 'seq')
- ln1_gain_grad: float32 [1024], P('seq')
- ln1_bias_grad: float32 [1024], P('seq')
- qkv_weight_grad: float32 [1024, 3072], P('seq')
- q_bias_grad: float32 [1024], P('seq')
- v_bias_grad: float32 [1024], P('seq')
- out_weight_grad: float32 [1024, 1024], P('seq')
- out_bias_grad: float32 [1024], P('seq')
- ln2_gain_grad: float32 [1024], P('seq')
- ln2_bias_grad: float32 [1024], P('seq')
- fc1_weight_grad: float32 [1024, 4096], P('seq')
- fc1_bias_grad: float32 [4096], P('seq')
- fc2_weight_grad: float32 [4096, 1024], P('seq')
- fc2_bias_grad: float32 [1024], P('seq')
The draws below stay inside these ranges and needn't reach their ends.
Inputs may be any that keep to these rules, and one draw needn't show every extreme that they name: In micro-batch m the images are contiguous runs in order: image i covers positions image_starts[m, i] to image_starts[m, i + 1] - 1 (the last one to 8191) and image_ids[m, t] names the image of position t; every image has exactly 577 tokens except one padding run, at a place drawn from the seed, of 8192 % 577 tokens. image_starts[m, 0] = 0 and the starts rise strictly; every start is a position of the stream.
All inputs are finite; a program needn't handle non-finite values.
Results may differ from the reference program's by a relative error of at most 0.013.
Values may be sent and summed in bfloat16 or wider, within the bound.
No kernel may reach another device: no remote copies, remote signals or barrier semaphores. Data moves between devices by JAX's collectives and lax.ppermute only.
A program may use at most 256 MiB of HBM per device.

```python
import math
import jax
import jax.numpy as jnp
from jax import lax

D = 1024
HEADS = 16
HEAD_DIM = 64
FF = 4096
IMG_TOK = 577
MB = 2
MB_TOK = 8192
IMAGES = 15


def image_lengths(key):
    full_count = MB_TOK // IMG_TOK
    spare_tokens = MB_TOK - full_count * IMG_TOK
    image_slots = jnp.arange(IMAGES, dtype=jnp.int32)
    length_rows = []
    for micro_index in range(MB):
        local_key = jax.random.fold_in(jax.random.fold_in(key, 4099), micro_index)
        chosen = jax.random.randint(local_key, (), 0, IMAGES, dtype=jnp.int32)
        length_rows.append(jnp.where(image_slots == chosen, spare_tokens, IMG_TOK).astype(jnp.int32))
    return jnp.stack(length_rows)


def draw_image_starts(key, part):
    lengths = image_lengths(key)
    return (jnp.cumsum(lengths, axis=1) - lengths).astype(jnp.int32)


def draw_image_ids(key, part):
    starts = draw_image_starts(key, part)
    rows_index = jnp.arange(MB, dtype=jnp.int32)[:, None]
    marks = jnp.zeros((MB, MB_TOK), jnp.int32).at[rows_index, starts].add(1)
    return (jnp.cumsum(marks, axis=1) - 1).astype(jnp.int32)


def shard_levels(key, dims, pieces, smallest, high):
    level, own = 1.0, jax.random.fold_in(key, 6)
    for position, shards_of in pieces:
        steps = jnp.exp(jax.random.uniform(jax.random.fold_in(own, position), (shards_of,), jnp.float32, smallest / len(pieces), high / len(pieces)))
        level = level * jnp.repeat(steps, dims[position] // shards_of).reshape([-1 if axis == position else 1 for axis in range(len(dims))])
    return level


def noise(key, dims, deviation, most, split=(), kind=jnp.bfloat16):
    drawn = deviation * jax.random.normal(key, dims, jnp.float32)
    if split:
        drawn = drawn * shard_levels(key, dims, split, -0.22, 0.18)
    return jnp.clip(drawn, -most, most).astype(kind)


def setup_inputs(seed: int = 0) -> dict:
    keys = jax.random.split(jax.random.key(seed), 18)
    return {
        "tokens": noise(keys[0], (MB, MB_TOK, D), 1.0, 6.0, ((1, 32),)),
        "ln1_gain": jnp.clip(1.0 + 0.1 * jax.random.normal(keys[1], (D,), jnp.float32), 0.5, 1.5).astype(jnp.bfloat16),
        "ln1_bias": noise(keys[2], (D,), 0.3, 1.75, ((0, 32),)),
        "qkv_weight": noise(keys[3], (D, 3 * D), D ** -0.5, 0.1875, ((0, 32),)),
        "q_bias": noise(keys[4], (D,), 0.3, 1.75, ((0, 32),)),
        "v_bias": noise(keys[5], (D,), 0.3, 1.75, ((0, 32),)),
        "out_weight": noise(keys[6], (D, D), (max(1, 3 * D // (2 * IMG_TOK))) ** -0.5, 4.0, ((0, 32),)),
        "out_bias": noise(keys[7], (D,), 0.3, 1.75, ((0, 32),)),
        "ln2_gain": jnp.clip(1.0 + 0.1 * jax.random.normal(keys[8], (D,), jnp.float32), 0.5, 1.5).astype(jnp.bfloat16),
        "ln2_bias": noise(keys[9], (D,), 0.3, 1.75, ((0, 32),)),
        "fc1_weight": noise(keys[10], (D, FF), D ** -0.5, 0.1875, ((0, 32),)),
        "fc1_bias": noise(keys[11], (FF,), 0.5, 3.0, ((0, 32),)),
        "fc2_weight": noise(keys[12], (FF, D), (FF // 2) ** -0.5, 0.125, ((0, 32),)),
        "fc2_bias": noise(keys[13], (D,), 0.3, 1.75, ((0, 32),)),
        "image_ids": draw_image_ids(jax.random.fold_in(keys[17], 71), 0),
        "image_starts": draw_image_starts(jax.random.fold_in(keys[17], 71), 0),
        "cotangent": noise(keys[16], (MB, MB_TOK, D), 1.0, 6.0, ((1, 32),)),
    }


@jax.custom_vjp
def low(v):
    return lax.optimization_barrier(v.astype(jnp.bfloat16)).astype(jnp.float32)

@jax.custom_vjp
def low_back(v):
    return v

def low_keep(v):
    return (low(v), None)

def low_pass(kept, grad):
    return (grad,)

def back_keep(v):
    return (v, None)

def back_low(kept, grad):
    return (low(grad),)
low.defvjp(low_keep, low_pass)
low_back.defvjp(back_keep, back_low)
epsilon = 1e-05
negative_fill = -1e+30

def matmul(left, right):
    return jnp.dot(left, right, precision=lax.Precision.HIGHEST)

def layer_norm(values, gain, shift):
    center = values - lax.optimization_barrier(jnp.mean(values, axis=-1, keepdims=True))
    spread = lax.optimization_barrier(jnp.mean(center * center, axis=-1, keepdims=True))
    return center * lax.rsqrt(spread + epsilon) * gain + shift

def attend(queries, key_rows, value_rows, low_bound, high_bound):
    row_count = queries.shape[0]
    block_rows = math.gcd(512, row_count)
    margin = IMG_TOK - 1
    key_span = block_rows + 2 * margin
    keys_padded = jnp.pad(key_rows, ((margin, margin), (0, 0)))
    values_padded = jnp.pad(value_rows, ((margin, margin), (0, 0)))
    score_scale = HEAD_DIM ** (-0.5)

    def one_block(index):
        begin = (index * block_rows).astype(jnp.int32)
        query_part = lax.dynamic_slice_in_dim(queries, begin, block_rows, 0).reshape(block_rows, HEADS, HEAD_DIM)
        key_part = lax.dynamic_slice_in_dim(keys_padded, begin, key_span, 0).reshape(key_span, HEADS, HEAD_DIM)
        value_part = lax.dynamic_slice_in_dim(values_padded, begin, key_span, 0).reshape(key_span, HEADS, HEAD_DIM)
        low_rows = lax.dynamic_slice_in_dim(low_bound, begin, block_rows, 0)
        high_rows = lax.dynamic_slice_in_dim(high_bound, begin, block_rows, 0)
        places = begin - margin + jnp.arange(key_span, dtype=jnp.int32)
        allowed = (places[None, :] >= low_rows[:, None]) & (places[None, :] < high_rows[:, None])
        scores = low_back(jnp.einsum('thd,shd->hts', query_part, key_part, precision=lax.Precision.HIGHEST) * score_scale)
        scores = jnp.where(allowed[None], scores, negative_fill)
        peak = lax.optimization_barrier(jnp.max(scores, axis=-1, keepdims=True))
        exponent = jnp.exp(scores - peak)
        shares = low(exponent / lax.optimization_barrier(jnp.sum(exponent, axis=-1, keepdims=True)))
        mixed = jnp.einsum('hts,shd->thd', shares, value_part, precision=lax.Precision.HIGHEST)
        return mixed.reshape(block_rows, HEADS * HEAD_DIM)
    blocks = lax.map(jax.checkpoint(one_block), jnp.arange(row_count // block_rows, dtype=jnp.int32))
    return blocks.reshape(row_count, HEADS * HEAD_DIM)

def forward(stream, ln1_gain, ln1_bias, qkv_weight, q_bias, v_bias, out_weight, out_bias, ln2_gain, ln2_bias, fc1_weight, fc1_bias, fc2_weight, fc2_bias, low_bound, high_bound):
    normed = low(layer_norm(stream, ln1_gain, ln1_bias))
    joined = matmul(normed, qkv_weight)
    queries = low(low_back(joined[:, :D] + q_bias))
    key_rows = low(low_back(joined[:, D:2 * D]))
    value_rows = low(low_back(joined[:, 2 * D:] + v_bias))
    mixed = low(low_back(attend(queries, key_rows, value_rows, low_bound, high_bound)))
    branch = low_back(matmul(mixed, out_weight) + out_bias)
    middle = stream + branch
    normed_two = low(layer_norm(middle, ln2_gain, ln2_bias))
    hidden = low_back(matmul(normed_two, fc1_weight) + fc1_bias)
    active = low(hidden * jax.nn.sigmoid(1.702 * hidden))
    result = low_back(matmul(active, fc2_weight) + fc2_bias)
    return middle + result

def reference(tokens, ln1_gain, ln1_bias, qkv_weight, q_bias, v_bias, out_weight, out_bias, ln2_gain, ln2_bias, fc1_weight, fc1_bias, fc2_weight, fc2_bias, image_ids, image_starts, cotangent):
    params = (ln1_gain, ln1_bias, qkv_weight, q_bias, v_bias, out_weight, out_bias, ln2_gain, ln2_bias, fc1_weight, fc1_bias, fc2_weight, fc2_bias)
    params = [item.astype(jnp.float32) for item in params]
    totals = [jnp.zeros_like(item) for item in params]
    outputs = []
    grad_inputs = []
    for micro_index in range(MB):
        starts_row = image_starts[micro_index]
        finish = jnp.concatenate([starts_row[1:], jnp.full((1,), MB_TOK, jnp.int32)])
        low_bound = starts_row[image_ids[micro_index]].astype(jnp.int32)
        high_bound = finish[image_ids[micro_index]].astype(jnp.int32)
        stream = tokens[micro_index].astype(jnp.float32)

        def apply(stream_in, *weights):
            return forward(stream_in, *weights, low_bound, high_bound)
        result, pullback = jax.vjp(apply, stream, *params)
        grads = pullback(cotangent[micro_index].astype(jnp.float32))
        outputs.append(result.astype(jnp.bfloat16))
        grad_inputs.append(grads[0].astype(jnp.bfloat16))
        totals = [total + grad for total, grad in zip(totals, grads[1:])]
    return (jnp.stack(outputs), jnp.stack(grad_inputs), totals[0], totals[1], totals[2], totals[3], totals[4], totals[5], totals[6], totals[7], totals[8], totals[9], totals[10], totals[11], totals[12])
```

```python
import functools

import jax
import jax.numpy as jnp
from jax import lax
from jax.experimental import pallas as pl
from jax.experimental.pallas import tpu as pltpu
from jax.sharding import PartitionSpec as P

HEAD_DIM = 64
IMG_TOK = 577
PLANE = 8
PAIR = 2 * HEAD_DIM
HALO = IMG_TOK - 1
LEAD = 640
WINDOW = 640
TILE = 256

epsilon = 1e-05
negative_fill = -1e30
bf16 = jnp.bfloat16
f32 = jnp.float32


def product(left, right):
    return jnp.dot(left, right, preferred_element_type=f32)


def product_tn(left, right):
    return lax.dot_general(left, right, (((0,), (0,)), ((), ())), preferred_element_type=f32)


def product_nt(left, right):
    return lax.dot_general(left, right, (((1,), (1,)), ((), ())), preferred_element_type=f32)


def swap(block, bit):
    n = lax.axis_size("seq")
    return lax.ppermute(block, "seq", [(i, i ^ bit) for i in range(n)])


def shift_plane(block, planes):
    n = lax.axis_size("seq")
    step = planes * PLANE
    return lax.ppermute(block, "seq", [(i, i + step) for i in range(n) if 0 <= i + step < n])


def places(order):
    held = [0]
    for bit in order:
        held = held + [r ^ bit for r in held]
    return held


def gather_bits(block, order):
    current = block[None]
    for bit in order[:-1]:
        current = jnp.concatenate([current, swap(current, bit)], axis=0)
    return current, swap(current, order[-1])


def collect_kernel(parts, info, spots, *refs):
    whole = refs[2 * parts]
    side = jnp.bitwise_and(info[0], 1)
    for k in range(parts):
        whole[0, side, k] = refs[2 * k][0]
        whole[0, 1 - side, k] = refs[2 * k + 1][0]


def spread_kernel(parts, info, spots, *refs):
    whole = refs[0]
    side = jnp.bitwise_and(info[0], 1)
    for k in range(parts):
        refs[1 + 2 * k][0] = whole[0, side, k]
        refs[2 + 2 * k][0] = whole[0, 1 - side, k]


def block_specs(parts, half, part_rows, columns):
    piece = [
        pl.BlockSpec((1, part_rows, columns), lambda s, info, spots, k=k: (spots[k, s], 0, 0))
        for k in range(parts)
        for _ in range(2)
    ]
    whole = pl.BlockSpec(
        (1, 2, parts, part_rows, columns),
        lambda s, info, spots: (jnp.bitwise_xor(info[0] >> 1, s), 0, 0, 0, 0),
    )
    return piece, whole


def spot_table(orders, half):
    table = []
    for order in orders:
        held = places(order)
        table.append([held.index(2 * s) for s in range(half)])
    return jnp.asarray(table, jnp.int32)


def gathered_weight(info, shard, orders):
    rows, columns = shard.shape
    n = lax.axis_size("seq")
    half = n // 2
    parts = len(orders)
    part_rows = rows // parts
    ins = []
    for k, order in enumerate(orders):
        ins += gather_bits(shard[k * part_rows : (k + 1) * part_rows], order)
    piece, whole = block_specs(parts, half, part_rows, columns)
    joined = pl.pallas_call(
        functools.partial(collect_kernel, parts),
        grid_spec=pltpu.PrefetchScalarGridSpec(
            num_scalar_prefetch=2, grid=(half,), in_specs=piece, out_specs=whole
        ),
        out_shape=jax.ShapeDtypeStruct((half, 2, parts, part_rows, columns), shard.dtype),
    )(info, spot_table([order[:-1] for order in orders], half), *ins)
    return joined.reshape(n * rows, columns)


def scattered_sum(info, partial, orders):
    n = lax.axis_size("seq")
    total_rows, columns = partial.shape
    rows = total_rows // n
    parts = len(orders)
    part_rows = rows // parts
    half = n // 2
    piece, whole = block_specs(parts, half, part_rows, columns)
    placed = pl.pallas_call(
        functools.partial(spread_kernel, parts),
        grid_spec=pltpu.PrefetchScalarGridSpec(
            num_scalar_prefetch=2, grid=(half,), in_specs=[whole], out_specs=piece
        ),
        out_shape=[jax.ShapeDtypeStruct((half, part_rows, columns), partial.dtype)] * (2 * parts),
    )(
        info,
        spot_table([order[1:][::-1] for order in orders], half),
        partial.reshape(half, 2, parts, part_rows, columns),
    )
    sums = []
    for k, order in enumerate(orders):
        keep, send = placed[2 * k], placed[2 * k + 1]
        size = half
        for bit in order:
            got = swap(send, bit)
            if size == 1:
                sums.append(keep[0].astype(f32) + got[0].astype(f32))
                break
            size //= 2
            send = (keep[size:].astype(f32) + got[size:].astype(f32)).astype(bf16)
            keep = (keep[:size].astype(f32) + got[:size].astype(f32)).astype(bf16)
    return jnp.concatenate(sums, axis=0) if len(sums) > 1 else sums[0]


def turn_kernel(info, blocks, turned):
    for r in range(blocks.shape[0]):
        turned[r] = blocks[jnp.bitwise_xor(info[0], r)]


def turn_blocks(info, blocks):
    return pl.pallas_call(
        turn_kernel,
        grid_spec=pltpu.PrefetchScalarGridSpec(
            num_scalar_prefetch=1,
            grid=(1,),
            in_specs=[pl.BlockSpec(blocks.shape, lambda g, i: (0, 0, 0))],
            out_specs=pl.BlockSpec(blocks.shape, lambda g, i: (0, 0, 0)),
        ),
        out_shape=jax.ShapeDtypeStruct(blocks.shape, blocks.dtype),
    )(info, blocks)


def load_rows(place_in_plane, qkv, before, after, queries, keys, values, sem):
    micro_count, blocks = qkv.shape[0], qkv.shape[1]
    rows = qkv.shape[2]
    own = blocks * rows
    for buffer in (keys, values):
        for m in range(micro_count):
            buffer[m, 0 : LEAD - HALO, :] = jnp.zeros((LEAD - HALO, PAIR), bf16)
            tail = buffer.shape[1] - (LEAD + own + HALO)
            buffer[m, LEAD + own + HALO :, :] = jnp.zeros((tail, PAIR), bf16)
    started = []
    for m in range(micro_count):
        for r in range(blocks):
            spot = pl.multiple_of(jnp.bitwise_xor(place_in_plane, r) * rows, rows)
            started += [
                pltpu.make_async_copy(
                    qkv.at[m, r, :, pl.ds(0, PAIR)], queries.at[m, pl.ds(spot, rows)], sem
                ),
                pltpu.make_async_copy(
                    qkv.at[m, r, :, pl.ds(PAIR, PAIR)], keys.at[m, pl.ds(LEAD + spot, rows)], sem
                ),
                pltpu.make_async_copy(
                    qkv.at[m, r, :, pl.ds(2 * PAIR, PAIR)], values.at[m, pl.ds(LEAD + spot, rows)], sem
                ),
            ]
        for which, buffer in enumerate((keys, values)):
            columns = pl.ds(which * PAIR, PAIR)
            started += [
                pltpu.make_async_copy(
                    before.at[m, :, columns], buffer.at[m, pl.ds(LEAD - HALO, HALO)], sem
                ),
                pltpu.make_async_copy(
                    after.at[m, :, columns], buffer.at[m, pl.ds(LEAD + own, HALO)], sem
                ),
            ]
    return started


def image_span(bounds, m, image, base):
    begin = bounds[m, image] - base + LEAD
    finish = bounds[m, image + 1] - base + LEAD
    return begin, finish


def key_block(keys, m, begin, finish, key_start, key_aug):
    key_aug[:, :PAIR] = keys[m, pl.ds(key_start, WINDOW), :]
    rows = key_start + lax.broadcasted_iota(jnp.int32, (WINDOW, PAIR), 0)
    inside = (rows >= begin) & (rows < finish)
    key_aug[:, PAIR:] = jnp.where(inside, 0.0, negative_fill).astype(bf16)


def split_heads(rows_f32, lanes):
    first = jnp.where(lanes < HEAD_DIM, rows_f32, 0.0).astype(bf16)
    second = jnp.where(lanes >= HEAD_DIM, rows_f32, 0.0).astype(bf16)
    return first, second


def attend_kernel(
    info, bounds, qkv, before, after, mixed, stats, queries, keys, values, result, result_low, key_aug, value_t, sem
):
    micro_count, blocks, rows, _ = qkv.shape
    own = blocks * rows
    place_in_plane, base = info[1], info[2]
    image_count = bounds.shape[1] - 1
    started = load_rows(place_in_plane, qkv, before, after, queries, keys, values, sem)
    for copy in started:
        copy.start()
    value_t[:, HEAD_DIM:, :] = jnp.ones((2, 16, WINDOW), bf16)
    lanes = lax.broadcasted_iota(jnp.int32, (TILE, PAIR), 1)
    rows_iota = lax.broadcasted_iota(jnp.int32, (TILE, PAIR), 0)
    lane_row = lax.broadcasted_iota(jnp.int32, (1, TILE), 1)
    query_mark = jnp.where(lanes == 0, 1.0, 0.0).astype(bf16)
    for copy in started:
        copy.wait()

    for m in range(micro_count):

        def one_image(image, carry):
            begin, finish = image_span(bounds, m, image, base)

            @pl.when((finish > LEAD) & (begin < LEAD + own))
            def _():
                key_start = pl.multiple_of((begin >> 4) << 4, 16)
                key_block(keys, m, begin, finish, key_start, key_aug)
                turned = values[m, pl.ds(key_start, WINDOW), :].astype(f32).T
                value_t[0, :HEAD_DIM, :] = turned[:HEAD_DIM].astype(bf16)
                value_t[1, :HEAD_DIM, :] = turned[HEAD_DIM:].astype(bf16)
                first_tile = jnp.maximum(begin - LEAD, 0) >> 8
                last_tile = (jnp.minimum(finish - LEAD, own) + TILE - 1) >> 8

                def one_tile(tile, carry):
                    spot = pl.multiple_of(tile * TILE, TILE)
                    scaled = queries[m, pl.ds(spot, TILE), :].astype(f32) * (HEAD_DIM**-0.5)
                    pieces = []
                    inside_lane = (lane_row + (spot + LEAD) >= begin) & (lane_row + (spot + LEAD) < finish)
                    for h, query in enumerate(split_heads(scaled, lanes)):
                        aug = jnp.concatenate([query, query_mark], axis=1)
                        scores = product_nt(key_aug[...], aug)
                        peak = jnp.max(scores, axis=0, keepdims=True)
                        weights = jnp.exp(scores - peak).astype(bf16)
                        out = product(value_t[h], weights)
                        total = out[HEAD_DIM : HEAD_DIM + 1]
                        pieces.append(out[:HEAD_DIM] / total)
                        row = (m * 2 + h) * blocks + tile
                        stats[pl.ds(row, 1), :] = jnp.where(
                            inside_lane, peak + jnp.log(total), stats[pl.ds(row, 1), :]
                        )
                    value = jnp.concatenate(pieces, axis=0).T
                    place_row = rows_iota + (spot + LEAD)
                    inside = (place_row >= begin) & (place_row < finish)
                    result[m, pl.ds(spot, TILE), :] = jnp.where(
                        inside, value, result[m, pl.ds(spot, TILE), :]
                    )
                    return carry

                lax.fori_loop(first_tile, last_tile, one_tile, 0)

            return carry

        lax.fori_loop(0, image_count, one_image, 0)

    result_low[...] = result[...].astype(bf16)
    started = []
    for m in range(micro_count):
        for r in range(blocks):
            spot = pl.multiple_of(jnp.bitwise_xor(place_in_plane, r) * rows, rows)
            started.append(pltpu.make_async_copy(result_low.at[m, pl.ds(spot, rows)], mixed.at[r, m], sem))
    for copy in started:
        copy.start()
    for copy in started:
        copy.wait()


def attend_back_kernel(
    info,
    bounds,
    qkv,
    before,
    after,
    mixed,
    grad_mixed,
    stats,
    grad_query,
    grad_pairs,
    grad_before,
    grad_after,
    queries,
    keys,
    values,
    result,
    grads,
    key_aug,
    key_t,
    acc_query,
    acc_key,
    acc_value,
    edge,
    sem,
):
    micro_count, blocks, rows, _ = qkv.shape
    own = blocks * rows
    place_in_plane, base = info[1], info[2]
    image_count = bounds.shape[1] - 1
    started = load_rows(place_in_plane, qkv, before, after, queries, keys, values, sem)
    for m in range(micro_count):
        for r in range(blocks):
            spot = pl.multiple_of(jnp.bitwise_xor(place_in_plane, r) * rows, rows)
            started += [
                pltpu.make_async_copy(mixed.at[r, m], result.at[m, pl.ds(spot, rows)], sem),
                pltpu.make_async_copy(grad_mixed.at[r, m], grads.at[m, pl.ds(spot, rows)], sem),
            ]
    for copy in started:
        copy.start()
    acc_query[...] = jnp.zeros_like(acc_query)
    acc_key[...] = jnp.zeros_like(acc_key)
    acc_value[...] = jnp.zeros_like(acc_value)
    lanes = lax.broadcasted_iota(jnp.int32, (TILE, PAIR), 1)
    lane_row = lax.broadcasted_iota(jnp.int32, (1, TILE), 1)
    query_mark = jnp.where(lanes == 0, 1.0, 0.0).astype(bf16)
    for copy in started:
        copy.wait()

    for m in range(micro_count):

        def one_image(image, carry):
            begin, finish = image_span(bounds, m, image, base)

            @pl.when((finish > LEAD) & (begin < LEAD + own))
            def _():
                key_start = pl.multiple_of((begin >> 4) << 4, 16)
                key_rows = pl.ds(key_start, WINDOW)
                key_block(keys, m, begin, finish, key_start, key_aug)
                turned = keys[m, key_rows, :].astype(f32).T
                key_t[0] = turned[:HEAD_DIM].astype(bf16)
                key_t[1] = turned[HEAD_DIM:].astype(bf16)
                first_tile = jnp.maximum(begin - LEAD, 0) >> 8
                last_tile = (jnp.minimum(finish - LEAD, own) + TILE - 1) >> 8

                def one_tile(tile, carry):
                    spot = pl.multiple_of(tile * TILE, TILE)
                    here = pl.ds(spot, TILE)
                    scaled = queries[m, here, :].astype(f32) * (HEAD_DIM**-0.5)
                    grad = grads[m, here, :].astype(f32)
                    dots = (grad * result[m, here, :].astype(f32)).T
                    inside_lane = (lane_row + (spot + LEAD) >= begin) & (lane_row + (spot + LEAD) < finish)
                    both = zip(split_heads(scaled, lanes), split_heads(grad, lanes))
                    pieces = []
                    add_key, add_value = None, None
                    for h, (query, grad_h) in enumerate(both):
                        row = (m * 2 + h) * blocks + tile
                        level = jnp.where(inside_lane, stats[pl.ds(row, 1), :], -negative_fill)
                        row_dot = jnp.sum(
                            dots[h * HEAD_DIM : (h + 1) * HEAD_DIM], axis=0, keepdims=True
                        )
                        aug = jnp.concatenate([query, query_mark], axis=1)
                        shares = jnp.exp(product_nt(key_aug[...], aug) - level)
                        grad_share = product_nt(values[m, key_rows, :], grad_h)
                        grad_scores = (shares * (grad_share - row_dot)).astype(bf16)
                        value_part = product(shares.astype(bf16), grad_h)
                        key_part = product(grad_scores, query)
                        add_value = value_part if h == 0 else add_value + value_part
                        add_key = key_part if h == 0 else add_key + key_part
                        pieces.append(product(key_t[h], grad_scores))
                    acc_value[m, key_rows, :] += add_value
                    acc_key[m, key_rows, :] += add_key
                    acc_query[m, here, :] += jnp.concatenate(pieces, axis=0).T * (HEAD_DIM**-0.5)
                    return carry

                lax.fori_loop(first_tile, last_tile, one_tile, 0)

            return carry

        lax.fori_loop(0, image_count, one_image, 0)

    started = []
    for m in range(micro_count):
        started.append(pltpu.make_async_copy(acc_query.at[m], grad_query.at[m], sem))
        for which, acc in enumerate((acc_key, acc_value)):
            columns = pl.ds(which * PAIR, PAIR)
            edge[0, m, :, which * PAIR : (which + 1) * PAIR] = acc[m, LEAD - HALO : LEAD, :].astype(bf16)
            edge[1, m, :, which * PAIR : (which + 1) * PAIR] = acc[
                m, LEAD + own : LEAD + own + HALO, :
            ].astype(bf16)
            started.append(
                pltpu.make_async_copy(acc.at[m, pl.ds(LEAD, own)], grad_pairs.at[m, :, columns], sem)
            )
        started.append(pltpu.make_async_copy(edge.at[0, m], grad_before.at[m], sem))
        started.append(pltpu.make_async_copy(edge.at[1, m], grad_after.at[m], sem))
    for copy in started:
        copy.start()
    for copy in started:
        copy.wait()


def any_specs(count):
    return [pl.BlockSpec(memory_space=pl.ANY)] * count


def attend(info, bounds, qkv, before, after):
    micro_count, blocks, rows, _ = qkv.shape
    own = blocks * rows
    span = LEAD + own + LEAD
    stat_rows = micro_count * 2 * blocks
    return pl.pallas_call(
        attend_kernel,
        grid_spec=pltpu.PrefetchScalarGridSpec(
            num_scalar_prefetch=2,
            grid=(1,),
            in_specs=any_specs(3),
            out_specs=any_specs(1) + [pl.BlockSpec((stat_rows, TILE), lambda g, a, b: (0, 0))],
            scratch_shapes=[
                pltpu.VMEM((micro_count, own, PAIR), bf16),
                pltpu.VMEM((micro_count, span, PAIR), bf16),
                pltpu.VMEM((micro_count, span, PAIR), bf16),
                pltpu.VMEM((micro_count, own, PAIR), f32),
                pltpu.VMEM((micro_count, own, PAIR), bf16),
                pltpu.VMEM((WINDOW, 2 * PAIR), bf16),
                pltpu.VMEM((2, HEAD_DIM + 16, WINDOW), bf16),
                pltpu.SemaphoreType.DMA,
            ],
        ),
        out_shape=[
            jax.ShapeDtypeStruct((blocks, micro_count, rows, PAIR), bf16),
            jax.ShapeDtypeStruct((stat_rows, TILE), f32),
        ],
    )(info, bounds, qkv, before, after)


def attend_back(info, bounds, qkv, before, after, mixed, grad_mixed, stats):
    micro_count, blocks, rows, _ = qkv.shape
    own = blocks * rows
    span = LEAD + own + LEAD
    stat_rows = micro_count * 2 * blocks
    return pl.pallas_call(
        attend_back_kernel,
        grid_spec=pltpu.PrefetchScalarGridSpec(
            num_scalar_prefetch=2,
            grid=(1,),
            in_specs=any_specs(5) + [pl.BlockSpec((stat_rows, TILE), lambda g, a, b: (0, 0))],
            out_specs=any_specs(4),
            scratch_shapes=[
                pltpu.VMEM((micro_count, own, PAIR), bf16),
                pltpu.VMEM((micro_count, span, PAIR), bf16),
                pltpu.VMEM((micro_count, span, PAIR), bf16),
                pltpu.VMEM((micro_count, own, PAIR), bf16),
                pltpu.VMEM((micro_count, own, PAIR), bf16),
                pltpu.VMEM((WINDOW, 2 * PAIR), bf16),
                pltpu.VMEM((2, HEAD_DIM, WINDOW), bf16),
                pltpu.VMEM((micro_count, own, PAIR), f32),
                pltpu.VMEM((micro_count, span, PAIR), f32),
                pltpu.VMEM((micro_count, span, PAIR), f32),
                pltpu.VMEM((2, micro_count, HALO, 2 * PAIR), bf16),
                pltpu.SemaphoreType.DMA,
            ],
        ),
        out_shape=[
            jax.ShapeDtypeStruct((micro_count, own, PAIR), f32),
            jax.ShapeDtypeStruct((micro_count, own, 2 * PAIR), f32),
            jax.ShapeDtypeStruct((micro_count, HALO, 2 * PAIR), bf16),
            jax.ShapeDtypeStruct((micro_count, HALO, 2 * PAIR), bf16),
        ],
    )(info, bounds, qkv, before, after, mixed, grad_mixed, stats)


def join_kernel(first_blocks, last_blocks, blocks, info, query, pairs, head, tail, joined):
    tile = pl.program_id(1)
    total = pairs[0]
    total = total + jnp.where(tile < first_blocks, head[0].astype(f32), 0.0)
    total = total + jnp.where(tile >= blocks - last_blocks, tail[0].astype(f32), 0.0)
    joined[0, 0, :, :PAIR] = query[0].astype(bf16)
    joined[0, 0, :, PAIR:] = total.astype(bf16)


def join_grads(info, grad_query, grad_pairs, head, tail, rows):
    micro_count, own, _ = grad_query.shape
    blocks = own // rows
    edge_blocks = -(-HALO // rows)
    spare = edge_blocks * rows - HALO
    head = jnp.pad(head, ((0, 0), (0, spare), (0, 0)))
    tail = jnp.pad(tail, ((0, 0), (spare, 0), (0, 0)))
    return pl.pallas_call(
        functools.partial(join_kernel, edge_blocks, edge_blocks, blocks),
        grid_spec=pltpu.PrefetchScalarGridSpec(
            num_scalar_prefetch=1,
            grid=(micro_count, blocks),
            in_specs=[
                pl.BlockSpec((1, rows, PAIR), lambda m, t, i: (m, t, 0)),
                pl.BlockSpec((1, rows, 2 * PAIR), lambda m, t, i: (m, t, 0)),
                pl.BlockSpec((1, rows, 2 * PAIR), lambda m, t, i: (m, jnp.minimum(t, edge_blocks - 1), 0)),
                pl.BlockSpec(
                    (1, rows, 2 * PAIR),
                    lambda m, t, i: (m, jnp.maximum(t - (blocks - edge_blocks), 0), 0),
                ),
            ],
            out_specs=pl.BlockSpec(
                (1, 1, rows, 3 * PAIR), lambda m, t, i: (m, jnp.bitwise_xor(t, i[1]), 0, 0)
            ),
        ),
        out_shape=jax.ShapeDtypeStruct((micro_count, blocks, rows, 3 * PAIR), bf16),
    )(info, grad_query, grad_pairs, head, tail)


def layer_norm_parts(values, gain, shift):
    center = values - jnp.mean(values, axis=-1, keepdims=True)
    inverse = lax.rsqrt(jnp.mean(center * center, axis=-1, keepdims=True) + epsilon)
    normal = center * inverse
    return (normal * gain + shift, normal, inverse)


def layer_norm_back(grad_normed, normal, inverse, gain):
    scaled = grad_normed * gain
    centered = scaled - jnp.mean(scaled, axis=-1, keepdims=True)
    return inverse * (centered - normal * jnp.mean(scaled * normal, axis=-1, keepdims=True))


def plane_tokens(block, order):
    near, far = gather_bits(block, order)
    held = places(order)
    half = PLANE // 2
    at = {r: (near[p] if p < half else far[p - half]) for p, r in enumerate(held)}
    return jnp.stack([at[r] for r in range(PLANE)])


def plane_scatter(partial, order):
    pieces = {r: partial[r].astype(bf16) for r in range(PLANE)}
    left = list(range(PLANE))
    total = None
    for step, bit in enumerate(order):
        keep = [r for r in left if not r & bit]
        got = swap(jnp.stack([pieces[r | bit] for r in keep]), bit)
        last = step == len(order) - 1
        for position, r in enumerate(keep):
            added = pieces[r].astype(f32) + got[position].astype(f32)
            pieces[r] = added if last else added.astype(bf16)
        left = keep
    return pieces[0]


def body(
    tokens,
    ln1_gain,
    ln1_bias,
    qkv_weight,
    q_bias,
    v_bias,
    out_weight,
    out_bias,
    ln2_gain,
    ln2_bias,
    fc1_weight,
    fc1_bias,
    fc2_weight,
    fc2_bias,
    image_ids,
    image_starts,
    cotangent,
):
    micro_count, tok_dev, model_width = tokens.shape
    n = lax.axis_size("seq")
    own_tokens = micro_count * tok_dev
    plane_rows = PLANE * tok_dev
    stream_len = tok_dev * n
    me = lax.axis_index("seq")
    mine = jnp.bitwise_and(me, PLANE - 1)
    base = (me - mine) * tok_dev
    info = jnp.stack([me, mine, base]).astype(jnp.int32)
    bounds = jnp.concatenate(
        [image_starts, jnp.full((micro_count, 1), stream_len, jnp.int32)], axis=1
    )
    plane_bits = [1, 2, 4]
    depth_bits = []
    bit = PLANE
    while bit < n:
        depth_bits.append(bit)
        bit *= 2
    order_a = depth_bits + [2, 4, 1]
    order_b = depth_bits + [4, 2, 1]

    small = [ln1_gain, ln1_bias, q_bias, v_bias, out_bias, ln2_gain, ln2_bias, fc2_bias, fc1_bias]
    shard_rows = qkv_weight.shape[0]
    small_len = sum(item.shape[0] for item in small)
    spare_rows = -(-small_len // (8 * 3 * PAIR)) * 8
    small_rows = jnp.pad(jnp.concatenate(small), (0, spare_rows * 3 * PAIR - small_len))
    small_rows = small_rows.reshape(spare_rows, 3 * PAIR)
    by_pair = qkv_weight.reshape(shard_rows, 3, PLANE, PAIR).transpose(2, 0, 1, 3)
    by_pair = by_pair.reshape(PLANE, shard_rows, 3 * PAIR)
    outgoing = jnp.concatenate(
        [by_pair, jnp.broadcast_to(small_rows[None], (PLANE,) + small_rows.shape)], axis=1
    )
    arrived = [lax.dynamic_index_in_dim(outgoing, mine, 0, keepdims=False)]
    for r in range(1, PLANE):
        arrived.append(
            swap(lax.dynamic_index_in_dim(outgoing, jnp.bitwise_xor(mine, r), 0, keepdims=False), r)
        )
    current = jnp.stack(arrived)
    for bit in depth_bits:
        current = jnp.concatenate([current, swap(current, bit)], axis=0)
    pair_blocks = turn_blocks(info, current)
    pair_weight = pair_blocks[:, :shard_rows].reshape(n * shard_rows, 3 * PAIR)
    small_all = pair_blocks[:, shard_rows:].reshape(n, -1).astype(f32)
    small_full = []
    offset = 0
    for item in small:
        width = item.shape[0]
        small_full.append(small_all[:, offset : offset + width].reshape(n * width))
        offset += width
    gain_one, shift_one, q_shift, v_shift, out_shift, gain_two, shift_two, down_shift, up_shift = small_full

    plane_stream = jnp.stack(
        [
            plane_tokens(tokens[m], [2, 4, 1] if m % 2 == 0 else [4, 2, 1])
            for m in range(micro_count)
        ]
    )
    plane_flat = plane_stream.reshape(micro_count * plane_rows, model_width)
    normed, _, _ = layer_norm_parts(plane_flat.astype(f32), gain_one, shift_one)
    normed_low = normed.astype(bf16)
    pair_shift = jnp.concatenate(
        [
            lax.dynamic_slice_in_dim(q_shift, mine * PAIR, PAIR),
            jnp.zeros((PAIR,), f32),
            lax.dynamic_slice_in_dim(v_shift, mine * PAIR, PAIR),
        ]
    )
    qkv = (product(normed_low, pair_weight) + pair_shift).astype(bf16)
    qkv = qkv.reshape(micro_count, PLANE, tok_dev, 3 * PAIR)

    edge_blocks = -(-HALO // tok_dev)

    def plane_block(index):
        return lax.dynamic_index_in_dim(qkv, jnp.bitwise_xor(mine, index), 1, keepdims=False)[:, :, PAIR:]

    last_rows = jnp.concatenate([plane_block(PLANE - edge_blocks + k) for k in range(edge_blocks)], axis=1)
    first_rows = jnp.concatenate([plane_block(k) for k in range(edge_blocks)], axis=1)
    before = shift_plane(last_rows[:, edge_blocks * tok_dev - HALO :], 1)
    after = shift_plane(first_rows[:, :HALO], -1)
    mixed_pair, stats = attend(info, bounds, qkv, before, after)

    def column(r):
        return jnp.bitwise_xor(mine, r) * PAIR

    mixed_low = jnp.zeros((own_tokens, model_width), bf16)
    for r in range(PLANE):
        part = mixed_pair[r] if r == 0 else swap(mixed_pair[r], r)
        mixed_low = lax.dynamic_update_slice(mixed_low, part.reshape(own_tokens, PAIR), (0, column(r)))

    out_full = gathered_weight(info, out_weight, [order_a])
    up_full = gathered_weight(info, fc1_weight, [order_a, order_b])
    down_full = gathered_weight(info, fc2_weight, [order_a, order_b])

    stream = tokens.reshape(own_tokens, model_width).astype(f32)
    cotangent_low = cotangent.reshape(own_tokens, model_width)
    middle = stream + product(mixed_low, out_full) + out_shift
    normed_two, normal_two, inverse_two = layer_norm_parts(middle, gain_two, shift_two)
    normed_two_low = normed_two.astype(bf16)
    hidden = product(normed_two_low, up_full) + up_shift
    gate = jax.nn.sigmoid(1.702 * hidden)
    active_low = (hidden * gate).astype(bf16)
    result = middle + product(active_low, down_full) + down_shift

    grad_active = product_nt(cotangent_low, down_full)
    grad_hidden_low = (grad_active * (gate + 1.702 * hidden * gate * (1.0 - gate))).astype(bf16)
    grad_normed_two = product_nt(grad_hidden_low, up_full)
    grad_middle = cotangent_low.astype(f32) + layer_norm_back(
        grad_normed_two, normal_two, inverse_two, gain_two
    )
    grad_branch_low = grad_middle.astype(bf16)
    grad_mixed_low = product_nt(grad_branch_low, out_full).astype(bf16)

    back_order_a = [1, 2, 4] + depth_bits[::-1]
    back_order_b = [1, 4, 2] + depth_bits[::-1]
    grad_parts = []
    for r in range(PLANE):
        part = lax.dynamic_slice(grad_mixed_low, (0, column(r)), (own_tokens, PAIR))
        part = part.reshape(micro_count, tok_dev, PAIR)
        grad_parts.append(part if r == 0 else swap(part, r))
    grad_mixed_pair = jnp.stack(grad_parts)

    grad_down = product_tn(active_low, cotangent_low).astype(bf16)
    down_sum = scattered_sum(info, grad_down, [back_order_a, back_order_b])
    grad_up = product_tn(normed_two_low, grad_hidden_low).astype(bf16)
    up_sum = scattered_sum(info, grad_up, [back_order_a, back_order_b])
    grad_out_weight = product_tn(mixed_low, grad_branch_low).astype(bf16)
    out_sum = scattered_sum(info, grad_out_weight, [back_order_a])

    grad_query, grad_pairs, grad_before, grad_after = attend_back(
        info, bounds, qkv, before, after, mixed_pair, grad_mixed_pair, stats
    )
    from_next = shift_plane(grad_before, -1)
    from_last = shift_plane(grad_after, 1)
    grad_joined = join_grads(info, grad_query, grad_pairs, from_last, from_next, tok_dev)
    grad_flat = grad_joined.reshape(micro_count * plane_rows, 3 * PAIR)

    grad_plane = product_nt(grad_flat, pair_weight).reshape(micro_count, PLANE, tok_dev, model_width)
    grad_normed = jnp.stack(
        [
            plane_scatter(grad_plane[m], [1, 2, 4] if m % 2 == 0 else [1, 4, 2])
            for m in range(micro_count)
        ]
    ).reshape(own_tokens, model_width)
    _, normal_one, inverse_one = layer_norm_parts(stream, gain_one, shift_one)
    grad_stream = grad_middle + layer_norm_back(grad_normed, normal_one, inverse_one, gain_one)

    grad_pair_weight = product_tn(normed_low, grad_flat)
    column_sum = jnp.sum(grad_flat.astype(f32), axis=0)
    wide = pair_weight.astype(f32)
    grad_shift_one = jnp.sum(wide * column_sum, axis=1)
    grad_gain_one = jnp.sum(wide * grad_pair_weight, axis=1)
    grad_gain_one = (grad_gain_one - shift_one * grad_shift_one) / gain_one

    def at_columns(part):
        return lax.dynamic_update_slice(jnp.zeros((model_width,), f32), part, (mine * PAIR,))

    small_grads = [
        grad_gain_one,
        grad_shift_one,
        at_columns(column_sum[:PAIR]),
        at_columns(column_sum[2 * PAIR :]),
        jnp.sum(grad_branch_low.astype(f32), axis=0),
        jnp.sum(grad_normed_two * normal_two, axis=0),
        jnp.sum(grad_normed_two, axis=0),
        jnp.sum(cotangent_low.astype(f32), axis=0),
        jnp.sum(grad_hidden_low.astype(f32), axis=0),
    ]
    small_out = jnp.concatenate([item.reshape(n, -1) for item in small_grads], axis=1).astype(bf16)
    small_out = jnp.pad(small_out, ((0, 0), (0, spare_rows * 3 * PAIR - small_len)))
    small_out = small_out.reshape(n, spare_rows, 3 * PAIR)
    leaving = jnp.concatenate(
        [grad_pair_weight.astype(bf16).reshape(n, shard_rows, 3 * PAIR), small_out], axis=1
    )
    turned = turn_blocks(info, leaving)
    size = n
    for bit in depth_bits[::-1]:
        size //= 2
        got = swap(turned[size:], bit)
        turned = (turned[:size].astype(f32) + got.astype(f32)).astype(bf16)
    qkv_sum = jnp.zeros((shard_rows, 3, model_width), f32)
    small_sum = jnp.zeros((spare_rows, 3 * PAIR), f32)
    for r in range(PLANE):
        part = turned[r] if r == 0 else swap(turned[r], r)
        columns = part[:shard_rows].reshape(shard_rows, 3, PAIR).astype(f32)
        qkv_sum = lax.dynamic_update_slice(qkv_sum, columns, (0, 0, column(r)))
        small_sum = small_sum + part[shard_rows:].astype(f32)
    qkv_sum = qkv_sum.reshape(shard_rows, 3 * model_width)
    small_sum = small_sum.reshape(-1)
    sums = []
    offset = 0
    for item in small:
        sums.append(small_sum[offset : offset + item.shape[0]])
        offset += item.shape[0]

    return (
        result.astype(bf16).reshape(micro_count, tok_dev, model_width),
        grad_stream.astype(bf16).reshape(micro_count, tok_dev, model_width),
        sums[0],
        sums[1],
        qkv_sum,
        sums[2],
        sums[3],
        out_sum,
        sums[4],
        sums[5],
        sums[6],
        up_sum,
        sums[8],
        down_sum,
        sums[7],
    )


def solution(mesh):
    return jax.shard_map(
        body,
        mesh=mesh,
        in_specs=(
            P(None, "seq", None),
            P("seq"),
            P("seq"),
            P("seq", None),
            P("seq"),
            P("seq"),
            P("seq", None),
            P("seq"),
            P("seq"),
            P("seq"),
            P("seq", None),
            P("seq"),
            P("seq", None),
            P("seq"),
            P(None, "seq"),
            P(),
            P(None, "seq", None),
        ),
        out_specs=(
            P(None, "seq", None),
            P(None, "seq", None),
            P("seq"),
            P("seq"),
            P("seq", None),
            P("seq"),
            P("seq"),
            P("seq", None),
            P("seq"),
            P("seq"),
            P("seq"),
            P("seq", None),
            P("seq"),
            P("seq", None),
            P("seq"),
        ),
        check_vma=False,
    )
```

```python
import functools

import jax
import jax.numpy as jnp
from jax import lax
from jax.experimental import pallas as pl
from jax.experimental.pallas import tpu as pltpu
from jax.sharding import PartitionSpec as P

HEAD_DIM = 64
IMG_TOK = 577
PLANE = 8
PAIR = 2 * HEAD_DIM
HALO = IMG_TOK - 1
LEAD = 640
WINDOW = 640
TILE = 256

epsilon = 1e-05
negative_fill = -1e30
bf16 = jnp.bfloat16
f32 = jnp.float32


def product(left, right):
    return jnp.dot(left, right, preferred_element_type=f32)


def product_tn(left, right):
    return lax.dot_general(left, right, (((0,), (0,)), ((), ())), preferred_element_type=f32)


def product_nt(left, right):
    return lax.dot_general(left, right, (((1,), (1,)), ((), ())), preferred_element_type=f32)


def swap(block, bit):
    n = lax.axis_size("seq")
    return lax.ppermute(block, "seq", [(i, i ^ bit) for i in range(n)])


def shift_plane(block, planes):
    n = lax.axis_size("seq")
    step = planes * PLANE
    return lax.ppermute(block, "seq", [(i, i + step) for i in range(n) if 0 <= i + step < n])


def places(order):
    held = [0]
    for bit in order:
        held = held + [r ^ bit for r in held]
    return held


def gather_bits(block, order):
    current = block[None]
    for bit in order[:-1]:
        current = jnp.concatenate([current, swap(current, bit)], axis=0)
    return current, swap(current, order[-1])


def tie(value, *earlier):
    return lax.optimization_barrier((value,) + earlier)[0]


def own_bit(me, bit):
    return jnp.where(jnp.bitwise_and(me, bit) != 0, 1, 0)


def pick(block, axis, index):
    return lax.dynamic_index_in_dim(block, index, axis, keepdims=False)


class Scatter:
    def __init__(self, me, partial, order):
        count = partial.shape[0]
        depth = count.bit_length() - 1
        self.me = me
        self.block = partial.reshape((2,) * depth + partial.shape[1:])
        self.bits = [1 << (depth - 1 - axis) for axis in range(depth)]
        self.order = list(order)
        self.got = None
        self.send = None
        self.split()

    def half(self, index, axis):
        part = pick(self.block, axis, index)
        if self.got is None:
            return part
        return (part.astype(f32) + pick(self.got, axis, index).astype(f32)).astype(bf16)

    def split(self):
        bit = self.order.pop(0)
        axis = self.bits.index(bit)
        self.bits.pop(axis)
        mine = own_bit(self.me, bit)
        self.send, keep = self.half(1 - mine, axis), self.half(mine, axis)
        self.block, self.got, self.bit = keep, None, bit

    def swap(self, *earlier):
        send = tie(self.send, *earlier) if earlier else self.send
        self.got = swap(send, self.bit)

    def advance(self, *earlier):
        self.split()
        self.swap(*earlier)

    def total(self):
        return self.block.astype(f32) + self.got.astype(f32)


def turn_kernel(info, blocks, turned):
    for r in range(blocks.shape[0]):
        turned[r] = blocks[jnp.bitwise_xor(info[0], r)]


def turn_blocks(info, blocks):
    return pl.pallas_call(
        turn_kernel,
        grid_spec=pltpu.PrefetchScalarGridSpec(
            num_scalar_prefetch=1,
            grid=(1,),
            in_specs=[pl.BlockSpec(blocks.shape, lambda g, i: (0, 0, 0))],
            out_specs=pl.BlockSpec(blocks.shape, lambda g, i: (0, 0, 0)),
        ),
        out_shape=jax.ShapeDtypeStruct(blocks.shape, blocks.dtype),
    )(info, blocks)


def load_rows(micros, place_in_plane, qkv, before, after, queries, keys, values, sem):
    blocks, rows = qkv.shape[1], qkv.shape[2]
    own = blocks * rows
    for buffer in (keys, values):
        for slot in range(len(micros)):
            buffer[slot, 0 : LEAD - HALO, :] = jnp.zeros((LEAD - HALO, PAIR), bf16)
            tail = buffer.shape[1] - (LEAD + own + HALO)
            buffer[slot, LEAD + own + HALO :, :] = jnp.zeros((tail, PAIR), bf16)
    started = []
    for slot, m in enumerate(micros):
        for r in range(blocks):
            spot = pl.multiple_of(jnp.bitwise_xor(place_in_plane, r) * rows, rows)
            started += [
                pltpu.make_async_copy(
                    qkv.at[m, r, :, pl.ds(0, PAIR)], queries.at[slot, pl.ds(spot, rows)], sem
                ),
                pltpu.make_async_copy(
                    qkv.at[m, r, :, pl.ds(PAIR, PAIR)], keys.at[slot, pl.ds(LEAD + spot, rows)], sem
                ),
                pltpu.make_async_copy(
                    qkv.at[m, r, :, pl.ds(2 * PAIR, PAIR)], values.at[slot, pl.ds(LEAD + spot, rows)], sem
                ),
            ]
        for which, buffer in enumerate((keys, values)):
            columns = pl.ds(which * PAIR, PAIR)
            started += [
                pltpu.make_async_copy(
                    before.at[m, :, columns], buffer.at[slot, pl.ds(LEAD - HALO, HALO)], sem
                ),
                pltpu.make_async_copy(
                    after.at[m, :, columns], buffer.at[slot, pl.ds(LEAD + own, HALO)], sem
                ),
            ]
    return started


def image_span(bounds, m, image, base):
    begin = bounds[m, image] - base + LEAD
    finish = bounds[m, image + 1] - base + LEAD
    return begin, finish


def key_block(keys, m, begin, finish, key_start, key_aug):
    key_aug[:, :PAIR] = keys[m, pl.ds(key_start, WINDOW), :]
    rows = key_start + lax.broadcasted_iota(jnp.int32, (WINDOW, PAIR), 0)
    inside = (rows >= begin) & (rows < finish)
    key_aug[:, PAIR:] = jnp.where(inside, 0.0, negative_fill).astype(bf16)


def split_heads(rows_f32, lanes):
    first = jnp.where(lanes < HEAD_DIM, rows_f32, 0.0).astype(bf16)
    second = jnp.where(lanes >= HEAD_DIM, rows_f32, 0.0).astype(bf16)
    return first, second


def attend_kernel(
    info, bounds, qkv, before, after, mixed, stats, queries, keys, values, result, result_low, key_aug, value_t, sem
):
    micro_count, blocks, rows, _ = qkv.shape
    own = blocks * rows
    place_in_plane, base = info[1], info[2]
    image_count = bounds.shape[1] - 1
    started = load_rows(range(micro_count), place_in_plane, qkv, before, after, queries, keys, values, sem)
    for copy in started:
        copy.start()
    value_t[:, HEAD_DIM:, :] = jnp.ones((2, 16, WINDOW), bf16)
    lanes = lax.broadcasted_iota(jnp.int32, (TILE, PAIR), 1)
    rows_iota = lax.broadcasted_iota(jnp.int32, (TILE, PAIR), 0)
    lane_row = lax.broadcasted_iota(jnp.int32, (1, TILE), 1)
    query_mark = jnp.where(lanes == 0, 1.0, 0.0).astype(bf16)
    for copy in started:
        copy.wait()

    for m in range(micro_count):

        def one_image(image, carry):
            begin, finish = image_span(bounds, m, image, base)

            @pl.when((finish > LEAD) & (begin < LEAD + own))
            def _():
                key_start = pl.multiple_of((begin >> 4) << 4, 16)
                key_block(keys, m, begin, finish, key_start, key_aug)
                turned = values[m, pl.ds(key_start, WINDOW), :].astype(f32).T
                value_t[0, :HEAD_DIM, :] = turned[:HEAD_DIM].astype(bf16)
                value_t[1, :HEAD_DIM, :] = turned[HEAD_DIM:].astype(bf16)
                first_tile = jnp.maximum(begin - LEAD, 0) >> 8
                last_tile = (jnp.minimum(finish - LEAD, own) + TILE - 1) >> 8

                def one_tile(tile, carry):
                    spot = pl.multiple_of(tile * TILE, TILE)
                    scaled = queries[m, pl.ds(spot, TILE), :].astype(f32) * (HEAD_DIM**-0.5)
                    pieces = []
                    inside_lane = (lane_row + (spot + LEAD) >= begin) & (lane_row + (spot + LEAD) < finish)
                    for h, query in enumerate(split_heads(scaled, lanes)):
                        aug = jnp.concatenate([query, query_mark], axis=1)
                        scores = product_nt(key_aug[...], aug)
                        peak = jnp.max(scores, axis=0, keepdims=True)
                        weights = jnp.exp(scores - peak).astype(bf16)
                        out = product(value_t[h], weights)
                        total = out[HEAD_DIM : HEAD_DIM + 1]
                        pieces.append(out[:HEAD_DIM] / total)
                        row = (m * 2 + h) * blocks + tile
                        stats[pl.ds(row, 1), :] = jnp.where(
                            inside_lane, peak + jnp.log(total), stats[pl.ds(row, 1), :]
                        )
                    value = jnp.concatenate(pieces, axis=0).T
                    place_row = rows_iota + (spot + LEAD)
                    inside = (place_row >= begin) & (place_row < finish)
                    result[m, pl.ds(spot, TILE), :] = jnp.where(
                        inside, value, result[m, pl.ds(spot, TILE), :]
                    )
                    return carry

                lax.fori_loop(first_tile, last_tile, one_tile, 0)

            return carry

        lax.fori_loop(0, image_count, one_image, 0)

    result_low[...] = result[...].astype(bf16)
    started = []
    for m in range(micro_count):
        for r in range(blocks):
            spot = pl.multiple_of(jnp.bitwise_xor(place_in_plane, r) * rows, rows)
            started.append(pltpu.make_async_copy(result_low.at[m, pl.ds(spot, rows)], mixed.at[r, m], sem))
    for copy in started:
        copy.start()
    for copy in started:
        copy.wait()


def attend_back_kernel(m, info, bounds, qkv, before, after, mixed, *refs):
    blocks, rows = qkv.shape[1], qkv.shape[2]
    own = blocks * rows
    grad_mixed, refs = refs[:blocks], refs[blocks:]
    stats, grad_query, grad_pairs, grad_before, grad_after, refs = *refs[:5], refs[5:]
    queries, keys, values, result, grads, key_aug, key_t, acc_query, acc_key, acc_value, edge, sem = refs
    place_in_plane, base = info[1], info[2]
    image_count = bounds.shape[1] - 1
    started = load_rows([m], place_in_plane, qkv, before, after, queries, keys, values, sem)
    for r in range(blocks):
        spot = pl.multiple_of(jnp.bitwise_xor(place_in_plane, r) * rows, rows)
        started += [
            pltpu.make_async_copy(mixed.at[r, m], result.at[pl.ds(spot, rows)], sem),
            pltpu.make_async_copy(grad_mixed[r].at[m], grads.at[pl.ds(spot, rows)], sem),
        ]
    for copy in started:
        copy.start()
    acc_query[...] = jnp.zeros_like(acc_query)
    acc_key[...] = jnp.zeros_like(acc_key)
    acc_value[...] = jnp.zeros_like(acc_value)
    lanes = lax.broadcasted_iota(jnp.int32, (TILE, PAIR), 1)
    lane_row = lax.broadcasted_iota(jnp.int32, (1, TILE), 1)
    query_mark = jnp.where(lanes == 0, 1.0, 0.0).astype(bf16)
    for copy in started:
        copy.wait()


    def one_image(image, carry):
        begin, finish = image_span(bounds, m, image, base)

        @pl.when((finish > LEAD) & (begin < LEAD + own))
        def _():
            key_start = pl.multiple_of((begin >> 4) << 4, 16)
            key_rows = pl.ds(key_start, WINDOW)
            key_block(keys, 0, begin, finish, key_start, key_aug)
            turned = keys[0, key_rows, :].astype(f32).T
            key_t[0] = turned[:HEAD_DIM].astype(bf16)
            key_t[1] = turned[HEAD_DIM:].astype(bf16)
            first_tile = jnp.maximum(begin - LEAD, 0) >> 8
            last_tile = (jnp.minimum(finish - LEAD, own) + TILE - 1) >> 8

            def one_tile(tile, carry):
                spot = pl.multiple_of(tile * TILE, TILE)
                here = pl.ds(spot, TILE)
                scaled = queries[0, here, :].astype(f32) * (HEAD_DIM**-0.5)
                grad = grads[ here, :].astype(f32)
                dots = (grad * result[ here, :].astype(f32)).T
                inside_lane = (lane_row + (spot + LEAD) >= begin) & (lane_row + (spot + LEAD) < finish)
                both = zip(split_heads(scaled, lanes), split_heads(grad, lanes))
                pieces = []
                add_key, add_value = None, None
                for h, (query, grad_h) in enumerate(both):
                    row = (m * 2 + h) * blocks + tile
                    level = jnp.where(inside_lane, stats[pl.ds(row, 1), :], -negative_fill)
                    row_dot = jnp.sum(
                        dots[h * HEAD_DIM : (h + 1) * HEAD_DIM], axis=0, keepdims=True
                    )
                    aug = jnp.concatenate([query, query_mark], axis=1)
                    shares = jnp.exp(product_nt(key_aug[...], aug) - level)
                    grad_share = product_nt(values[0, key_rows, :], grad_h)
                    grad_scores = (shares * (grad_share - row_dot)).astype(bf16)
                    value_part = product(shares.astype(bf16), grad_h)
                    key_part = product(grad_scores, query)
                    add_value = value_part if h == 0 else add_value + value_part
                    add_key = key_part if h == 0 else add_key + key_part
                    pieces.append(product(key_t[h], grad_scores))
                acc_value[ key_rows, :] += add_value
                acc_key[ key_rows, :] += add_key
                acc_query[ here, :] += jnp.concatenate(pieces, axis=0).T * (HEAD_DIM**-0.5)
                return carry

            lax.fori_loop(first_tile, last_tile, one_tile, 0)

        return carry

    lax.fori_loop(0, image_count, one_image, 0)

    edge_rows = grad_before.shape[0]
    edge[0, : edge_rows - HALO, :] = jnp.zeros((edge_rows - HALO, 2 * PAIR), bf16)
    edge[1, HALO:, :] = jnp.zeros((edge_rows - HALO, 2 * PAIR), bf16)
    started = [pltpu.make_async_copy(acc_query, grad_query, sem)]
    for which, acc in enumerate((acc_key, acc_value)):
        columns = pl.ds(which * PAIR, PAIR)
        edge[0, edge_rows - HALO :, which * PAIR : (which + 1) * PAIR] = acc[LEAD - HALO : LEAD, :].astype(bf16)
        edge[1, :HALO, which * PAIR : (which + 1) * PAIR] = acc[LEAD + own : LEAD + own + HALO, :].astype(bf16)
        started.append(pltpu.make_async_copy(acc.at[pl.ds(LEAD, own)], grad_pairs.at[:, columns], sem))
    started.append(pltpu.make_async_copy(edge.at[0], grad_before, sem))
    started.append(pltpu.make_async_copy(edge.at[1], grad_after, sem))
    for copy in started:
        copy.start()
    for copy in started:
        copy.wait()


def any_specs(count):
    return [pl.BlockSpec(memory_space=pl.ANY)] * count


def attend(info, bounds, qkv, before, after):
    micro_count, blocks, rows, _ = qkv.shape
    own = blocks * rows
    span = LEAD + own + LEAD
    stat_rows = micro_count * 2 * blocks
    return pl.pallas_call(
        attend_kernel,
        grid_spec=pltpu.PrefetchScalarGridSpec(
            num_scalar_prefetch=2,
            grid=(1,),
            in_specs=any_specs(3),
            out_specs=any_specs(1) + [pl.BlockSpec((stat_rows, TILE), lambda g, a, b: (0, 0))],
            scratch_shapes=[
                pltpu.VMEM((micro_count, own, PAIR), bf16),
                pltpu.VMEM((micro_count, span, PAIR), bf16),
                pltpu.VMEM((micro_count, span, PAIR), bf16),
                pltpu.VMEM((micro_count, own, PAIR), f32),
                pltpu.VMEM((micro_count, own, PAIR), bf16),
                pltpu.VMEM((WINDOW, 2 * PAIR), bf16),
                pltpu.VMEM((2, HEAD_DIM + 16, WINDOW), bf16),
                pltpu.SemaphoreType.DMA,
            ],
        ),
        out_shape=[
            jax.ShapeDtypeStruct((blocks, micro_count, rows, PAIR), bf16),
            jax.ShapeDtypeStruct((stat_rows, TILE), f32),
        ],
    )(info, bounds, qkv, before, after)


def attend_back(m, info, bounds, qkv, before, after, mixed, grad_mixed, stats):
    _, blocks, rows, _ = qkv.shape
    own = blocks * rows
    span = LEAD + own + LEAD
    edge_rows = -(-HALO // rows) * rows
    return pl.pallas_call(
        functools.partial(attend_back_kernel, m),
        grid_spec=pltpu.PrefetchScalarGridSpec(
            num_scalar_prefetch=2,
            grid=(1,),
            in_specs=any_specs(4 + blocks) + [pl.BlockSpec(stats.shape, lambda g, a, b: (0, 0))],
            out_specs=any_specs(4),
            scratch_shapes=[
                pltpu.VMEM((1, own, PAIR), bf16),
                pltpu.VMEM((1, span, PAIR), bf16),
                pltpu.VMEM((1, span, PAIR), bf16),
                pltpu.VMEM((own, PAIR), bf16),
                pltpu.VMEM((own, PAIR), bf16),
                pltpu.VMEM((WINDOW, 2 * PAIR), bf16),
                pltpu.VMEM((2, HEAD_DIM, WINDOW), bf16),
                pltpu.VMEM((own, PAIR), f32),
                pltpu.VMEM((span, PAIR), f32),
                pltpu.VMEM((span, PAIR), f32),
                pltpu.VMEM((2, edge_rows, 2 * PAIR), bf16),
                pltpu.SemaphoreType.DMA,
            ],
        ),
        out_shape=[
            jax.ShapeDtypeStruct((own, PAIR), f32),
            jax.ShapeDtypeStruct((own, 2 * PAIR), f32),
            jax.ShapeDtypeStruct((edge_rows, 2 * PAIR), bf16),
            jax.ShapeDtypeStruct((edge_rows, 2 * PAIR), bf16),
        ],
    )(info, bounds, qkv, before, after, mixed, *grad_mixed, stats)


def join_kernel(info, query, pairs, head, tail, joined):
    blocks, rows, _ = joined.shape
    edge_blocks = head.shape[0] // rows
    for tile in range(blocks):
        here = pl.ds(tile * rows, rows)
        total = pairs[here, :]
        if tile < edge_blocks:
            total = total + head[here, :].astype(f32)
        if tile >= blocks - edge_blocks:
            total = total + tail[pl.ds((tile - (blocks - edge_blocks)) * rows, rows), :].astype(f32)
        target = jnp.bitwise_xor(info[1], tile)
        joined[target, :, :PAIR] = query[here, :].astype(bf16)
        joined[target, :, PAIR:] = total.astype(bf16)


def join_grads(info, grad_query, grad_pairs, head, tail, rows):
    own = grad_query.shape[0]
    blocks = own // rows
    ins = (grad_query, grad_pairs, head, tail)
    return pl.pallas_call(
        join_kernel,
        grid_spec=pltpu.PrefetchScalarGridSpec(
            num_scalar_prefetch=1,
            grid=(1,),
            in_specs=[pl.BlockSpec(item.shape, lambda g, i: (0, 0)) for item in ins],
            out_specs=pl.BlockSpec((blocks, rows, 3 * PAIR), lambda g, i: (0, 0, 0)),
        ),
        out_shape=jax.ShapeDtypeStruct((blocks, rows, 3 * PAIR), bf16),
    )(info, *ins)


def layer_norm_parts(values, gain, shift):
    center = values - jnp.mean(values, axis=-1, keepdims=True)
    inverse = lax.rsqrt(jnp.mean(center * center, axis=-1, keepdims=True) + epsilon)
    normal = center * inverse
    return (normal * gain + shift, normal, inverse)


def layer_norm_back(grad_normed, normal, inverse, gain):
    scaled = grad_normed * gain
    centered = scaled - jnp.mean(scaled, axis=-1, keepdims=True)
    return inverse * (centered - normal * jnp.mean(scaled * normal, axis=-1, keepdims=True))


def plane_tokens(block, order):
    near, far = gather_bits(block, order)
    held = places(order)
    half = PLANE // 2
    at = {r: (near[p] if p < half else far[p - half]) for p, r in enumerate(held)}
    return jnp.stack([at[r] for r in range(PLANE)])


def plane_scatter(partial, order):
    pieces = {r: partial[r].astype(bf16) for r in range(PLANE)}
    left = list(range(PLANE))
    total = None
    for step, bit in enumerate(order):
        keep = [r for r in left if not r & bit]
        got = swap(jnp.stack([pieces[r | bit] for r in keep]), bit)
        last = step == len(order) - 1
        for position, r in enumerate(keep):
            added = pieces[r].astype(f32) + got[position].astype(f32)
            pieces[r] = added if last else added.astype(bf16)
        left = keep
    return pieces[0]


def body(
    tokens,
    ln1_gain,
    ln1_bias,
    qkv_weight,
    q_bias,
    v_bias,
    out_weight,
    out_bias,
    ln2_gain,
    ln2_bias,
    fc1_weight,
    fc1_bias,
    fc2_weight,
    fc2_bias,
    image_ids,
    image_starts,
    cotangent,
):
    micro_count, tok_dev, model_width = tokens.shape
    n = lax.axis_size("seq")
    own_tokens = micro_count * tok_dev
    plane_rows = PLANE * tok_dev
    stream_len = tok_dev * n
    me = lax.axis_index("seq")
    mine = jnp.bitwise_and(me, PLANE - 1)
    base = (me - mine) * tok_dev
    info = jnp.stack([me, mine, base]).astype(jnp.int32)
    bounds = jnp.concatenate(
        [image_starts, jnp.full((micro_count, 1), stream_len, jnp.int32)], axis=1
    )
    plane_bits = [1, 2, 4]
    depth_bits = []
    bit = PLANE
    while bit < n:
        depth_bits.append(bit)
        bit *= 2

    wide_parts = fc1_weight.shape[1] // model_width
    shards = [out_weight]
    shards += [fc1_weight[:, k * model_width : (k + 1) * model_width] for k in range(wide_parts)]
    every = lax.all_gather(jnp.concatenate(shards + [fc2_weight], axis=0), "seq")
    step = out_weight.shape[0]
    out_full = every[:, :step].reshape(model_width, model_width)
    up_full = every[:, step : (1 + wide_parts) * step].reshape(n, wide_parts, step, model_width)
    up_full = up_full.transpose(0, 2, 1, 3).reshape(model_width, wide_parts * model_width)
    down_full = every[:, (1 + wide_parts) * step :].reshape(wide_parts * model_width, model_width)

    small = [ln1_gain, ln1_bias, q_bias, v_bias, out_bias, ln2_gain, ln2_bias, fc2_bias, fc1_bias]
    shard_rows = qkv_weight.shape[0]
    small_len = sum(item.shape[0] for item in small)
    spare_rows = -(-small_len // (8 * 3 * PAIR)) * 8
    small_rows = jnp.pad(jnp.concatenate(small), (0, spare_rows * 3 * PAIR - small_len))
    small_rows = small_rows.reshape(spare_rows, 3 * PAIR)
    by_pair = qkv_weight.reshape(shard_rows, 3, PLANE, PAIR).transpose(2, 0, 1, 3)
    by_pair = by_pair.reshape(PLANE, shard_rows, 3 * PAIR)
    outgoing = jnp.concatenate(
        [by_pair, jnp.broadcast_to(small_rows[None], (PLANE,) + small_rows.shape)], axis=1
    )
    arrived = [lax.dynamic_index_in_dim(outgoing, mine, 0, keepdims=False)]
    for r in range(1, PLANE):
        arrived.append(
            swap(lax.dynamic_index_in_dim(outgoing, jnp.bitwise_xor(mine, r), 0, keepdims=False), r)
        )
    current = jnp.stack(arrived)
    for bit in depth_bits:
        current = jnp.concatenate([current, swap(current, bit)], axis=0)
    pair_blocks = turn_blocks(info, current)
    pair_weight = pair_blocks[:, :shard_rows].reshape(n * shard_rows, 3 * PAIR)
    small_all = pair_blocks[:, shard_rows:].reshape(n, -1).astype(f32)
    small_full = []
    offset = 0
    for item in small:
        width = item.shape[0]
        small_full.append(small_all[:, offset : offset + width].reshape(n * width))
        offset += width
    gain_one, shift_one, q_shift, v_shift, out_shift, gain_two, shift_two, down_shift, up_shift = small_full

    plane_stream = jnp.stack(
        [
            plane_tokens(tokens[m], [2, 4, 1] if m % 2 == 0 else [4, 2, 1])
            for m in range(micro_count)
        ]
    )
    plane_flat = plane_stream.reshape(micro_count * plane_rows, model_width)
    normed, _, _ = layer_norm_parts(plane_flat.astype(f32), gain_one, shift_one)
    normed_low = normed.astype(bf16)
    pair_shift = jnp.concatenate(
        [
            lax.dynamic_slice_in_dim(q_shift, mine * PAIR, PAIR),
            jnp.zeros((PAIR,), f32),
            lax.dynamic_slice_in_dim(v_shift, mine * PAIR, PAIR),
        ]
    )
    qkv = (product(normed_low, pair_weight) + pair_shift).astype(bf16)
    qkv = qkv.reshape(micro_count, PLANE, tok_dev, 3 * PAIR)

    edge_blocks = -(-HALO // tok_dev)

    def plane_block(index):
        return lax.dynamic_index_in_dim(qkv, jnp.bitwise_xor(mine, index), 1, keepdims=False)[:, :, PAIR:]

    last_rows = jnp.concatenate([plane_block(PLANE - edge_blocks + k) for k in range(edge_blocks)], axis=1)
    first_rows = jnp.concatenate([plane_block(k) for k in range(edge_blocks)], axis=1)
    before = shift_plane(last_rows[:, edge_blocks * tok_dev - HALO :], 1)
    after = shift_plane(first_rows[:, :HALO], -1)
    mixed_pair, stats = attend(info, bounds, qkv, before, after)

    def column(r):
        return jnp.bitwise_xor(mine, r) * PAIR

    mixed_low = jnp.zeros((own_tokens, model_width), bf16)
    for r in range(PLANE):
        part = mixed_pair[r] if r == 0 else swap(mixed_pair[r], r)
        mixed_low = lax.dynamic_update_slice(mixed_low, part.reshape(own_tokens, PAIR), (0, column(r)))

    stream = tokens.reshape(own_tokens, model_width).astype(f32)
    cotangent_low = cotangent.reshape(own_tokens, model_width)
    middle = stream + product(mixed_low, out_full) + out_shift
    normed_two, normal_two, inverse_two = layer_norm_parts(middle, gain_two, shift_two)
    normed_two_low = normed_two.astype(bf16)
    hidden = product(normed_two_low, up_full) + up_shift
    gate = jax.nn.sigmoid(1.702 * hidden)
    active_low = (hidden * gate).astype(bf16)
    grad_active = product_nt(cotangent_low, down_full)
    grad_hidden_low = (grad_active * (gate + 1.702 * hidden * gate * (1.0 - gate))).astype(bf16)

    order_a = [1, 2, 4] + depth_bits[::-1]
    order_b = [1, 4, 2] + depth_bits[::-1]
    grad_down = product_tn(active_low, cotangent_low).astype(bf16).reshape(n, -1, model_width)
    half = grad_down.shape[1] // 2
    down = [Scatter(me, grad_down[:, :half], order_a), Scatter(me, grad_down[:, half:], order_b)]
    for part in down:
        part.swap()
    grad_hidden_low = tie(grad_hidden_low, *[part.send for part in down])

    grad_normed_two = product_nt(grad_hidden_low, up_full)
    grad_middle = cotangent_low.astype(f32) + layer_norm_back(
        grad_normed_two, normal_two, inverse_two, gain_two
    )
    grad_branch_low = grad_middle.astype(bf16)
    grad_mixed_low = product_nt(grad_branch_low, out_full).astype(bf16)
    grad_parts = []
    for r in range(PLANE):
        part = lax.dynamic_slice(grad_mixed_low, (0, column(r)), (own_tokens, PAIR))
        part = part.reshape(micro_count, tok_dev, PAIR)
        grad_parts.append(part if r == 0 else swap(part, r))

    for part in down:
        part.advance(grad_branch_low)

    later = tie(normed_two_low, grad_mixed_low)
    grad_up = product_tn(later, grad_hidden_low).astype(bf16).reshape(n, step, -1)
    up = [Scatter(me, grad_up[:, : step // 2], order_a), Scatter(me, grad_up[:, step // 2 :], order_b)]
    for part in up:
        part.swap()
    grad_out_weight = product_tn(mixed_low, grad_branch_low).astype(bf16).reshape(n, step, model_width)
    out_part = Scatter(me, grad_out_weight, order_b)
    out_part.swap()
    result = middle + product(tie(active_low, grad_mixed_low), down_full) + down_shift
    result_low = result.astype(bf16)
    moving = up + [out_part]
    for part in moving:
        part.advance()

    grad_flat = []
    before_back = [part.send for part in moving] + [result_low]
    for m in range(micro_count):
        own_grad = tie(grad_parts[0], *before_back)
        grad_query, grad_pairs, grad_before, grad_after = attend_back(
            m, info, bounds, qkv, before, after, mixed_pair, [own_grad] + grad_parts[1:], stats
        )
        from_next = shift_plane(grad_before, -1)
        from_last = shift_plane(grad_after, 1)
        if m == 0:
            for part in down:
                part.advance(grad_before)
            before_back = [part.send for part in down]
        joined = join_grads(info, grad_query, grad_pairs, from_last, from_next, tok_dev)
        grad_flat.append(joined.reshape(plane_rows, 3 * PAIR))
        last_grad = grad_before

    for part in moving + down:
        part.advance(last_grad)

    grad_normed = []
    for m in range(micro_count):
        grad_plane = product_nt(grad_flat[m], pair_weight).reshape(PLANE, tok_dev, model_width)
        grad_normed.append(plane_scatter(grad_plane, [1, 2, 4] if m % 2 == 0 else [1, 4, 2]))
    grad_normed = jnp.concatenate(grad_normed, axis=0)
    for part in moving + down:
        while part.order:
            part.advance()
    down_sum = jnp.concatenate([part.total() for part in down], axis=0)
    up_sum = jnp.concatenate([part.total() for part in up], axis=0)
    out_sum = out_part.total()
    _, normal_one, inverse_one = layer_norm_parts(stream, gain_one, shift_one)
    grad_stream = grad_middle + layer_norm_back(grad_normed, normal_one, inverse_one, gain_one)
    grad_flat = jnp.concatenate(grad_flat, axis=0)

    grad_pair_weight = product_tn(normed_low, grad_flat)
    column_sum = jnp.sum(grad_flat.astype(f32), axis=0)
    wide = pair_weight.astype(f32)
    grad_shift_one = jnp.sum(wide * column_sum, axis=1)
    grad_gain_one = jnp.sum(wide * grad_pair_weight, axis=1)
    grad_gain_one = (grad_gain_one - shift_one * grad_shift_one) / gain_one

    def at_columns(part):
        return lax.dynamic_update_slice(jnp.zeros((model_width,), f32), part, (mine * PAIR,))

    small_grads = [
        grad_gain_one,
        grad_shift_one,
        at_columns(column_sum[:PAIR]),
        at_columns(column_sum[2 * PAIR :]),
        jnp.sum(grad_branch_low.astype(f32), axis=0),
        jnp.sum(grad_normed_two * normal_two, axis=0),
        jnp.sum(grad_normed_two, axis=0),
        jnp.sum(cotangent_low.astype(f32), axis=0),
        jnp.sum(grad_hidden_low.astype(f32), axis=0),
    ]
    small_out = jnp.concatenate([item.reshape(n, -1) for item in small_grads], axis=1).astype(bf16)
    small_out = jnp.pad(small_out, ((0, 0), (0, spare_rows * 3 * PAIR - small_len)))
    small_out = small_out.reshape(n, spare_rows, 3 * PAIR)
    leaving = jnp.concatenate(
        [grad_pair_weight.astype(bf16).reshape(n, shard_rows, 3 * PAIR), small_out], axis=1
    )
    turned = turn_blocks(info, leaving)
    size = n
    for bit in depth_bits[::-1]:
        size //= 2
        got = swap(turned[size:], bit)
        turned = (turned[:size].astype(f32) + got.astype(f32)).astype(bf16)
    qkv_sum = jnp.zeros((shard_rows, 3, model_width), f32)
    small_sum = jnp.zeros((spare_rows, 3 * PAIR), f32)
    for r in range(PLANE):
        part = turned[r] if r == 0 else swap(turned[r], r)
        columns = part[:shard_rows].reshape(shard_rows, 3, PAIR).astype(f32)
        qkv_sum = lax.dynamic_update_slice(qkv_sum, columns, (0, 0, column(r)))
        small_sum = small_sum + part[shard_rows:].astype(f32)
    qkv_sum = qkv_sum.reshape(shard_rows, 3 * model_width)
    small_sum = small_sum.reshape(-1)
    sums = []
    offset = 0
    for item in small:
        sums.append(small_sum[offset : offset + item.shape[0]])
        offset += item.shape[0]

    return (
        result_low.reshape(micro_count, tok_dev, model_width),
        grad_stream.astype(bf16).reshape(micro_count, tok_dev, model_width),
        sums[0],
        sums[1],
        qkv_sum,
        sums[2],
        sums[3],
        out_sum,
        sums[4],
        sums[5],
        sums[6],
        up_sum,
        sums[8],
        down_sum,
        sums[7],
    )


def solution(mesh):
    return jax.shard_map(
        body,
        mesh=mesh,
        in_specs=(
            P(None, "seq", None),
            P("seq"),
            P("seq"),
            P("seq", None),
            P("seq"),
            P("seq"),
            P("seq", None),
            P("seq"),
            P("seq"),
            P("seq"),
            P("seq", None),
            P("seq"),
            P("seq", None),
            P("seq"),
            P(None, "seq"),
            P(),
            P(None, "seq", None),
        ),
        out_specs=(
            P(None, "seq", None),
            P(None, "seq", None),
            P("seq"),
            P("seq"),
            P("seq", None),
            P("seq"),
            P("seq"),
            P("seq", None),
            P("seq"),
            P("seq"),
            P("seq"),
            P("seq", None),
            P("seq"),
            P("seq", None),
            P("seq"),
        ),
        check_vma=False,
    )
```

```python
import functools

import jax
import jax.numpy as jnp
from jax import lax
from jax.experimental import pallas as pl
from jax.experimental.pallas import tpu as pltpu
from jax.sharding import PartitionSpec as P

HEAD_DIM = 64
IMG_TOK = 577
PLANE = 8
PAIR = 2 * HEAD_DIM
HALO = IMG_TOK - 1
LEAD = 640
WINDOW = 640
TILE = 256

epsilon = 1e-05
negative_fill = -1e30
bf16 = jnp.bfloat16
f32 = jnp.float32


def product(left, right):
    return jnp.dot(left, right, preferred_element_type=f32)


def product_tn(left, right):
    return lax.dot_general(left, right, (((0,), (0,)), ((), ())), preferred_element_type=f32)


def product_nt(left, right):
    return lax.dot_general(left, right, (((1,), (1,)), ((), ())), preferred_element_type=f32)


def swap(block, bit):
    n = lax.axis_size("seq")
    return lax.ppermute(block, "seq", [(i, i ^ bit) for i in range(n)])


def shift_plane(block, planes):
    n = lax.axis_size("seq")
    step = planes * PLANE
    return lax.ppermute(block, "seq", [(i, i + step) for i in range(n) if 0 <= i + step < n])


def places(order):
    held = [0]
    for bit in order:
        held = held + [r ^ bit for r in held]
    return held


def gather_bits(block, order):
    current = block[None]
    for bit in order[:-1]:
        current = jnp.concatenate([current, swap(current, bit)], axis=0)
    return current, swap(current, order[-1])


def tie(value, *earlier):
    return lax.optimization_barrier((value,) + earlier)[0]


def own_bit(me, bit):
    return jnp.where(jnp.bitwise_and(me, bit) != 0, 1, 0)


def pick(block, axis, index):
    return lax.dynamic_index_in_dim(block, index, axis, keepdims=False)


def exchange(blocks):
    bits = PLANE.bit_length() - 1
    cube = blocks.reshape((2,) * bits + blocks.shape[1:])
    for axis in reversed(range(bits)):
        got = swap(lax.index_in_dim(cube, 1, axis, keepdims=False), 1 << (bits - 1 - axis))
        cube = jnp.stack([lax.index_in_dim(cube, 0, axis, keepdims=False), got], axis=axis)
    return cube.reshape(blocks.shape)


class Scatter:
    def __init__(self, me, partials, order):
        count = partials[0].shape[0]
        depth = count.bit_length() - 1
        self.me = me
        self.blocks = [item.reshape((2,) * depth + item.shape[1:]) for item in partials]
        self.bits = [1 << (depth - 1 - axis) for axis in range(depth)]
        self.order = list(order)
        self.got = None
        self.split()

    def half(self, axis, index):
        if self.got is None:
            picked = [pick(block, axis, index) for block in self.blocks]
            return picked[0] if len(picked) == 1 else jnp.concatenate(picked, axis=-2)
        kept = pick(self.blocks[0], axis, index).astype(f32)
        return (kept + pick(self.got, axis, index).astype(f32)).astype(bf16)

    def split(self):
        self.bit = self.order.pop(0)
        axis = self.bits.index(self.bit)
        self.bits.pop(axis)
        mine = own_bit(self.me, self.bit)
        self.send, keep = self.half(axis, 1 - mine), self.half(axis, mine)
        self.blocks, self.got = [keep], None

    def swap(self):
        self.got = swap(self.send, self.bit)

    def advance(self, *earlier):
        if earlier:
            self.got = tie(self.got, *earlier)
        self.split()
        self.swap()

    def total(self):
        return self.blocks[0].astype(f32) + self.got.astype(f32)


def turn_kernel(info, blocks, turned):
    for r in range(blocks.shape[0]):
        turned[r] = blocks[jnp.bitwise_xor(info[0], r)]


def turn_blocks(info, blocks):
    return pl.pallas_call(
        turn_kernel,
        grid_spec=pltpu.PrefetchScalarGridSpec(
            num_scalar_prefetch=1,
            grid=(1,),
            in_specs=[pl.BlockSpec(blocks.shape, lambda g, i: (0, 0, 0))],
            out_specs=pl.BlockSpec(blocks.shape, lambda g, i: (0, 0, 0)),
        ),
        out_shape=jax.ShapeDtypeStruct(blocks.shape, blocks.dtype),
    )(info, blocks)


def load_rows(micros, place_in_plane, qkv, before, after, queries, keys, values, sem):
    blocks, rows = qkv.shape[1], qkv.shape[2]
    own = blocks * rows
    for buffer in (keys, values):
        for slot in range(len(micros)):
            buffer[slot, 0 : LEAD - HALO, :] = jnp.zeros((LEAD - HALO, PAIR), bf16)
            tail = buffer.shape[1] - (LEAD + own + HALO)
            buffer[slot, LEAD + own + HALO :, :] = jnp.zeros((tail, PAIR), bf16)
    started = []
    for slot, m in enumerate(micros):
        for r in range(blocks):
            spot = pl.multiple_of(jnp.bitwise_xor(place_in_plane, r) * rows, rows)
            started += [
                pltpu.make_async_copy(
                    qkv.at[m, r, :, pl.ds(0, PAIR)], queries.at[slot, pl.ds(spot, rows)], sem
                ),
                pltpu.make_async_copy(
                    qkv.at[m, r, :, pl.ds(PAIR, PAIR)], keys.at[slot, pl.ds(LEAD + spot, rows)], sem
                ),
                pltpu.make_async_copy(
                    qkv.at[m, r, :, pl.ds(2 * PAIR, PAIR)], values.at[slot, pl.ds(LEAD + spot, rows)], sem
                ),
            ]
        for which, buffer in enumerate((keys, values)):
            columns = pl.ds(which * PAIR, PAIR)
            started += [
                pltpu.make_async_copy(
                    before.at[m, :, columns], buffer.at[slot, pl.ds(LEAD - HALO, HALO)], sem
                ),
                pltpu.make_async_copy(
                    after.at[m, :, columns], buffer.at[slot, pl.ds(LEAD + own, HALO)], sem
                ),
            ]
    return started


def image_span(bounds, m, image, base):
    begin = bounds[m, image] - base + LEAD
    finish = bounds[m, image + 1] - base + LEAD
    return begin, finish


def key_block(keys, m, begin, finish, key_start, key_aug):
    key_aug[:, :PAIR] = keys[m, pl.ds(key_start, WINDOW), :]
    rows = key_start + lax.broadcasted_iota(jnp.int32, (WINDOW, PAIR), 0)
    inside = (rows >= begin) & (rows < finish)
    key_aug[:, PAIR:] = jnp.where(inside, 0.0, negative_fill).astype(bf16)


def split_heads(rows_f32, lanes):
    first = jnp.where(lanes < HEAD_DIM, rows_f32, 0.0).astype(bf16)
    second = jnp.where(lanes >= HEAD_DIM, rows_f32, 0.0).astype(bf16)
    return first, second


def attend_kernel(
    info, bounds, qkv, before, after, mixed, stats, queries, keys, values, result, result_low, key_aug, value_t, sem
):
    micro_count, blocks, rows, _ = qkv.shape
    own = blocks * rows
    place_in_plane, base = info[1], info[2]
    image_count = bounds.shape[1] - 1
    started = load_rows(range(micro_count), place_in_plane, qkv, before, after, queries, keys, values, sem)
    for copy in started:
        copy.start()
    value_t[:, HEAD_DIM:, :] = jnp.ones((2, 16, WINDOW), bf16)
    lanes = lax.broadcasted_iota(jnp.int32, (TILE, PAIR), 1)
    rows_iota = lax.broadcasted_iota(jnp.int32, (TILE, PAIR), 0)
    lane_row = lax.broadcasted_iota(jnp.int32, (1, TILE), 1)
    query_mark = jnp.where(lanes == 0, 1.0, 0.0).astype(bf16)
    for copy in started:
        copy.wait()

    for m in range(micro_count):

        def one_image(image, carry):
            begin, finish = image_span(bounds, m, image, base)

            @pl.when((finish > LEAD) & (begin < LEAD + own))
            def _():
                key_start = pl.multiple_of((begin >> 4) << 4, 16)
                key_block(keys, m, begin, finish, key_start, key_aug)
                turned = values[m, pl.ds(key_start, WINDOW), :].astype(f32).T
                value_t[0, :HEAD_DIM, :] = turned[:HEAD_DIM].astype(bf16)
                value_t[1, :HEAD_DIM, :] = turned[HEAD_DIM:].astype(bf16)
                first_tile = jnp.maximum(begin - LEAD, 0) >> 8
                last_tile = (jnp.minimum(finish - LEAD, own) + TILE - 1) >> 8

                def one_tile(tile, carry):
                    spot = pl.multiple_of(tile * TILE, TILE)
                    scaled = queries[m, pl.ds(spot, TILE), :].astype(f32) * (HEAD_DIM**-0.5)
                    pieces = []
                    inside_lane = (lane_row + (spot + LEAD) >= begin) & (lane_row + (spot + LEAD) < finish)
                    for h, query in enumerate(split_heads(scaled, lanes)):
                        aug = jnp.concatenate([query, query_mark], axis=1)
                        scores = product_nt(key_aug[...], aug)
                        peak = jnp.max(scores, axis=0, keepdims=True)
                        weights = jnp.exp(scores - peak).astype(bf16)
                        out = product(value_t[h], weights)
                        total = out[HEAD_DIM : HEAD_DIM + 1]
                        pieces.append(out[:HEAD_DIM] / total)
                        row = (m * 2 + h) * blocks + tile
                        stats[pl.ds(row, 1), :] = jnp.where(
                            inside_lane, peak + jnp.log(total), stats[pl.ds(row, 1), :]
                        )
                    value = jnp.concatenate(pieces, axis=0).T
                    place_row = rows_iota + (spot + LEAD)
                    inside = (place_row >= begin) & (place_row < finish)
                    result[m, pl.ds(spot, TILE), :] = jnp.where(
                        inside, value, result[m, pl.ds(spot, TILE), :]
                    )
                    return carry

                lax.fori_loop(first_tile, last_tile, one_tile, 0)

            return carry

        lax.fori_loop(0, image_count, one_image, 0)

    result_low[...] = result[...].astype(bf16)
    started = []
    for m in range(micro_count):
        for r in range(blocks):
            spot = pl.multiple_of(jnp.bitwise_xor(place_in_plane, r) * rows, rows)
            started.append(pltpu.make_async_copy(result_low.at[m, pl.ds(spot, rows)], mixed.at[r, m], sem))
    for copy in started:
        copy.start()
    for copy in started:
        copy.wait()


def attend_back_kernel(m, info, bounds, qkv, before, after, mixed, *refs):
    blocks, rows = qkv.shape[1], qkv.shape[2]
    own = blocks * rows
    grad_mixed, refs = refs[:blocks], refs[blocks:]
    stats, grad_query, grad_pairs, grad_before, grad_after, refs = *refs[:5], refs[5:]
    queries, keys, values, result, grads, key_aug, key_t, acc_query, acc_key, acc_value, edge, sem = refs
    place_in_plane, base = info[1], info[2]
    image_count = bounds.shape[1] - 1
    started = load_rows([m], place_in_plane, qkv, before, after, queries, keys, values, sem)
    for r in range(blocks):
        spot = pl.multiple_of(jnp.bitwise_xor(place_in_plane, r) * rows, rows)
        started += [
            pltpu.make_async_copy(mixed.at[r, m], result.at[pl.ds(spot, rows)], sem),
            pltpu.make_async_copy(grad_mixed[r].at[m], grads.at[pl.ds(spot, rows)], sem),
        ]
    for copy in started:
        copy.start()
    acc_query[...] = jnp.zeros_like(acc_query)
    acc_key[...] = jnp.zeros_like(acc_key)
    acc_value[...] = jnp.zeros_like(acc_value)
    lanes = lax.broadcasted_iota(jnp.int32, (TILE, PAIR), 1)
    lane_row = lax.broadcasted_iota(jnp.int32, (1, TILE), 1)
    query_mark = jnp.where(lanes == 0, 1.0, 0.0).astype(bf16)
    for copy in started:
        copy.wait()


    def one_image(image, carry):
        begin, finish = image_span(bounds, m, image, base)

        @pl.when((finish > LEAD) & (begin < LEAD + own))
        def _():
            key_start = pl.multiple_of((begin >> 4) << 4, 16)
            key_rows = pl.ds(key_start, WINDOW)
            key_block(keys, 0, begin, finish, key_start, key_aug)
            turned = keys[0, key_rows, :].astype(f32).T
            key_t[0] = turned[:HEAD_DIM].astype(bf16)
            key_t[1] = turned[HEAD_DIM:].astype(bf16)
            first_tile = jnp.maximum(begin - LEAD, 0) >> 8
            last_tile = (jnp.minimum(finish - LEAD, own) + TILE - 1) >> 8

            def one_tile(tile, carry):
                spot = pl.multiple_of(tile * TILE, TILE)
                here = pl.ds(spot, TILE)
                scaled = queries[0, here, :].astype(f32) * (HEAD_DIM**-0.5)
                grad = grads[ here, :].astype(f32)
                dots = (grad * result[ here, :].astype(f32)).T
                inside_lane = (lane_row + (spot + LEAD) >= begin) & (lane_row + (spot + LEAD) < finish)
                both = zip(split_heads(scaled, lanes), split_heads(grad, lanes))
                pieces = []
                add_key, add_value = None, None
                for h, (query, grad_h) in enumerate(both):
                    row = (m * 2 + h) * blocks + tile
                    level = jnp.where(inside_lane, stats[pl.ds(row, 1), :], -negative_fill)
                    row_dot = jnp.sum(
                        dots[h * HEAD_DIM : (h + 1) * HEAD_DIM], axis=0, keepdims=True
                    )
                    aug = jnp.concatenate([query, query_mark], axis=1)
                    shares = jnp.exp(product_nt(key_aug[...], aug) - level)
                    grad_share = product_nt(values[0, key_rows, :], grad_h)
                    grad_scores = (shares * (grad_share - row_dot)).astype(bf16)
                    value_part = product(shares.astype(bf16), grad_h)
                    key_part = product(grad_scores, query)
                    add_value = value_part if h == 0 else add_value + value_part
                    add_key = key_part if h == 0 else add_key + key_part
                    pieces.append(product(key_t[h], grad_scores))
                acc_value[ key_rows, :] += add_value
                acc_key[ key_rows, :] += add_key
                acc_query[ here, :] += jnp.concatenate(pieces, axis=0).T * (HEAD_DIM**-0.5)
                return carry

            lax.fori_loop(first_tile, last_tile, one_tile, 0)

        return carry

    lax.fori_loop(0, image_count, one_image, 0)

    edge_rows = grad_before.shape[0]
    edge[0, : edge_rows - HALO, :] = jnp.zeros((edge_rows - HALO, 2 * PAIR), bf16)
    edge[1, HALO:, :] = jnp.zeros((edge_rows - HALO, 2 * PAIR), bf16)
    started = [pltpu.make_async_copy(acc_query, grad_query, sem)]
    for which, acc in enumerate((acc_key, acc_value)):
        columns = pl.ds(which * PAIR, PAIR)
        edge[0, edge_rows - HALO :, which * PAIR : (which + 1) * PAIR] = acc[LEAD - HALO : LEAD, :].astype(bf16)
        edge[1, :HALO, which * PAIR : (which + 1) * PAIR] = acc[LEAD + own : LEAD + own + HALO, :].astype(bf16)
        started.append(pltpu.make_async_copy(acc.at[pl.ds(LEAD, own)], grad_pairs.at[:, columns], sem))
    started.append(pltpu.make_async_copy(edge.at[0], grad_before, sem))
    started.append(pltpu.make_async_copy(edge.at[1], grad_after, sem))
    for copy in started:
        copy.start()
    for copy in started:
        copy.wait()


def cover(rows, passes):
    scores = 2 * rows * WINDOW
    return pl.CostEstimate(
        flops=4 * scores * PAIR, transcendentals=scores, bytes_accessed=passes * scores
    )


def any_specs(count):
    return [pl.BlockSpec(memory_space=pl.ANY)] * count


def attend(info, bounds, qkv, before, after):
    micro_count, blocks, rows, _ = qkv.shape
    own = blocks * rows
    span = LEAD + own + LEAD
    stat_rows = micro_count * 2 * blocks
    return pl.pallas_call(
        attend_kernel,
        grid_spec=pltpu.PrefetchScalarGridSpec(
            num_scalar_prefetch=2,
            grid=(1,),
            in_specs=any_specs(3),
            out_specs=any_specs(1) + [pl.BlockSpec((stat_rows, TILE), lambda g, a, b: (0, 0))],
            scratch_shapes=[
                pltpu.VMEM((micro_count, own, PAIR), bf16),
                pltpu.VMEM((micro_count, span, PAIR), bf16),
                pltpu.VMEM((micro_count, span, PAIR), bf16),
                pltpu.VMEM((micro_count, own, PAIR), f32),
                pltpu.VMEM((micro_count, own, PAIR), bf16),
                pltpu.VMEM((WINDOW, 2 * PAIR), bf16),
                pltpu.VMEM((2, HEAD_DIM + 16, WINDOW), bf16),
                pltpu.SemaphoreType.DMA,
            ],
        ),
        out_shape=[
            jax.ShapeDtypeStruct((blocks, micro_count, rows, PAIR), bf16),
            jax.ShapeDtypeStruct((stat_rows, TILE), f32),
        ],
        cost_estimate=cover(micro_count * own, 30),
    )(info, bounds, qkv, before, after)


def attend_back(m, info, bounds, qkv, before, after, mixed, grad_mixed, stats):
    _, blocks, rows, _ = qkv.shape
    own = blocks * rows
    span = LEAD + own + LEAD
    edge_rows = -(-HALO // rows) * rows
    return pl.pallas_call(
        functools.partial(attend_back_kernel, m),
        grid_spec=pltpu.PrefetchScalarGridSpec(
            num_scalar_prefetch=2,
            grid=(1,),
            in_specs=any_specs(4 + blocks) + [pl.BlockSpec(stats.shape, lambda g, a, b: (0, 0))],
            out_specs=any_specs(4),
            scratch_shapes=[
                pltpu.VMEM((1, own, PAIR), bf16),
                pltpu.VMEM((1, span, PAIR), bf16),
                pltpu.VMEM((1, span, PAIR), bf16),
                pltpu.VMEM((own, PAIR), bf16),
                pltpu.VMEM((own, PAIR), bf16),
                pltpu.VMEM((WINDOW, 2 * PAIR), bf16),
                pltpu.VMEM((2, HEAD_DIM, WINDOW), bf16),
                pltpu.VMEM((own, PAIR), f32),
                pltpu.VMEM((span, PAIR), f32),
                pltpu.VMEM((span, PAIR), f32),
                pltpu.VMEM((2, edge_rows, 2 * PAIR), bf16),
                pltpu.SemaphoreType.DMA,
            ],
        ),
        out_shape=[
            jax.ShapeDtypeStruct((own, PAIR), f32),
            jax.ShapeDtypeStruct((own, 2 * PAIR), f32),
            jax.ShapeDtypeStruct((edge_rows, 2 * PAIR), bf16),
            jax.ShapeDtypeStruct((edge_rows, 2 * PAIR), bf16),
        ],
        cost_estimate=cover(own, 35),
    )(info, bounds, qkv, before, after, mixed, *grad_mixed, stats)


def join_kernel(info, query, pairs, head, tail, joined):
    blocks, rows, _ = joined.shape
    edge_blocks = head.shape[0] // rows
    for tile in range(blocks):
        here = pl.ds(tile * rows, rows)
        total = pairs[here, :]
        if tile < edge_blocks:
            total = total + head[here, :].astype(f32)
        if tile >= blocks - edge_blocks:
            total = total + tail[pl.ds((tile - (blocks - edge_blocks)) * rows, rows), :].astype(f32)
        target = jnp.bitwise_xor(info[1], tile)
        joined[target, :, :PAIR] = query[here, :].astype(bf16)
        joined[target, :, PAIR:] = total.astype(bf16)


def join_grads(info, grad_query, grad_pairs, head, tail, rows):
    own = grad_query.shape[0]
    blocks = own // rows
    ins = (grad_query, grad_pairs, head, tail)
    return pl.pallas_call(
        join_kernel,
        grid_spec=pltpu.PrefetchScalarGridSpec(
            num_scalar_prefetch=1,
            grid=(1,),
            in_specs=[pl.BlockSpec(item.shape, lambda g, i: (0, 0)) for item in ins],
            out_specs=pl.BlockSpec((blocks, rows, 3 * PAIR), lambda g, i: (0, 0, 0)),
        ),
        out_shape=jax.ShapeDtypeStruct((blocks, rows, 3 * PAIR), bf16),
    )(info, *ins)


def layer_norm_parts(values, gain, shift):
    center = values - jnp.mean(values, axis=-1, keepdims=True)
    inverse = lax.rsqrt(jnp.mean(center * center, axis=-1, keepdims=True) + epsilon)
    normal = center * inverse
    return (normal * gain + shift, normal, inverse)


def layer_norm_back(grad_normed, normal, inverse, gain):
    scaled = grad_normed * gain
    centered = scaled - jnp.mean(scaled, axis=-1, keepdims=True)
    return inverse * (centered - normal * jnp.mean(scaled * normal, axis=-1, keepdims=True))


def plane_tokens(near, far, order):
    held = places(order)
    half = PLANE // 2
    at = {r: (near[p] if p < half else far[p - half]) for p, r in enumerate(held)}
    return jnp.stack([at[r] for r in range(PLANE)])


class PlaneScatter:
    def __init__(self, partial, order):
        self.pieces = [partial[r].astype(bf16) for r in range(PLANE)]
        self.left = list(range(PLANE))
        self.order = list(order)

    def start(self, *earlier):
        self.bit = self.order.pop(0)
        self.keep = [r for r in self.left if not r & self.bit]
        self.send = jnp.stack([self.pieces[r | self.bit] for r in self.keep])
        if earlier:
            self.send = tie(self.send, *earlier)
        self.got = swap(self.send, self.bit)

    def finish(self):
        for position, r in enumerate(self.keep):
            added = self.pieces[r].astype(f32) + self.got[position].astype(f32)
            self.pieces[r] = added.astype(bf16) if self.order else added
        self.left = self.keep


def body(
    tokens,
    ln1_gain,
    ln1_bias,
    qkv_weight,
    q_bias,
    v_bias,
    out_weight,
    out_bias,
    ln2_gain,
    ln2_bias,
    fc1_weight,
    fc1_bias,
    fc2_weight,
    fc2_bias,
    image_ids,
    image_starts,
    cotangent,
):
    micro_count, tok_dev, model_width = tokens.shape
    n = lax.axis_size("seq")
    own_tokens = micro_count * tok_dev
    plane_rows = PLANE * tok_dev
    stream_len = tok_dev * n
    me = lax.axis_index("seq")
    mine = jnp.bitwise_and(me, PLANE - 1)
    base = (me - mine) * tok_dev
    info = jnp.stack([me, mine, base]).astype(jnp.int32)
    bounds = jnp.concatenate(
        [image_starts, jnp.full((micro_count, 1), stream_len, jnp.int32)], axis=1
    )
    plane_bits = [1, 2, 4]
    depth_bits = []
    bit = PLANE
    while bit < n:
        depth_bits.append(bit)
        bit *= 2

    small = [ln1_gain, ln1_bias, q_bias, v_bias, out_bias, ln2_gain, ln2_bias, fc2_bias, fc1_bias]
    shard_rows = qkv_weight.shape[0]
    small_len = sum(item.shape[0] for item in small)
    spare_rows = -(-small_len // (8 * 3 * PAIR)) * 8
    small_rows = jnp.pad(jnp.concatenate(small), (0, spare_rows * 3 * PAIR - small_len))
    small_rows = small_rows.reshape(spare_rows, 3 * PAIR)
    by_pair = qkv_weight.reshape(shard_rows, 3, PLANE, PAIR).transpose(2, 0, 1, 3)
    by_pair = by_pair.reshape(PLANE, shard_rows, 3 * PAIR)
    outgoing = jnp.concatenate(
        [by_pair, jnp.broadcast_to(small_rows[None], (PLANE,) + small_rows.shape)], axis=1
    )
    arrived = exchange(outgoing[jnp.bitwise_xor(mine, jnp.arange(PLANE))])

    token_orders = [[2, 4, 1] if m % 2 == 0 else [4, 2, 1] for m in range(micro_count)]
    gathered = [tokens[m][None] for m in range(micro_count)]
    current = arrived
    for k in range(3):
        if k == 1:
            gathered = [tie(item, arrived) for item in gathered]
        got = [swap(item, token_orders[m][k]) for m, item in enumerate(gathered)]
        if k == 1:
            for bit in depth_bits:
                current = jnp.concatenate([current, swap(current, bit)], axis=0)
            got[0] = tie(got[0], current)
        halves = list(zip(gathered, got))
        gathered = [jnp.concatenate(pair, axis=0) for pair in halves]

    step = out_weight.shape[0]
    wide_parts = fc1_weight.shape[1] // model_width
    up_shard = fc1_weight.reshape(step, n, wide_parts, step).transpose(2, 0, 1, 3)
    shards = [out_weight, up_shard.reshape(wide_parts * step, model_width), fc2_weight]
    packed = tie(jnp.concatenate(shards, axis=0), current, *[near for near, _ in halves])
    every = lax.all_gather(packed, "seq")

    def whole_part(k):
        return every[:, k * step : (k + 1) * step].reshape(model_width, model_width)

    out_full = whole_part(0)
    ups = [whole_part(1 + k) for k in range(wide_parts)]
    downs = [whole_part(1 + wide_parts + k) for k in range(wide_parts)]

    pair_blocks = turn_blocks(info, current)
    pair_weight = pair_blocks[:, :shard_rows].reshape(n * shard_rows, 3 * PAIR)
    small_all = pair_blocks[:, shard_rows:].reshape(n, -1).astype(f32)
    small_full = []
    offset = 0
    for item in small:
        width = item.shape[0]
        small_full.append(small_all[:, offset : offset + width].reshape(n * width))
        offset += width
    gain_one, shift_one, q_shift, v_shift, out_shift, gain_two, shift_two, down_shift, up_shift = small_full

    plane_stream = jnp.stack([plane_tokens(near, far, order) for (near, far), order in zip(halves, token_orders)])
    plane_flat = plane_stream.reshape(micro_count * plane_rows, model_width)
    normed, _, _ = layer_norm_parts(plane_flat.astype(f32), gain_one, shift_one)
    normed_low = normed.astype(bf16)
    pair_shift = jnp.concatenate(
        [
            lax.dynamic_slice_in_dim(q_shift, mine * PAIR, PAIR),
            jnp.zeros((PAIR,), f32),
            lax.dynamic_slice_in_dim(v_shift, mine * PAIR, PAIR),
        ]
    )
    qkv = (product(normed_low, pair_weight) + pair_shift).astype(bf16)
    qkv = qkv.reshape(micro_count, PLANE, tok_dev, 3 * PAIR)

    edge_blocks = -(-HALO // tok_dev)

    def plane_block(index):
        return lax.dynamic_index_in_dim(qkv, jnp.bitwise_xor(mine, index), 1, keepdims=False)[:, :, PAIR:]

    last_rows = jnp.concatenate([plane_block(PLANE - edge_blocks + k) for k in range(edge_blocks)], axis=1)
    first_rows = jnp.concatenate([plane_block(k) for k in range(edge_blocks)], axis=1)
    before = shift_plane(last_rows[:, edge_blocks * tok_dev - HALO :], 1)
    after = shift_plane(first_rows[:, :HALO], -1)
    mixed_pair, stats = attend(info, bounds, qkv, before, after)

    def column(r):
        return jnp.bitwise_xor(mine, r) * PAIR

    mixed_low = jnp.zeros((own_tokens, model_width), bf16)
    for r in range(PLANE):
        part = mixed_pair[r] if r == 0 else swap(mixed_pair[r], r)
        mixed_low = lax.dynamic_update_slice(mixed_low, part.reshape(own_tokens, PAIR), (0, column(r)))

    stream = tokens.reshape(own_tokens, model_width).astype(f32)
    cotangent_low = cotangent.reshape(own_tokens, model_width)
    middle = stream + product(mixed_low, out_full) + out_shift
    normed_two, normal_two, inverse_two = layer_norm_parts(middle, gain_two, shift_two)
    normed_two_low = normed_two.astype(bf16)
    up_shifts = up_shift.reshape(n, wide_parts, step).transpose(1, 0, 2).reshape(wide_parts, model_width)
    actives, grad_hiddens = [], []
    for k in range(wide_parts):
        hidden = product(normed_two_low, ups[k]) + up_shifts[k]
        gate = jax.nn.sigmoid(1.702 * hidden)
        actives.append((hidden * gate).astype(bf16))
        grad_active = product_nt(cotangent_low, downs[k])
        grad_hiddens.append((grad_active * (gate + 1.702 * hidden * gate * (1.0 - gate))).astype(bf16))

    def by_device(partial):
        return partial.astype(bf16).reshape(n, -1, model_width)

    order_a = [1, 2, 4] + depth_bits[::-1]
    order_b = [1, 4, 2] + depth_bits[::-1]
    grad_downs = [by_device(product_tn(active, cotangent_low)) for active in actives]
    mid = wide_parts // 2
    down = [Scatter(me, grad_downs[:mid], order_a), Scatter(me, grad_downs[mid:], order_b)]
    for part in down:
        part.swap()
    grad_hiddens[0] = tie(grad_hiddens[0], *[part.send for part in down])

    grad_normed_two = product_nt(grad_hiddens[0], ups[0])
    for k in range(1, wide_parts):
        grad_normed_two = grad_normed_two + product_nt(grad_hiddens[k], ups[k])
    for part in down:
        part.advance(grad_normed_two)
    grad_normed_two = tie(grad_normed_two, *[part.send for part in down])
    grad_middle = cotangent_low.astype(f32) + layer_norm_back(
        grad_normed_two, normal_two, inverse_two, gain_two
    )
    grad_branch_low = grad_middle.astype(bf16)
    grad_mixed_low = product_nt(grad_branch_low, out_full).astype(bf16)
    grad_parts = []
    for r in range(PLANE):
        part = lax.dynamic_slice(grad_mixed_low, (0, column(r)), (own_tokens, PAIR))
        part = part.reshape(micro_count, tok_dev, PAIR)
        grad_parts.append(part if r == 0 else swap(part, r))

    later = tie(normed_two_low, grad_mixed_low)
    grad_ups = [by_device(product_tn(later, grad_hidden)) for grad_hidden in grad_hiddens]
    grad_out_weight = by_device(product_tn(mixed_low, grad_branch_low))
    up = [
        Scatter(me, grad_ups[:mid] + [grad_out_weight[:, : step // 2]], order_a),
        Scatter(me, grad_ups[mid:] + [grad_out_weight[:, step // 2 :]], order_b),
    ]
    for part in up:
        part.swap()
    result = middle + down_shift
    after_up = tie(actives[0], *[part.send for part in up])
    for k in range(wide_parts):
        result = result + product(after_up if k == 0 else actives[k], downs[k])
    result_low = result.astype(bf16)
    for part in up:
        part.advance(result_low, *grad_parts)

    grad_flat = []
    before_back = [part.send for part in up]
    joined_parts = []
    for m in range(micro_count):
        own_grad = tie(grad_parts[0], *before_back)
        grad_query, grad_pairs, grad_before, grad_after = attend_back(
            m, info, bounds, qkv, before, after, mixed_pair, [own_grad] + grad_parts[1:], stats
        )
        from_next = shift_plane(grad_before, -1)
        from_last = shift_plane(grad_after, 1)
        moving = down if m % 2 == 0 else up
        for part in moving:
            part.advance(grad_before)
        before_back = [part.send for part in moving]
        joined_parts.append((grad_query, grad_pairs, from_last, from_next))
    grad_planes = []
    for m in range(micro_count):
        grad_query, grad_pairs, from_last, from_next = joined_parts[m]
        grad_query = tie(grad_query, *before_back)
        joined = join_grads(info, grad_query, grad_pairs, from_last, from_next, tok_dev)
        grad_flat.append(joined.reshape(plane_rows, 3 * PAIR))
        grad_plane = product_nt(grad_flat[m], pair_weight).reshape(PLANE, tok_dev, model_width)
        order = [1, 2, 4] if m % 2 == 0 else [1, 4, 2]
        grad_planes.append(PlaneScatter(grad_plane, order))
        grad_planes[m].start()
        moving = down if m % 2 == 0 else up
        for part in moving:
            part.advance(joined)
        before_back = [part.send for part in moving]
    for plane in grad_planes:
        plane.finish()
        plane.start(*before_back)
    plane_sends = [plane.send for plane in grad_planes]
    grad_flat = tie(jnp.concatenate(grad_flat, axis=0), *plane_sends)

    grad_pair_weight = product_tn(normed_low, grad_flat)
    column_sum = jnp.sum(grad_flat.astype(f32), axis=0)
    wide = pair_weight.astype(f32)
    grad_shift_one = jnp.sum(wide * column_sum, axis=1)
    grad_gain_one = jnp.sum(wide * grad_pair_weight, axis=1)
    grad_gain_one = (grad_gain_one - shift_one * grad_shift_one) / gain_one

    def at_columns(part):
        return lax.dynamic_update_slice(jnp.zeros((model_width,), f32), part, (mine * PAIR,))

    small_grads = [
        grad_gain_one,
        grad_shift_one,
        at_columns(column_sum[:PAIR]),
        at_columns(column_sum[2 * PAIR :]),
        jnp.sum(grad_branch_low.astype(f32), axis=0),
        jnp.sum(grad_normed_two * normal_two, axis=0),
        jnp.sum(grad_normed_two, axis=0),
        jnp.sum(cotangent_low.astype(f32), axis=0),
        jnp.stack([jnp.sum(item.astype(f32), axis=0).reshape(n, step) for item in grad_hiddens], axis=1),
    ]
    small_out = jnp.concatenate([item.reshape(n, -1) for item in small_grads], axis=1).astype(bf16)
    small_out = jnp.pad(small_out, ((0, 0), (0, spare_rows * 3 * PAIR - small_len)))
    small_out = small_out.reshape(n, spare_rows, 3 * PAIR)
    leaving = jnp.concatenate(
        [grad_pair_weight.astype(bf16).reshape(n, shard_rows, 3 * PAIR), small_out], axis=1
    )
    turned = turn_blocks(info, leaving)

    for part in down:
        part.advance(turned)
    size = n
    for index, bit in enumerate(depth_bits[::-1]):
        size //= 2
        got = swap(turned[size:], bit)
        if index == 0:
            for plane in grad_planes:
                plane.got = tie(plane.got, turned)
                plane.finish()
                plane.start()
            got = tie(got, *[plane.send for plane in grad_planes])
        turned = (turned[:size].astype(f32) + got.astype(f32)).astype(bf16)
    for part in up:
        part.advance(turned)
    for plane in grad_planes:
        plane.got = tie(plane.got, *[part.send for part in up])
        plane.finish()
    grad_normed = jnp.concatenate([plane.pieces[0] for plane in grad_planes], axis=0)
    _, normal_one, inverse_one = layer_norm_parts(stream, gain_one, shift_one)
    grad_stream = grad_middle + layer_norm_back(grad_normed, normal_one, inverse_one, gain_one)
    stream_low = grad_stream.astype(bf16)
    for part in up + down:
        while part.order:
            part.advance(stream_low)
    down_sum = jnp.concatenate([part.total() for part in down], axis=0)
    up_totals = [part.total() for part in up]
    out_sum = jnp.concatenate([total[mid * step :] for total in up_totals], axis=0)
    up_sum = jnp.concatenate([total[: mid * step] for total in up_totals], axis=0)
    up_sum = up_sum.reshape(wide_parts, step, n, step).transpose(1, 2, 0, 3).reshape(step, -1)
    back = exchange(turned).astype(f32)
    qkv_sum = jnp.zeros((shard_rows, 3, model_width), f32)
    for r in range(PLANE):
        columns = back[r, :shard_rows].reshape(shard_rows, 3, PAIR)
        qkv_sum = lax.dynamic_update_slice(qkv_sum, columns, (0, 0, column(r)))
    small_sum = jnp.sum(back[:, shard_rows:], axis=0)
    qkv_sum = qkv_sum.reshape(shard_rows, 3 * model_width)
    small_sum = small_sum.reshape(-1)
    sums = []
    offset = 0
    for item in small:
        sums.append(small_sum[offset : offset + item.shape[0]])
        offset += item.shape[0]

    return (
        result_low.reshape(micro_count, tok_dev, model_width),
        stream_low.reshape(micro_count, tok_dev, model_width),
        sums[0],
        sums[1],
        qkv_sum,
        sums[2],
        sums[3],
        out_sum,
        sums[4],
        sums[5],
        sums[6],
        up_sum,
        sums[8],
        down_sum,
        sums[7],
    )


def solution(mesh):
    return jax.shard_map(
        body,
        mesh=mesh,
        in_specs=(
            P(None, "seq", None),
            P("seq"),
            P("seq"),
            P("seq", None),
            P("seq"),
            P("seq"),
            P("seq", None),
            P("seq"),
            P("seq"),
            P("seq"),
            P("seq", None),
            P("seq"),
            P("seq", None),
            P("seq"),
            P(None, "seq"),
            P(),
            P(None, "seq", None),
        ),
        out_specs=(
            P(None, "seq", None),
            P(None, "seq", None),
            P("seq"),
            P("seq"),
            P("seq", None),
            P("seq"),
            P("seq"),
            P("seq", None),
            P("seq"),
            P("seq"),
            P("seq"),
            P("seq", None),
            P("seq"),
            P("seq", None),
            P("seq"),
        ),
        check_vma=False,
    )
```

```python
import functools

import jax
import jax.numpy as jnp
from jax import lax
from jax.experimental import pallas as pl
from jax.experimental.pallas import tpu as pltpu
from jax.sharding import PartitionSpec as P

HEAD_DIM = 64
IMG_TOK = 577
PLANE = 8
PAIR = 2 * HEAD_DIM
HALO = IMG_TOK - 1
LEAD = 640
WINDOW = 640
TILE = 256

epsilon = 1e-05
negative_fill = -1e30
bf16 = jnp.bfloat16
f32 = jnp.float32


def product(left, right):
    return jnp.dot(left, right, preferred_element_type=f32)


def product_tn(left, right):
    return lax.dot_general(left, right, (((0,), (0,)), ((), ())), preferred_element_type=f32)


def product_nt(left, right):
    return lax.dot_general(left, right, (((1,), (1,)), ((), ())), preferred_element_type=f32)


def swap(block, bit):
    n = lax.axis_size("seq")
    return lax.ppermute(block, "seq", [(i, i ^ bit) for i in range(n)])


def shift_plane(block, planes):
    n = lax.axis_size("seq")
    step = planes * PLANE
    return lax.ppermute(block, "seq", [(i, i + step) for i in range(n) if 0 <= i + step < n])


def places(order):
    held = [0]
    for bit in order:
        held = held + [r ^ bit for r in held]
    return held


def gather_bits(block, order):
    current = block[None]
    for bit in order[:-1]:
        current = jnp.concatenate([current, swap(current, bit)], axis=0)
    return current, swap(current, order[-1])


def position(r, order):
    return sum(((r >> (bit.bit_length() - 1)) & 1) << k for k, bit in enumerate(order))


def tie(value, *earlier):
    return lax.optimization_barrier((value,) + earlier)[0]


def own_bit(me, bit):
    return jnp.where(jnp.bitwise_and(me, bit) != 0, 1, 0)


def pick(block, axis, index):
    return lax.dynamic_index_in_dim(block, index, axis, keepdims=False)


def exchange(blocks):
    bits = PLANE.bit_length() - 1
    cube = blocks.reshape((2,) * bits + blocks.shape[1:])
    for axis in reversed(range(bits)):
        got = swap(lax.index_in_dim(cube, 1, axis, keepdims=False), 1 << (bits - 1 - axis))
        cube = jnp.stack([lax.index_in_dim(cube, 0, axis, keepdims=False), got], axis=axis)
    return cube.reshape(blocks.shape)


class Scatter:
    def __init__(self, me, partials, order):
        self.me = me
        self.partials = partials
        depth = sum(item.shape[0] for item in partials[0]).bit_length() - 1
        self.bits = [1 << (depth - 1 - axis) for axis in range(depth)]
        self.order = list(order)
        self.split()

    def half(self, axis, index):
        if self.partials is None:
            kept = pick(self.block, axis, index).astype(f32)
            return (kept + pick(self.got, axis, index).astype(f32)).astype(bf16)
        joined = []
        for items in self.partials:
            picked = [pick(item.reshape((-1, 2) + item.shape[1:]), 1, index) for item in items]
            joined.append(picked[0] if len(picked) == 1 else jnp.concatenate(picked, axis=0))
        joined = joined[0] if len(joined) == 1 else jnp.concatenate(joined, axis=1)
        return joined.reshape((2,) * len(self.bits) + joined.shape[1:])

    def split(self):
        self.bit = self.order.pop(0)
        axis = self.bits.index(self.bit)
        self.bits.pop(axis)
        mine = own_bit(self.me, self.bit)
        self.send, keep = self.half(axis, 1 - mine), self.half(axis, mine)
        self.block, self.got, self.partials = keep, None, None

    def swap(self):
        self.got = swap(self.send, self.bit)

    def advance(self, *earlier):
        if earlier:
            self.got = tie(self.got, *earlier)
        self.split()
        self.swap()

    def total(self):
        return self.block.astype(f32) + self.got.astype(f32)


def turn_kernel(info, blocks, turned):
    for r in range(blocks.shape[0]):
        turned[r] = blocks[jnp.bitwise_xor(info[0], r)]


def turn_blocks(info, blocks):
    return pl.pallas_call(
        turn_kernel,
        grid_spec=pltpu.PrefetchScalarGridSpec(
            num_scalar_prefetch=1,
            grid=(1,),
            in_specs=[pl.BlockSpec(blocks.shape, lambda g, i: (0, 0, 0))],
            out_specs=pl.BlockSpec(blocks.shape, lambda g, i: (0, 0, 0)),
        ),
        out_shape=jax.ShapeDtypeStruct(blocks.shape, blocks.dtype),
    )(info, blocks)


def load_rows(orders, micros, place_in_plane, qkv, before, after, queries, keys, values, sem):
    blocks, rows = qkv.shape[1], qkv.shape[2]
    own = blocks * rows
    for buffer in (keys, values):
        for slot in range(len(micros)):
            buffer[slot, 0 : LEAD - HALO, :] = jnp.zeros((LEAD - HALO, PAIR), bf16)
            tail = buffer.shape[1] - (LEAD + own + HALO)
            buffer[slot, LEAD + own + HALO :, :] = jnp.zeros((tail, PAIR), bf16)
    started = []
    for slot, m in enumerate(micros):
        for p, r in enumerate(places(orders[m])):
            spot = pl.multiple_of(jnp.bitwise_xor(place_in_plane, r) * rows, rows)
            started += [
                pltpu.make_async_copy(
                    qkv.at[m, p, :, pl.ds(0, PAIR)], queries.at[slot, pl.ds(spot, rows)], sem
                ),
                pltpu.make_async_copy(
                    qkv.at[m, p, :, pl.ds(PAIR, PAIR)], keys.at[slot, pl.ds(LEAD + spot, rows)], sem
                ),
                pltpu.make_async_copy(
                    qkv.at[m, p, :, pl.ds(2 * PAIR, PAIR)], values.at[slot, pl.ds(LEAD + spot, rows)], sem
                ),
            ]
        for which, buffer in enumerate((keys, values)):
            columns = pl.ds(which * PAIR, PAIR)
            started += [
                pltpu.make_async_copy(
                    before.at[m, :, columns], buffer.at[slot, pl.ds(LEAD - HALO, HALO)], sem
                ),
                pltpu.make_async_copy(
                    after.at[m, :, columns], buffer.at[slot, pl.ds(LEAD + own, HALO)], sem
                ),
            ]
    return started


def image_span(bounds, m, image, base):
    begin = bounds[m, image] - base + LEAD
    finish = bounds[m, image + 1] - base + LEAD
    return begin, finish


def key_block(keys, m, begin, finish, key_start, key_aug):
    key_aug[:, :PAIR] = keys[m, pl.ds(key_start, WINDOW), :]
    rows = key_start + lax.broadcasted_iota(jnp.int32, (WINDOW, PAIR), 0)
    inside = (rows >= begin) & (rows < finish)
    key_aug[:, PAIR:] = jnp.where(inside, 0.0, negative_fill).astype(bf16)


def split_heads(rows_f32, lanes):
    first = jnp.where(lanes < HEAD_DIM, rows_f32, 0.0).astype(bf16)
    second = jnp.where(lanes >= HEAD_DIM, rows_f32, 0.0).astype(bf16)
    return first, second


def attend_kernel(
    orders, info, bounds, qkv, before, after, mixed, stats, queries, keys, values, result, result_low, key_aug, value_t, sem
):
    micro_count, blocks, rows, _ = qkv.shape
    own = blocks * rows
    place_in_plane, base = info[1], info[2]
    image_count = bounds.shape[1] - 1
    started = load_rows(orders, range(micro_count), place_in_plane, qkv, before, after, queries, keys, values, sem)
    for copy in started:
        copy.start()
    value_t[:, HEAD_DIM:, :] = jnp.ones((2, 16, WINDOW), bf16)
    lanes = lax.broadcasted_iota(jnp.int32, (TILE, PAIR), 1)
    rows_iota = lax.broadcasted_iota(jnp.int32, (TILE, PAIR), 0)
    lane_row = lax.broadcasted_iota(jnp.int32, (1, TILE), 1)
    query_mark = jnp.where(lanes == 0, 1.0, 0.0).astype(bf16)
    for copy in started:
        copy.wait()

    for m in range(micro_count):

        def one_image(image, carry):
            begin, finish = image_span(bounds, m, image, base)

            @pl.when((finish > LEAD) & (begin < LEAD + own))
            def _():
                key_start = pl.multiple_of((begin >> 4) << 4, 16)
                key_block(keys, m, begin, finish, key_start, key_aug)
                turned = values[m, pl.ds(key_start, WINDOW), :].astype(f32).T
                value_t[0, :HEAD_DIM, :] = turned[:HEAD_DIM].astype(bf16)
                value_t[1, :HEAD_DIM, :] = turned[HEAD_DIM:].astype(bf16)
                first_tile = jnp.maximum(begin - LEAD, 0) >> 8
                last_tile = (jnp.minimum(finish - LEAD, own) + TILE - 1) >> 8

                def one_tile(tile, carry):
                    spot = pl.multiple_of(tile * TILE, TILE)
                    scaled = queries[m, pl.ds(spot, TILE), :].astype(f32) * (HEAD_DIM**-0.5)
                    pieces = []
                    inside_lane = (lane_row + (spot + LEAD) >= begin) & (lane_row + (spot + LEAD) < finish)
                    for h, query in enumerate(split_heads(scaled, lanes)):
                        aug = jnp.concatenate([query, query_mark], axis=1)
                        scores = product_nt(key_aug[...], aug)
                        peak = jnp.max(scores, axis=0, keepdims=True)
                        weights = jnp.exp(scores - peak).astype(bf16)
                        out = product(value_t[h], weights)
                        total = out[HEAD_DIM : HEAD_DIM + 1]
                        pieces.append(out[:HEAD_DIM] / total)
                        row = (m * 2 + h) * blocks + tile
                        stats[pl.ds(row, 1), :] = jnp.where(
                            inside_lane, peak + jnp.log(total), stats[pl.ds(row, 1), :]
                        )
                    value = jnp.concatenate(pieces, axis=0).T
                    place_row = rows_iota + (spot + LEAD)
                    inside = (place_row >= begin) & (place_row < finish)
                    result[m, pl.ds(spot, TILE), :] = jnp.where(
                        inside, value, result[m, pl.ds(spot, TILE), :]
                    )
                    return carry

                lax.fori_loop(first_tile, last_tile, one_tile, 0)

            return carry

        lax.fori_loop(0, image_count, one_image, 0)

    result_low[...] = result[...].astype(bf16)
    started = []
    for m in range(micro_count):
        for r in range(blocks):
            spot = pl.multiple_of(jnp.bitwise_xor(place_in_plane, r) * rows, rows)
            started.append(pltpu.make_async_copy(result_low.at[m, pl.ds(spot, rows)], mixed.at[r, m], sem))
    for copy in started:
        copy.start()
    for copy in started:
        copy.wait()


def attend_back_kernel(m, orders, info, bounds, qkv, before, after, mixed, *refs):
    blocks, rows = qkv.shape[1], qkv.shape[2]
    own = blocks * rows
    grad_mixed, refs = refs[:blocks], refs[blocks:]
    stats, grad_query, grad_pairs, grad_before, grad_after, refs = *refs[:5], refs[5:]
    queries, keys, values, result, grads, key_aug, key_t, acc_query, acc_key, acc_value, edge, sem = refs
    place_in_plane, base = info[1], info[2]
    image_count = bounds.shape[1] - 1
    started = load_rows(orders, [m], place_in_plane, qkv, before, after, queries, keys, values, sem)
    for r in range(blocks):
        spot = pl.multiple_of(jnp.bitwise_xor(place_in_plane, r) * rows, rows)
        started += [
            pltpu.make_async_copy(mixed.at[r, m], result.at[pl.ds(spot, rows)], sem),
            pltpu.make_async_copy(grad_mixed[r].at[m], grads.at[pl.ds(spot, rows)], sem),
        ]
    for copy in started:
        copy.start()
    acc_query[...] = jnp.zeros_like(acc_query)
    acc_key[...] = jnp.zeros_like(acc_key)
    acc_value[...] = jnp.zeros_like(acc_value)
    lanes = lax.broadcasted_iota(jnp.int32, (TILE, PAIR), 1)
    lane_row = lax.broadcasted_iota(jnp.int32, (1, TILE), 1)
    query_mark = jnp.where(lanes == 0, 1.0, 0.0).astype(bf16)
    for copy in started:
        copy.wait()


    def one_image(image, carry):
        begin, finish = image_span(bounds, m, image, base)

        @pl.when((finish > LEAD) & (begin < LEAD + own))
        def _():
            key_start = pl.multiple_of((begin >> 4) << 4, 16)
            key_rows = pl.ds(key_start, WINDOW)
            key_block(keys, 0, begin, finish, key_start, key_aug)
            turned = keys[0, key_rows, :].astype(f32).T
            key_t[0] = turned[:HEAD_DIM].astype(bf16)
            key_t[1] = turned[HEAD_DIM:].astype(bf16)
            first_tile = jnp.maximum(begin - LEAD, 0) >> 8
            last_tile = (jnp.minimum(finish - LEAD, own) + TILE - 1) >> 8

            def one_tile(tile, carry):
                spot = pl.multiple_of(tile * TILE, TILE)
                here = pl.ds(spot, TILE)
                scaled = queries[0, here, :].astype(f32) * (HEAD_DIM**-0.5)
                grad = grads[ here, :].astype(f32)
                dots = (grad * result[ here, :].astype(f32)).T
                inside_lane = (lane_row + (spot + LEAD) >= begin) & (lane_row + (spot + LEAD) < finish)
                both = zip(split_heads(scaled, lanes), split_heads(grad, lanes))
                pieces = []
                add_key, add_value = None, None
                for h, (query, grad_h) in enumerate(both):
                    row = (m * 2 + h) * blocks + tile
                    level = jnp.where(inside_lane, stats[pl.ds(row, 1), :], -negative_fill)
                    row_dot = jnp.sum(
                        dots[h * HEAD_DIM : (h + 1) * HEAD_DIM], axis=0, keepdims=True
                    )
                    aug = jnp.concatenate([query, query_mark], axis=1)
                    shares = jnp.exp(product_nt(key_aug[...], aug) - level)
                    grad_share = product_nt(values[0, key_rows, :], grad_h)
                    grad_scores = (shares * (grad_share - row_dot)).astype(bf16)
                    value_part = product(shares.astype(bf16), grad_h)
                    key_part = product(grad_scores, query)
                    add_value = value_part if h == 0 else add_value + value_part
                    add_key = key_part if h == 0 else add_key + key_part
                    pieces.append(product(key_t[h], grad_scores))
                acc_value[ key_rows, :] += add_value
                acc_key[ key_rows, :] += add_key
                acc_query[ here, :] += jnp.concatenate(pieces, axis=0).T * (HEAD_DIM**-0.5)
                return carry

            lax.fori_loop(first_tile, last_tile, one_tile, 0)

        return carry

    lax.fori_loop(0, image_count, one_image, 0)

    edge_rows = grad_before.shape[0]
    edge[0, : edge_rows - HALO, :] = jnp.zeros((edge_rows - HALO, 2 * PAIR), bf16)
    edge[1, HALO:, :] = jnp.zeros((edge_rows - HALO, 2 * PAIR), bf16)
    started = [pltpu.make_async_copy(acc_query, grad_query, sem)]
    for which, acc in enumerate((acc_key, acc_value)):
        columns = pl.ds(which * PAIR, PAIR)
        edge[0, edge_rows - HALO :, which * PAIR : (which + 1) * PAIR] = acc[LEAD - HALO : LEAD, :].astype(bf16)
        edge[1, :HALO, which * PAIR : (which + 1) * PAIR] = acc[LEAD + own : LEAD + own + HALO, :].astype(bf16)
        started.append(pltpu.make_async_copy(acc.at[pl.ds(LEAD, own)], grad_pairs.at[:, columns], sem))
    started.append(pltpu.make_async_copy(edge.at[0], grad_before, sem))
    started.append(pltpu.make_async_copy(edge.at[1], grad_after, sem))
    for copy in started:
        copy.start()
    for copy in started:
        copy.wait()


def cover(rows, passes):
    scores = 2 * rows * WINDOW
    return pl.CostEstimate(
        flops=4 * scores * PAIR, transcendentals=scores, bytes_accessed=passes * scores
    )


def any_specs(count):
    return [pl.BlockSpec(memory_space=pl.ANY)] * count


def attend(orders, info, bounds, qkv, before, after):
    micro_count, blocks, rows, _ = qkv.shape
    own = blocks * rows
    span = LEAD + own + LEAD
    stat_rows = micro_count * 2 * blocks
    return pl.pallas_call(
        functools.partial(attend_kernel, orders),
        grid_spec=pltpu.PrefetchScalarGridSpec(
            num_scalar_prefetch=2,
            grid=(1,),
            in_specs=any_specs(3),
            out_specs=any_specs(1) + [pl.BlockSpec((stat_rows, TILE), lambda g, a, b: (0, 0))],
            scratch_shapes=[
                pltpu.VMEM((micro_count, own, PAIR), bf16),
                pltpu.VMEM((micro_count, span, PAIR), bf16),
                pltpu.VMEM((micro_count, span, PAIR), bf16),
                pltpu.VMEM((micro_count, own, PAIR), f32),
                pltpu.VMEM((micro_count, own, PAIR), bf16),
                pltpu.VMEM((WINDOW, 2 * PAIR), bf16),
                pltpu.VMEM((2, HEAD_DIM + 16, WINDOW), bf16),
                pltpu.SemaphoreType.DMA,
            ],
        ),
        out_shape=[
            jax.ShapeDtypeStruct((blocks, micro_count, rows, PAIR), bf16),
            jax.ShapeDtypeStruct((stat_rows, TILE), f32),
        ],
        cost_estimate=cover(micro_count * own, 30),
    )(info, bounds, qkv, before, after)


def attend_back(m, orders, info, bounds, qkv, before, after, mixed, grad_mixed, stats):
    _, blocks, rows, _ = qkv.shape
    own = blocks * rows
    span = LEAD + own + LEAD
    edge_rows = -(-HALO // rows) * rows
    return pl.pallas_call(
        functools.partial(attend_back_kernel, m, orders),
        grid_spec=pltpu.PrefetchScalarGridSpec(
            num_scalar_prefetch=2,
            grid=(1,),
            in_specs=any_specs(4 + blocks) + [pl.BlockSpec(stats.shape, lambda g, a, b: (0, 0))],
            out_specs=any_specs(4),
            scratch_shapes=[
                pltpu.VMEM((1, own, PAIR), bf16),
                pltpu.VMEM((1, span, PAIR), bf16),
                pltpu.VMEM((1, span, PAIR), bf16),
                pltpu.VMEM((own, PAIR), bf16),
                pltpu.VMEM((own, PAIR), bf16),
                pltpu.VMEM((WINDOW, 2 * PAIR), bf16),
                pltpu.VMEM((2, HEAD_DIM, WINDOW), bf16),
                pltpu.VMEM((own, PAIR), f32),
                pltpu.VMEM((span, PAIR), f32),
                pltpu.VMEM((span, PAIR), f32),
                pltpu.VMEM((2, edge_rows, 2 * PAIR), bf16),
                pltpu.SemaphoreType.DMA,
            ],
        ),
        out_shape=[
            jax.ShapeDtypeStruct((own, PAIR), f32),
            jax.ShapeDtypeStruct((own, 2 * PAIR), f32),
            jax.ShapeDtypeStruct((edge_rows, 2 * PAIR), bf16),
            jax.ShapeDtypeStruct((edge_rows, 2 * PAIR), bf16),
        ],
        cost_estimate=cover(own, 35),
    )(info, bounds, qkv, before, after, mixed, *grad_mixed, stats)


def join_kernel(order, info, query, pairs, head, tail, joined):
    blocks, rows, _ = joined.shape
    edge_blocks = head.shape[0] // rows
    for tile in range(blocks):
        here = pl.ds(tile * rows, rows)
        total = pairs[here, :]
        if tile < edge_blocks:
            total = total + head[here, :].astype(f32)
        if tile >= blocks - edge_blocks:
            total = total + tail[pl.ds((tile - (blocks - edge_blocks)) * rows, rows), :].astype(f32)
        target = position(jnp.bitwise_xor(info[1], tile), order)
        joined[target, :, :PAIR] = query[here, :].astype(bf16)
        joined[target, :, PAIR:] = total.astype(bf16)


def join_grads(order, info, grad_query, grad_pairs, head, tail, rows):
    own = grad_query.shape[0]
    blocks = own // rows
    ins = (grad_query, grad_pairs, head, tail)
    return pl.pallas_call(
        functools.partial(join_kernel, order),
        grid_spec=pltpu.PrefetchScalarGridSpec(
            num_scalar_prefetch=1,
            grid=(1,),
            in_specs=[pl.BlockSpec(item.shape, lambda g, i: (0, 0)) for item in ins],
            out_specs=pl.BlockSpec((blocks, rows, 3 * PAIR), lambda g, i: (0, 0, 0)),
        ),
        out_shape=jax.ShapeDtypeStruct((blocks, rows, 3 * PAIR), bf16),
    )(info, *ins)


def layer_norm_parts(values, gain, shift):
    center = values - jnp.mean(values, axis=-1, keepdims=True)
    inverse = lax.rsqrt(jnp.mean(center * center, axis=-1, keepdims=True) + epsilon)
    normal = center * inverse
    return (normal * gain + shift, normal, inverse)


def layer_norm_back(grad_normed, normal, inverse, gain):
    scaled = grad_normed * gain
    centered = scaled - jnp.mean(scaled, axis=-1, keepdims=True)
    return inverse * (centered - normal * jnp.mean(scaled * normal, axis=-1, keepdims=True))


class PlaneScatter:
    def __init__(self, partial, held, order):
        self.pieces = [partial[position(r, held)].astype(bf16) for r in range(PLANE)]
        self.left = list(range(PLANE))
        self.order = list(order)

    def start(self, *earlier):
        self.bit = self.order.pop(0)
        self.keep = [r for r in self.left if not r & self.bit]
        self.send = jnp.stack([self.pieces[r | self.bit] for r in self.keep])
        if earlier:
            self.send = tie(self.send, *earlier)
        self.got = swap(self.send, self.bit)

    def finish(self):
        for position, r in enumerate(self.keep):
            added = self.pieces[r].astype(f32) + self.got[position].astype(f32)
            self.pieces[r] = added.astype(bf16) if self.order else added
        self.left = self.keep


def body(
    tokens,
    ln1_gain,
    ln1_bias,
    qkv_weight,
    q_bias,
    v_bias,
    out_weight,
    out_bias,
    ln2_gain,
    ln2_bias,
    fc1_weight,
    fc1_bias,
    fc2_weight,
    fc2_bias,
    image_ids,
    image_starts,
    cotangent,
):
    micro_count, tok_dev, model_width = tokens.shape
    n = lax.axis_size("seq")
    own_tokens = micro_count * tok_dev
    plane_rows = PLANE * tok_dev
    stream_len = tok_dev * n
    me = lax.axis_index("seq")
    mine = jnp.bitwise_and(me, PLANE - 1)
    base = (me - mine) * tok_dev
    info = jnp.stack([me, mine, base]).astype(jnp.int32)
    bounds = jnp.concatenate(
        [image_starts, jnp.full((micro_count, 1), stream_len, jnp.int32)], axis=1
    )
    plane_bits = [1, 2, 4]
    depth_bits = []
    bit = PLANE
    while bit < n:
        depth_bits.append(bit)
        bit *= 2

    small = [ln1_gain, ln1_bias, q_bias, v_bias, out_bias, ln2_gain, ln2_bias, fc2_bias, fc1_bias]
    shard_rows = qkv_weight.shape[0]
    small_len = sum(item.shape[0] for item in small)
    spare_rows = -(-small_len // (8 * 3 * PAIR)) * 8
    narrow = small[0].shape[0]
    small_rows = jnp.concatenate([item.reshape(-1, narrow) for item in small], axis=0)
    used = small_rows.shape[0]
    small_rows = jnp.pad(small_rows, ((0, -used % 16), (0, 3 * PAIR - narrow)))
    by_pair = qkv_weight.reshape(shard_rows, 3, PLANE, PAIR).transpose(2, 0, 1, 3)
    by_pair = by_pair.reshape(PLANE, shard_rows, 3 * PAIR)
    outgoing = jnp.concatenate(
        [by_pair, jnp.broadcast_to(small_rows[None], (PLANE,) + small_rows.shape)], axis=1
    )
    arrived = exchange(outgoing[jnp.bitwise_xor(mine, jnp.arange(PLANE))])

    token_orders = [[2, 4, 1] if m % 2 == 0 else [4, 2, 1] for m in range(micro_count)]
    gathered = [tokens[m][None] for m in range(micro_count)]
    current = arrived
    for k in range(3):
        got = [swap(item, token_orders[m][k]) for m, item in enumerate(gathered)]
        if k == 1:
            for bit in depth_bits:
                current = jnp.concatenate([current, swap(current, bit)], axis=0)
            early = got + [current]
            got[0] = tie(got[0], current)
        gathered = [jnp.concatenate(pair, axis=0) for pair in zip(gathered, got)]

    step = out_weight.shape[0]
    wide_parts = fc1_weight.shape[1] // model_width
    shards = [out_weight]
    shards += [fc1_weight[:, k * model_width : (k + 1) * model_width] for k in range(wide_parts)]
    packed = tie(jnp.concatenate(shards + [fc2_weight], axis=0), *early)
    every = lax.all_gather(packed, "seq")
    out_full = every[:, :step].reshape(model_width, model_width)
    ups = [every[:, (1 + k) * step : (2 + k) * step].reshape(model_width, -1) for k in range(wide_parts)]
    share = n // wide_parts
    downs = [
        every[k * share : (k + 1) * share, (1 + wide_parts) * step :].reshape(-1, model_width)
        for k in range(wide_parts)
    ]

    pair_blocks = turn_blocks(info, current)
    pair_weight = pair_blocks[:, :shard_rows].reshape(n * shard_rows, 3 * PAIR)
    small_all = pair_blocks[:, shard_rows : shard_rows + used, :narrow].astype(f32)
    small_full = [small_all[:, k].reshape(-1) for k in range(len(small) - 1)]
    small_full.append(small_all[:, len(small) - 1 :].reshape(-1))
    gain_one, shift_one, q_shift, v_shift, out_shift, gain_two, shift_two, down_shift, up_shift = small_full

    plane_stream = jnp.stack(gathered)
    plane_flat = plane_stream.reshape(micro_count * plane_rows, model_width)
    normed, _, _ = layer_norm_parts(plane_flat.astype(f32), gain_one, shift_one)
    normed_low = normed.astype(bf16)
    pair_shift = jnp.concatenate(
        [
            lax.dynamic_slice_in_dim(q_shift, mine * PAIR, PAIR),
            jnp.zeros((PAIR,), f32),
            lax.dynamic_slice_in_dim(v_shift, mine * PAIR, PAIR),
        ]
    )
    qkv = (product(normed_low, pair_weight) + pair_shift).astype(bf16)
    qkv = qkv.reshape(micro_count, PLANE, tok_dev, 3 * PAIR)

    edge_blocks = -(-HALO // tok_dev)

    def plane_block(index):
        offset = jnp.bitwise_xor(mine, index)
        blocks = [pick(qkv[m], 0, position(offset, order)) for m, order in enumerate(token_orders)]
        return jnp.stack(blocks)[:, :, PAIR:]

    last_rows = jnp.concatenate([plane_block(PLANE - edge_blocks + k) for k in range(edge_blocks)], axis=1)
    first_rows = jnp.concatenate([plane_block(k) for k in range(edge_blocks)], axis=1)
    before = shift_plane(last_rows[:, edge_blocks * tok_dev - HALO :], 1)
    after = shift_plane(first_rows[:, :HALO], -1)
    mixed_pair, stats = attend(token_orders, info, bounds, qkv, before, after)

    def column(r):
        return jnp.bitwise_xor(mine, r) * PAIR

    mixed_low = jnp.zeros((own_tokens, model_width), bf16)
    for r in range(PLANE):
        part = mixed_pair[r] if r == 0 else swap(mixed_pair[r], r)
        mixed_low = lax.dynamic_update_slice(mixed_low, part.reshape(own_tokens, PAIR), (0, column(r)))

    stream = tokens.reshape(own_tokens, model_width).astype(f32)
    cotangent_low = cotangent.reshape(own_tokens, model_width)
    middle = stream + product(mixed_low, out_full) + out_shift
    normed_two, normal_two, inverse_two = layer_norm_parts(middle, gain_two, shift_two)
    normed_two_low = normed_two.astype(bf16)
    up_shifts = up_shift.reshape(wide_parts, model_width)
    actives, grad_hiddens = [], []
    for k in range(wide_parts):
        hidden = product(normed_two_low, ups[k]) + up_shifts[k]
        gate = jax.nn.sigmoid(1.702 * hidden)
        actives.append((hidden * gate).astype(bf16))
        grad_active = product_nt(cotangent_low, downs[k])
        grad_hiddens.append((grad_active * (gate + 1.702 * hidden * gate * (1.0 - gate))).astype(bf16))

    def by_device(partial, devices=n):
        return partial.astype(bf16).reshape(devices, -1, model_width)

    order_a = [1, 2, 4] + depth_bits[::-1]
    order_b = [1, 4, 2] + depth_bits[::-1]
    grad_downs = [by_device(product_tn(active, cotangent_low), share) for active in actives]
    half = grad_downs[0].shape[1] // 2
    down = [
        Scatter(me, [[item[:, :half] for item in grad_downs]], [1] + depth_bits + [2, 4]),
        Scatter(me, [[item[:, half:] for item in grad_downs]], [1] + depth_bits + [4, 2]),
    ]
    for part in down:
        part.swap()
    grad_hiddens[0] = tie(grad_hiddens[0], *[part.send for part in down])

    grad_normed_two = product_nt(grad_hiddens[0], ups[0])
    for k in range(1, wide_parts):
        grad_normed_two = grad_normed_two + product_nt(grad_hiddens[k], ups[k])
    for part in down:
        part.advance(grad_normed_two)
    grad_normed_two = tie(grad_normed_two, *[part.send for part in down])
    grad_middle = cotangent_low.astype(f32) + layer_norm_back(
        grad_normed_two, normal_two, inverse_two, gain_two
    )
    grad_branch_low = grad_middle.astype(bf16)
    grad_mixed_low = product_nt(grad_branch_low, out_full).astype(bf16)
    grad_parts = []
    for r in range(PLANE):
        part = lax.dynamic_slice(grad_mixed_low, (0, column(r)), (own_tokens, PAIR))
        part = part.reshape(micro_count, tok_dev, PAIR)
        grad_parts.append(part if r == 0 else swap(part, r))

    later = tie(normed_two_low, grad_mixed_low)
    grad_ups = [by_device(product_tn(later, grad_hidden)) for grad_hidden in grad_hiddens]
    grad_out_weight = by_device(product_tn(mixed_low, grad_branch_low))
    mid = wide_parts // 2
    up = [
        Scatter(me, [[item] for item in grad_ups[:mid] + [grad_out_weight[:, : step // 2]]], order_a),
        Scatter(me, [[item] for item in grad_ups[mid:] + [grad_out_weight[:, step // 2 :]]], order_b),
    ]
    for part in up:
        part.swap()
    result = middle + down_shift
    after_up = tie(actives[0], *[part.send for part in up])
    for k in range(wide_parts):
        result = result + product(after_up if k == 0 else actives[k], downs[k])
    result_low = result.astype(bf16)
    for part in up:
        part.advance(result_low, *grad_parts)

    grad_flat = []
    before_back = [part.send for part in up]
    joined_parts = []
    for m in range(micro_count):
        own_grad = tie(grad_parts[0], *before_back)
        grad_query, grad_pairs, grad_before, grad_after = attend_back(
            m, token_orders, info, bounds, qkv, before, after, mixed_pair, [own_grad] + grad_parts[1:], stats
        )
        from_next = shift_plane(grad_before, -1)
        from_last = shift_plane(grad_after, 1)
        moving = up + down if m % 2 == 0 else up
        for part in moving:
            part.advance(grad_before)
        before_back = [part.send for part in moving]
        joined_parts.append((grad_query, grad_pairs, from_last, from_next))
    grad_planes = []
    for m in range(micro_count):
        grad_query, grad_pairs, from_last, from_next = joined_parts[m]
        grad_query = tie(grad_query, *before_back)
        joined = join_grads(token_orders[m], info, grad_query, grad_pairs, from_last, from_next, tok_dev)
        grad_flat.append(joined.reshape(plane_rows, 3 * PAIR))
        grad_plane = product_nt(grad_flat[m], pair_weight).reshape(PLANE, tok_dev, model_width)
        order = [1, 2, 4] if m % 2 == 0 else [1, 4, 2]
        grad_planes.append(PlaneScatter(grad_plane, token_orders[m], order))
        grad_planes[m].start()
        if m == 0:
            for part in down:
                part.advance(joined)
            before_back = [part.send for part in down]
    for plane in grad_planes:
        plane.finish()
        plane.start()
    plane_sends = [plane.send for plane in grad_planes]
    grad_flat = tie(jnp.concatenate(grad_flat, axis=0), *plane_sends)

    grad_pair_weight = product_tn(normed_low, grad_flat)
    column_sum = jnp.sum(grad_flat.astype(f32), axis=0)
    wide = pair_weight.astype(f32)
    grad_shift_one = jnp.sum(wide * column_sum, axis=1)
    grad_gain_one = jnp.sum(wide * grad_pair_weight, axis=1)
    grad_gain_one = (grad_gain_one - shift_one * grad_shift_one) / gain_one

    def at_columns(part):
        return lax.dynamic_update_slice(jnp.zeros((model_width,), f32), part, (mine * PAIR,))

    small_grads = [
        grad_gain_one,
        grad_shift_one,
        at_columns(column_sum[:PAIR]),
        at_columns(column_sum[2 * PAIR :]),
        jnp.sum(grad_branch_low.astype(f32), axis=0),
        jnp.sum(grad_normed_two * normal_two, axis=0),
        jnp.sum(grad_normed_two, axis=0),
        jnp.sum(cotangent_low.astype(f32), axis=0),
        jnp.concatenate([jnp.sum(item.astype(f32), axis=0) for item in grad_hiddens]),
    ]
    small_out = jnp.concatenate([item.reshape(n, -1) for item in small_grads], axis=1).astype(bf16)
    small_out = jnp.pad(small_out, ((0, 0), (0, spare_rows * 3 * PAIR - small_len)))
    small_out = small_out.reshape(n, spare_rows, 3 * PAIR)
    leaving = jnp.concatenate(
        [grad_pair_weight.astype(bf16).reshape(n, shard_rows, 3 * PAIR), small_out], axis=1
    )
    turned = turn_blocks(info, leaving)

    size = n
    for index, bit in enumerate(depth_bits[::-1]):
        size //= 2
        got = swap(turned[size:], bit)
        if index == 0:
            for plane in grad_planes:
                plane.got = tie(plane.got, turned)
                plane.finish()
                plane.start()
            got = tie(got, *[plane.send for plane in grad_planes])
            for part in up:
                part.advance(turned, *[plane.send for plane in grad_planes])
        turned = (turned[:size].astype(f32) + got.astype(f32)).astype(bf16)
    for plane in grad_planes:
        plane.finish()
    grad_normed = jnp.concatenate([plane.pieces[0] for plane in grad_planes], axis=0)
    _, normal_one, inverse_one = layer_norm_parts(stream, gain_one, shift_one)
    grad_stream = grad_middle + layer_norm_back(grad_normed, normal_one, inverse_one, gain_one)
    stream_low = grad_stream.astype(bf16)
    for part in up + down:
        while part.order:
            part.advance(stream_low)
    down_sum = jnp.concatenate([part.total() for part in down], axis=0)
    up_totals = [part.total() for part in up]
    out_sum = jnp.concatenate([total[mid * step :] for total in up_totals], axis=0)
    up_sum = jnp.concatenate([total[: mid * step] for total in up_totals], axis=0)
    up_sum = jnp.concatenate([up_sum[k * step : (k + 1) * step] for k in range(wide_parts)], axis=1)
    back = exchange(turned).astype(f32)
    qkv_sum = jnp.zeros((shard_rows, 3, model_width), f32)
    for r in range(PLANE):
        columns = back[r, :shard_rows].reshape(shard_rows, 3, PAIR)
        qkv_sum = lax.dynamic_update_slice(qkv_sum, columns, (0, 0, column(r)))
    small_sum = jnp.sum(back[:, shard_rows:], axis=0)
    qkv_sum = qkv_sum.reshape(shard_rows, 3 * model_width)
    small_sum = small_sum.reshape(-1)
    sums = []
    offset = 0
    for item in small:
        sums.append(small_sum[offset : offset + item.shape[0]])
        offset += item.shape[0]

    return (
        result_low.reshape(micro_count, tok_dev, model_width),
        stream_low.reshape(micro_count, tok_dev, model_width),
        sums[0],
        sums[1],
        qkv_sum,
        sums[2],
        sums[3],
        out_sum,
        sums[4],
        sums[5],
        sums[6],
        up_sum,
        sums[8],
        down_sum,
        sums[7],
    )


def solution(mesh):
    return jax.shard_map(
        body,
        mesh=mesh,
        in_specs=(
            P(None, "seq", None),
            P("seq"),
            P("seq"),
            P("seq", None),
            P("seq"),
            P("seq"),
            P("seq", None),
            P("seq"),
            P("seq"),
            P("seq"),
            P("seq", None),
            P("seq"),
            P("seq", None),
            P("seq"),
            P(None, "seq"),
            P(),
            P(None, "seq", None),
        ),
        out_specs=(
            P(None, "seq", None),
            P(None, "seq", None),
            P("seq"),
            P("seq"),
            P("seq", None),
            P("seq"),
            P("seq"),
            P("seq", None),
            P("seq"),
            P("seq"),
            P("seq"),
            P("seq", None),
            P("seq"),
            P("seq", None),
            P("seq"),
        ),
        check_vma=False,
    )
```

```python
import functools

import jax
import jax.numpy as jnp
from jax import lax
from jax.experimental import pallas as pl
from jax.experimental.pallas import tpu as pltpu
from jax.sharding import PartitionSpec as P

HEAD_DIM = 64
IMG_TOK = 577
PLANE = 8
PAIR = 2 * HEAD_DIM
HALO = IMG_TOK - 1
LEAD = 640
WINDOW = 640
TILE = 256

epsilon = 1e-05
negative_fill = -1e30
bf16 = jnp.bfloat16
f32 = jnp.float32


def product(left, right):
    return jnp.dot(left, right, preferred_element_type=f32)


def product_tn(left, right):
    return lax.dot_general(left, right, (((0,), (0,)), ((), ())), preferred_element_type=f32)


def product_nt(left, right):
    return lax.dot_general(left, right, (((1,), (1,)), ((), ())), preferred_element_type=f32)


def swap(block, bit):
    n = lax.axis_size("seq")
    return lax.ppermute(block, "seq", [(i, i ^ bit) for i in range(n)])


def shift_plane(block, planes):
    n = lax.axis_size("seq")
    step = planes * PLANE
    return lax.ppermute(block, "seq", [(i, i + step) for i in range(n) if 0 <= i + step < n])


def places(order):
    held = [0]
    for bit in order:
        held = held + [r ^ bit for r in held]
    return held


def gather_bits(block, order):
    current = block[None]
    for bit in order[:-1]:
        current = jnp.concatenate([current, swap(current, bit)], axis=0)
    return current, swap(current, order[-1])


def position(r, order):
    return sum(((r >> (bit.bit_length() - 1)) & 1) << k for k, bit in enumerate(order))


def tie(value, *earlier):
    return lax.optimization_barrier((value,) + earlier)[0]


def own_bit(me, bit):
    return jnp.where(jnp.bitwise_and(me, bit) != 0, 1, 0)


def pick(block, axis, index):
    return lax.dynamic_index_in_dim(block, index, axis, keepdims=False)


def exchange(blocks):
    bits = PLANE.bit_length() - 1
    cube = blocks.reshape((2,) * bits + blocks.shape[1:])
    for axis in reversed(range(bits)):
        got = swap(lax.index_in_dim(cube, 1, axis, keepdims=False), 1 << (bits - 1 - axis))
        cube = jnp.stack([lax.index_in_dim(cube, 0, axis, keepdims=False), got], axis=axis)
    return cube.reshape(blocks.shape)


class Scatter:
    def __init__(self, me, partials, order):
        self.me = me
        self.partials = partials
        depth = sum(item.shape[0] for item in partials[0]).bit_length() - 1
        self.bits = [1 << (depth - 1 - axis) for axis in range(depth)]
        self.order = list(order)
        self.split()

    def half(self, axis, index):
        if self.partials is None:
            kept = pick(self.block, axis, index).astype(f32)
            return (kept + pick(self.got, axis, index).astype(f32)).astype(bf16)
        joined = []
        for items in self.partials:
            picked = [pick(item.reshape((-1, 2) + item.shape[1:]), 1, index) for item in items]
            joined.append(picked[0] if len(picked) == 1 else jnp.concatenate(picked, axis=0))
        joined = joined[0] if len(joined) == 1 else jnp.concatenate(joined, axis=1)
        return joined.reshape((2,) * len(self.bits) + joined.shape[1:])

    def split(self):
        self.bit = self.order.pop(0)
        axis = self.bits.index(self.bit)
        self.bits.pop(axis)
        mine = own_bit(self.me, self.bit)
        self.send, keep = self.half(axis, 1 - mine), self.half(axis, mine)
        self.block, self.got, self.partials = keep, None, None

    def swap(self):
        self.got = swap(self.send, self.bit)

    def advance(self, *earlier):
        if earlier:
            self.got = tie(self.got, *earlier)
        self.split()
        self.swap()

    def total(self):
        return self.block.astype(f32) + self.got.astype(f32)


def turn_kernel(info, blocks, turned):
    for r in range(blocks.shape[0]):
        turned[r] = blocks[jnp.bitwise_xor(info[0], r)]


def turn_blocks(info, blocks):
    return pl.pallas_call(
        turn_kernel,
        grid_spec=pltpu.PrefetchScalarGridSpec(
            num_scalar_prefetch=1,
            grid=(1,),
            in_specs=[pl.BlockSpec(blocks.shape, lambda g, i: (0, 0, 0))],
            out_specs=pl.BlockSpec(blocks.shape, lambda g, i: (0, 0, 0)),
        ),
        out_shape=jax.ShapeDtypeStruct(blocks.shape, blocks.dtype),
    )(info, blocks)


def load_rows(orders, micros, place_in_plane, qkv, before, after, queries, keys, values, sem):
    blocks, rows = qkv.shape[1], qkv.shape[2]
    own = blocks * rows
    for buffer in (keys, values):
        for slot in range(len(micros)):
            buffer[slot, 0 : LEAD - HALO, :] = jnp.zeros((LEAD - HALO, PAIR), bf16)
            tail = buffer.shape[1] - (LEAD + own + HALO)
            buffer[slot, LEAD + own + HALO :, :] = jnp.zeros((tail, PAIR), bf16)
    started = []
    for slot, m in enumerate(micros):
        for p, r in enumerate(places(orders[m])):
            spot = pl.multiple_of(jnp.bitwise_xor(place_in_plane, r) * rows, rows)
            started += [
                pltpu.make_async_copy(
                    qkv.at[m, p, :, pl.ds(0, PAIR)], queries.at[slot, pl.ds(spot, rows)], sem
                ),
                pltpu.make_async_copy(
                    qkv.at[m, p, :, pl.ds(PAIR, PAIR)], keys.at[slot, pl.ds(LEAD + spot, rows)], sem
                ),
                pltpu.make_async_copy(
                    qkv.at[m, p, :, pl.ds(2 * PAIR, PAIR)], values.at[slot, pl.ds(LEAD + spot, rows)], sem
                ),
            ]
        for which, buffer in enumerate((keys, values)):
            columns = pl.ds(which * PAIR, PAIR)
            started += [
                pltpu.make_async_copy(
                    before.at[m, :, columns], buffer.at[slot, pl.ds(LEAD - HALO, HALO)], sem
                ),
                pltpu.make_async_copy(
                    after.at[m, :, columns], buffer.at[slot, pl.ds(LEAD + own, HALO)], sem
                ),
            ]
    return started


def image_span(bounds, m, image, base):
    begin = bounds[m, image] - base + LEAD
    finish = bounds[m, image + 1] - base + LEAD
    return begin, finish


def key_block(keys, m, begin, finish, key_start, key_aug):
    key_aug[:, :PAIR] = keys[m, pl.ds(key_start, WINDOW), :]
    rows = key_start + lax.broadcasted_iota(jnp.int32, (WINDOW, PAIR), 0)
    inside = (rows >= begin) & (rows < finish)
    key_aug[:, PAIR:] = jnp.where(inside, 0.0, negative_fill).astype(bf16)


def split_heads(rows_f32, lanes):
    first = jnp.where(lanes < HEAD_DIM, rows_f32, 0.0).astype(bf16)
    second = jnp.where(lanes >= HEAD_DIM, rows_f32, 0.0).astype(bf16)
    return first, second


def attend_kernel(
    orders, info, bounds, qkv, before, after, mixed, stats, queries, keys, values, result, result_low, key_aug, value_t, sem
):
    micro_count, blocks, rows, _ = qkv.shape
    own = blocks * rows
    place_in_plane, base = info[1], info[2]
    image_count = bounds.shape[1] - 1
    started = load_rows(orders, range(micro_count), place_in_plane, qkv, before, after, queries, keys, values, sem)
    for copy in started:
        copy.start()
    value_t[:, HEAD_DIM:, :] = jnp.ones((2, 16, WINDOW), bf16)
    lanes = lax.broadcasted_iota(jnp.int32, (TILE, PAIR), 1)
    rows_iota = lax.broadcasted_iota(jnp.int32, (TILE, PAIR), 0)
    lane_row = lax.broadcasted_iota(jnp.int32, (1, TILE), 1)
    query_mark = jnp.where(lanes == 0, 1.0, 0.0).astype(bf16)
    for copy in started:
        copy.wait()

    for m in range(micro_count):

        def one_image(image, carry):
            begin, finish = image_span(bounds, m, image, base)

            @pl.when((finish > LEAD) & (begin < LEAD + own))
            def _():
                key_start = pl.multiple_of((begin >> 4) << 4, 16)
                key_block(keys, m, begin, finish, key_start, key_aug)
                turned = values[m, pl.ds(key_start, WINDOW), :].astype(f32).T
                value_t[0, :HEAD_DIM, :] = turned[:HEAD_DIM].astype(bf16)
                value_t[1, :HEAD_DIM, :] = turned[HEAD_DIM:].astype(bf16)
                first_tile = jnp.maximum(begin - LEAD, 0) >> 8
                last_tile = (jnp.minimum(finish - LEAD, own) + TILE - 1) >> 8

                def one_tile(tile, carry):
                    spot = pl.multiple_of(tile * TILE, TILE)
                    scaled = queries[m, pl.ds(spot, TILE), :].astype(f32) * (HEAD_DIM**-0.5)
                    pieces = []
                    inside_lane = (lane_row + (spot + LEAD) >= begin) & (lane_row + (spot + LEAD) < finish)
                    for h, query in enumerate(split_heads(scaled, lanes)):
                        aug = jnp.concatenate([query, query_mark], axis=1)
                        scores = product_nt(key_aug[...], aug)
                        peak = jnp.max(scores, axis=0, keepdims=True)
                        weights = jnp.exp(scores - peak).astype(bf16)
                        out = product(value_t[h], weights)
                        total = out[HEAD_DIM : HEAD_DIM + 1]
                        pieces.append(out[:HEAD_DIM] / total)
                        row = (m * 2 + h) * blocks + tile
                        stats[pl.ds(row, 1), :] = jnp.where(
                            inside_lane, peak + jnp.log(total), stats[pl.ds(row, 1), :]
                        )
                    value = jnp.concatenate(pieces, axis=0).T
                    place_row = rows_iota + (spot + LEAD)
                    inside = (place_row >= begin) & (place_row < finish)
                    result[m, pl.ds(spot, TILE), :] = jnp.where(
                        inside, value, result[m, pl.ds(spot, TILE), :]
                    )
                    return carry

                lax.fori_loop(first_tile, last_tile, one_tile, 0)

            return carry

        lax.fori_loop(0, image_count, one_image, 0)

    result_low[...] = result[...].astype(bf16)
    started = []
    for m in range(micro_count):
        for r in range(blocks):
            spot = pl.multiple_of(jnp.bitwise_xor(place_in_plane, r) * rows, rows)
            started.append(pltpu.make_async_copy(result_low.at[m, pl.ds(spot, rows)], mixed.at[r, m], sem))
    for copy in started:
        copy.start()
    for copy in started:
        copy.wait()


def attend_back_kernel(m, orders, info, bounds, qkv, before, after, mixed, *refs):
    blocks, rows = qkv.shape[1], qkv.shape[2]
    own = blocks * rows
    grad_mixed, refs = refs[:blocks], refs[blocks:]
    stats, grad_query, grad_pairs, grad_before, grad_after, refs = *refs[:5], refs[5:]
    queries, keys, values, result, grads, key_aug, key_t, acc_query, acc_key, acc_value, edge, sem = refs
    place_in_plane, base = info[1], info[2]
    image_count = bounds.shape[1] - 1
    started = load_rows(orders, [m], place_in_plane, qkv, before, after, queries, keys, values, sem)
    for r in range(blocks):
        spot = pl.multiple_of(jnp.bitwise_xor(place_in_plane, r) * rows, rows)
        started += [
            pltpu.make_async_copy(mixed.at[r, m], result.at[pl.ds(spot, rows)], sem),
            pltpu.make_async_copy(grad_mixed[r].at[m], grads.at[pl.ds(spot, rows)], sem),
        ]
    for copy in started:
        copy.start()
    acc_query[...] = jnp.zeros_like(acc_query)
    acc_key[...] = jnp.zeros_like(acc_key)
    acc_value[...] = jnp.zeros_like(acc_value)
    lanes = lax.broadcasted_iota(jnp.int32, (TILE, PAIR), 1)
    lane_row = lax.broadcasted_iota(jnp.int32, (1, TILE), 1)
    query_mark = jnp.where(lanes == 0, 1.0, 0.0).astype(bf16)
    for copy in started:
        copy.wait()


    def one_image(image, carry):
        begin, finish = image_span(bounds, m, image, base)

        @pl.when((finish > LEAD) & (begin < LEAD + own))
        def _():
            key_start = pl.multiple_of((begin >> 4) << 4, 16)
            key_rows = pl.ds(key_start, WINDOW)
            key_block(keys, 0, begin, finish, key_start, key_aug)
            turned = keys[0, key_rows, :].astype(f32).T
            key_t[0] = turned[:HEAD_DIM].astype(bf16)
            key_t[1] = turned[HEAD_DIM:].astype(bf16)
            first_tile = jnp.maximum(begin - LEAD, 0) >> 8
            last_tile = (jnp.minimum(finish - LEAD, own) + TILE - 1) >> 8

            def one_tile(tile, carry):
                spot = pl.multiple_of(tile * TILE, TILE)
                here = pl.ds(spot, TILE)
                scaled = queries[0, here, :].astype(f32) * (HEAD_DIM**-0.5)
                grad = grads[ here, :].astype(f32)
                dots = (grad * result[ here, :].astype(f32)).T
                inside_lane = (lane_row + (spot + LEAD) >= begin) & (lane_row + (spot + LEAD) < finish)
                both = zip(split_heads(scaled, lanes), split_heads(grad, lanes))
                pieces = []
                add_key, add_value = None, None
                for h, (query, grad_h) in enumerate(both):
                    row = (m * 2 + h) * blocks + tile
                    level = jnp.where(inside_lane, stats[pl.ds(row, 1), :], -negative_fill)
                    row_dot = jnp.sum(
                        dots[h * HEAD_DIM : (h + 1) * HEAD_DIM], axis=0, keepdims=True
                    )
                    aug = jnp.concatenate([query, query_mark], axis=1)
                    shares = jnp.exp(product_nt(key_aug[...], aug) - level)
                    grad_share = product_nt(values[0, key_rows, :], grad_h)
                    grad_scores = (shares * (grad_share - row_dot)).astype(bf16)
                    value_part = product(shares.astype(bf16), grad_h)
                    key_part = product(grad_scores, query)
                    add_value = value_part if h == 0 else add_value + value_part
                    add_key = key_part if h == 0 else add_key + key_part
                    pieces.append(product(key_t[h], grad_scores))
                acc_value[ key_rows, :] += add_value
                acc_key[ key_rows, :] += add_key
                acc_query[ here, :] += jnp.concatenate(pieces, axis=0).T * (HEAD_DIM**-0.5)
                return carry

            lax.fori_loop(first_tile, last_tile, one_tile, 0)

        return carry

    lax.fori_loop(0, image_count, one_image, 0)

    edge_rows = grad_before.shape[0]
    edge[0, : edge_rows - HALO, :] = jnp.zeros((edge_rows - HALO, 2 * PAIR), bf16)
    edge[1, HALO:, :] = jnp.zeros((edge_rows - HALO, 2 * PAIR), bf16)
    started = [pltpu.make_async_copy(acc_query, grad_query, sem)]
    for which, acc in enumerate((acc_key, acc_value)):
        columns = pl.ds(which * PAIR, PAIR)
        edge[0, edge_rows - HALO :, which * PAIR : (which + 1) * PAIR] = acc[LEAD - HALO : LEAD, :].astype(bf16)
        edge[1, :HALO, which * PAIR : (which + 1) * PAIR] = acc[LEAD + own : LEAD + own + HALO, :].astype(bf16)
        started.append(pltpu.make_async_copy(acc.at[pl.ds(LEAD, own)], grad_pairs.at[:, columns], sem))
    started.append(pltpu.make_async_copy(edge.at[0], grad_before, sem))
    started.append(pltpu.make_async_copy(edge.at[1], grad_after, sem))
    for copy in started:
        copy.start()
    for copy in started:
        copy.wait()


def cover(rows, passes):
    scores = 2 * rows * WINDOW
    return pl.CostEstimate(
        flops=4 * scores * PAIR, transcendentals=scores, bytes_accessed=passes * scores
    )


def any_specs(count):
    return [pl.BlockSpec(memory_space=pl.ANY)] * count


def attend(orders, info, bounds, qkv, before, after):
    micro_count, blocks, rows, _ = qkv.shape
    own = blocks * rows
    span = LEAD + own + LEAD
    stat_rows = micro_count * 2 * blocks
    return pl.pallas_call(
        functools.partial(attend_kernel, orders),
        grid_spec=pltpu.PrefetchScalarGridSpec(
            num_scalar_prefetch=2,
            grid=(1,),
            in_specs=any_specs(3),
            out_specs=any_specs(1) + [pl.BlockSpec((stat_rows, TILE), lambda g, a, b: (0, 0))],
            scratch_shapes=[
                pltpu.VMEM((micro_count, own, PAIR), bf16),
                pltpu.VMEM((micro_count, span, PAIR), bf16),
                pltpu.VMEM((micro_count, span, PAIR), bf16),
                pltpu.VMEM((micro_count, own, PAIR), f32),
                pltpu.VMEM((micro_count, own, PAIR), bf16),
                pltpu.VMEM((WINDOW, 2 * PAIR), bf16),
                pltpu.VMEM((2, HEAD_DIM + 16, WINDOW), bf16),
                pltpu.SemaphoreType.DMA,
            ],
        ),
        out_shape=[
            jax.ShapeDtypeStruct((blocks, micro_count, rows, PAIR), bf16),
            jax.ShapeDtypeStruct((stat_rows, TILE), f32),
        ],
        cost_estimate=cover(micro_count * own, 30),
    )(info, bounds, qkv, before, after)


def attend_back(m, orders, info, bounds, qkv, before, after, mixed, grad_mixed, stats):
    _, blocks, rows, _ = qkv.shape
    own = blocks * rows
    span = LEAD + own + LEAD
    edge_rows = -(-HALO // rows) * rows
    return pl.pallas_call(
        functools.partial(attend_back_kernel, m, orders),
        grid_spec=pltpu.PrefetchScalarGridSpec(
            num_scalar_prefetch=2,
            grid=(1,),
            in_specs=any_specs(4 + blocks) + [pl.BlockSpec(stats.shape, lambda g, a, b: (0, 0))],
            out_specs=any_specs(4),
            scratch_shapes=[
                pltpu.VMEM((1, own, PAIR), bf16),
                pltpu.VMEM((1, span, PAIR), bf16),
                pltpu.VMEM((1, span, PAIR), bf16),
                pltpu.VMEM((own, PAIR), bf16),
                pltpu.VMEM((own, PAIR), bf16),
                pltpu.VMEM((WINDOW, 2 * PAIR), bf16),
                pltpu.VMEM((2, HEAD_DIM, WINDOW), bf16),
                pltpu.VMEM((own, PAIR), f32),
                pltpu.VMEM((span, PAIR), f32),
                pltpu.VMEM((span, PAIR), f32),
                pltpu.VMEM((2, edge_rows, 2 * PAIR), bf16),
                pltpu.SemaphoreType.DMA,
            ],
        ),
        out_shape=[
            jax.ShapeDtypeStruct((own, PAIR), f32),
            jax.ShapeDtypeStruct((own, 2 * PAIR), f32),
            jax.ShapeDtypeStruct((edge_rows, 2 * PAIR), bf16),
            jax.ShapeDtypeStruct((edge_rows, 2 * PAIR), bf16),
        ],
        cost_estimate=cover(own, 35),
    )(info, bounds, qkv, before, after, mixed, *grad_mixed, stats)


def join_kernel(order, info, query, pairs, head, tail, joined):
    blocks, rows, _ = joined.shape
    edge_blocks = head.shape[0] // rows
    for tile in range(blocks):
        here = pl.ds(tile * rows, rows)
        total = pairs[here, :]
        if tile < edge_blocks:
            total = total + head[here, :].astype(f32)
        if tile >= blocks - edge_blocks:
            total = total + tail[pl.ds((tile - (blocks - edge_blocks)) * rows, rows), :].astype(f32)
        target = position(jnp.bitwise_xor(info[1], tile), order)
        joined[target, :, :PAIR] = query[here, :].astype(bf16)
        joined[target, :, PAIR:] = total.astype(bf16)


def join_grads(order, info, grad_query, grad_pairs, head, tail, rows):
    own = grad_query.shape[0]
    blocks = own // rows
    ins = (grad_query, grad_pairs, head, tail)
    return pl.pallas_call(
        functools.partial(join_kernel, order),
        grid_spec=pltpu.PrefetchScalarGridSpec(
            num_scalar_prefetch=1,
            grid=(1,),
            in_specs=[pl.BlockSpec(item.shape, lambda g, i: (0, 0)) for item in ins],
            out_specs=pl.BlockSpec((blocks, rows, 3 * PAIR), lambda g, i: (0, 0, 0)),
        ),
        out_shape=jax.ShapeDtypeStruct((blocks, rows, 3 * PAIR), bf16),
    )(info, *ins)


def layer_norm_parts(values, gain, shift):
    center = values - jnp.mean(values, axis=-1, keepdims=True)
    inverse = lax.rsqrt(jnp.mean(center * center, axis=-1, keepdims=True) + epsilon)
    normal = center * inverse
    return (normal * gain + shift, normal, inverse)


def layer_norm_back(grad_normed, normal, inverse, gain):
    scaled = grad_normed * gain
    centered = scaled - jnp.mean(scaled, axis=-1, keepdims=True)
    return inverse * (centered - normal * jnp.mean(scaled * normal, axis=-1, keepdims=True))


class PlaneScatter:
    def __init__(self, partial, held, order):
        self.pieces = [partial[position(r, held)].astype(bf16) for r in range(PLANE)]
        self.left = list(range(PLANE))
        self.order = list(order)

    def start(self, *earlier):
        self.bit = self.order.pop(0)
        self.keep = [r for r in self.left if not r & self.bit]
        self.send = jnp.stack([self.pieces[r | self.bit] for r in self.keep])
        if earlier:
            self.send = tie(self.send, *earlier)
        self.got = swap(self.send, self.bit)

    def finish(self):
        for position, r in enumerate(self.keep):
            added = self.pieces[r].astype(f32) + self.got[position].astype(f32)
            self.pieces[r] = added.astype(bf16) if self.order else added
        self.left = self.keep


def body(
    tokens,
    ln1_gain,
    ln1_bias,
    qkv_weight,
    q_bias,
    v_bias,
    out_weight,
    out_bias,
    ln2_gain,
    ln2_bias,
    fc1_weight,
    fc1_bias,
    fc2_weight,
    fc2_bias,
    image_ids,
    image_starts,
    cotangent,
):
    micro_count, tok_dev, model_width = tokens.shape
    n = lax.axis_size("seq")
    own_tokens = micro_count * tok_dev
    plane_rows = PLANE * tok_dev
    stream_len = tok_dev * n
    me = lax.axis_index("seq")
    mine = jnp.bitwise_and(me, PLANE - 1)
    base = (me - mine) * tok_dev
    info = jnp.stack([me, mine, base]).astype(jnp.int32)
    bounds = jnp.concatenate(
        [image_starts, jnp.full((micro_count, 1), stream_len, jnp.int32)], axis=1
    )
    plane_bits = [1, 2, 4]
    depth_bits = []
    bit = PLANE
    while bit < n:
        depth_bits.append(bit)
        bit *= 2

    small = [ln1_gain, ln1_bias, q_bias, v_bias, out_bias, ln2_gain, ln2_bias, fc2_bias, fc1_bias]
    shard_rows = qkv_weight.shape[0]
    small_len = sum(item.shape[0] for item in small)
    spare_rows = -(-small_len // (8 * 3 * PAIR)) * 8
    narrow = small[0].shape[0]
    small_rows = jnp.concatenate([item.reshape(-1, narrow) for item in small], axis=0)
    used = small_rows.shape[0]
    small_rows = jnp.pad(small_rows, ((0, -used % 16), (0, 3 * PAIR - narrow)))
    by_pair = qkv_weight.reshape(shard_rows, 3, PLANE, PAIR).transpose(2, 0, 1, 3)
    by_pair = by_pair.reshape(PLANE, shard_rows, 3 * PAIR)
    outgoing = jnp.concatenate(
        [by_pair, jnp.broadcast_to(small_rows[None], (PLANE,) + small_rows.shape)], axis=1
    )
    arrived = exchange(outgoing[jnp.bitwise_xor(mine, jnp.arange(PLANE))])

    token_orders = [[2, 4, 1] if m % 2 == 0 else [4, 2, 1] for m in range(micro_count)]
    gathered = [tokens[m][None] for m in range(micro_count)]
    current = arrived
    for k in range(3):
        got = [swap(item, token_orders[m][k]) for m, item in enumerate(gathered)]
        if k == 1:
            current = current[None]
            for bit in depth_bits[::-1]:
                current = jnp.stack([current, swap(current, bit)], axis=1)
                current = current.reshape((-1,) + arrived.shape)
            current = current.reshape((n,) + arrived.shape[1:])
            early = got + [current]
            got[0] = tie(got[0], current)
        gathered = [jnp.concatenate(pair, axis=0) for pair in zip(gathered, got)]

    step = out_weight.shape[0]
    wide_parts = fc1_weight.shape[1] // model_width
    shards = [out_weight]
    shards += [fc1_weight[:, k * model_width : (k + 1) * model_width] for k in range(wide_parts)]
    packed = tie(jnp.concatenate(shards + [fc2_weight], axis=0), *early)
    every = lax.all_gather(packed, "seq")
    out_full = every[:, :step].reshape(model_width, model_width)
    ups = [every[:, (1 + k) * step : (2 + k) * step].reshape(model_width, -1) for k in range(wide_parts)]
    share = n // wide_parts
    downs = [
        every[k * share : (k + 1) * share, (1 + wide_parts) * step :].reshape(-1, model_width)
        for k in range(wide_parts)
    ]

    pair_blocks = turn_blocks(info, current)
    pair_weight = pair_blocks[:, :shard_rows].reshape(n * shard_rows, 3 * PAIR)
    small_all = pair_blocks[:, shard_rows : shard_rows + used, :narrow].astype(f32)
    small_full = [small_all[:, k].reshape(-1) for k in range(len(small) - 1)]
    small_full.append(small_all[:, len(small) - 1 :].reshape(-1))
    gain_one, shift_one, q_shift, v_shift, out_shift, gain_two, shift_two, down_shift, up_shift = small_full

    plane_stream = jnp.stack(gathered)
    plane_flat = plane_stream.reshape(micro_count * plane_rows, model_width)
    normed, _, _ = layer_norm_parts(plane_flat.astype(f32), gain_one, shift_one)
    normed_low = normed.astype(bf16)
    pair_shift = jnp.concatenate(
        [
            lax.dynamic_slice_in_dim(q_shift, mine * PAIR, PAIR),
            jnp.zeros((PAIR,), f32),
            lax.dynamic_slice_in_dim(v_shift, mine * PAIR, PAIR),
        ]
    )
    qkv = (product(normed_low, pair_weight) + pair_shift).astype(bf16)
    qkv = qkv.reshape(micro_count, PLANE, tok_dev, 3 * PAIR)

    edge_blocks = -(-HALO // tok_dev)

    def plane_block(index):
        offset = jnp.bitwise_xor(mine, index)
        blocks = [pick(qkv[m], 0, position(offset, order)) for m, order in enumerate(token_orders)]
        return jnp.stack(blocks)[:, :, PAIR:]

    last_rows = jnp.concatenate([plane_block(PLANE - edge_blocks + k) for k in range(edge_blocks)], axis=1)
    first_rows = jnp.concatenate([plane_block(k) for k in range(edge_blocks)], axis=1)
    before = shift_plane(last_rows[:, edge_blocks * tok_dev - HALO :], 1)
    after = shift_plane(first_rows[:, :HALO], -1)
    mixed_pair, stats = attend(token_orders, info, bounds, qkv, before, after)

    def column(r):
        return jnp.bitwise_xor(mine, r) * PAIR

    mixed_low = jnp.zeros((own_tokens, model_width), bf16)
    for r in range(PLANE):
        part = mixed_pair[r] if r == 0 else swap(mixed_pair[r], r)
        mixed_low = lax.dynamic_update_slice(mixed_low, part.reshape(own_tokens, PAIR), (0, column(r)))

    stream = tokens.reshape(own_tokens, model_width).astype(f32)
    cotangent_low = cotangent.reshape(own_tokens, model_width)
    middle = stream + product(mixed_low, out_full) + out_shift
    normed_two, normal_two, inverse_two = layer_norm_parts(middle, gain_two, shift_two)
    normed_two_low = normed_two.astype(bf16)
    up_shifts = up_shift.reshape(wide_parts, model_width)
    actives, grad_hiddens = [], []
    for k in range(wide_parts):
        hidden = product(normed_two_low, ups[k]) + up_shifts[k]
        gate = jax.nn.sigmoid(1.702 * hidden)
        actives.append((hidden * gate).astype(bf16))
        grad_active = product_nt(cotangent_low, downs[k])
        grad_hiddens.append((grad_active * (gate + 1.702 * hidden * gate * (1.0 - gate))).astype(bf16))

    def by_device(partial, devices=n):
        return partial.astype(bf16).reshape(devices, -1, model_width)

    order_a = [1, 2, 4] + depth_bits
    order_b = [1, 4, 2] + depth_bits
    grad_downs = [by_device(product_tn(active, cotangent_low), share) for active in actives]
    half = grad_downs[0].shape[1] // 2
    down = [
        Scatter(me, [[item[:, :half] for item in grad_downs]], [1] + depth_bits[:1] + [2, 4] + depth_bits[1:]),
        Scatter(me, [[item[:, half:] for item in grad_downs]], [1] + depth_bits[:1] + [4, 2] + depth_bits[1:]),
    ]
    for part in down:
        part.swap()
    grad_hiddens[0] = tie(grad_hiddens[0], *[part.send for part in down])

    grad_normed_two = product_nt(grad_hiddens[0], ups[0])
    for k in range(1, wide_parts):
        grad_normed_two = grad_normed_two + product_nt(grad_hiddens[k], ups[k])
    for part in down:
        part.advance(grad_normed_two)
    grad_normed_two = tie(grad_normed_two, *[part.send for part in down])
    grad_middle = cotangent_low.astype(f32) + layer_norm_back(
        grad_normed_two, normal_two, inverse_two, gain_two
    )
    grad_branch_low = grad_middle.astype(bf16)
    grad_mixed_low = product_nt(grad_branch_low, out_full).astype(bf16)
    grad_parts = []
    for r in range(PLANE):
        part = lax.dynamic_slice(grad_mixed_low, (0, column(r)), (own_tokens, PAIR))
        part = part.reshape(micro_count, tok_dev, PAIR)
        grad_parts.append(part if r == 0 else swap(part, r))

    later = tie(normed_two_low, grad_mixed_low)
    grad_ups = [by_device(product_tn(later, grad_hidden)) for grad_hidden in grad_hiddens]
    grad_out_weight = by_device(product_tn(mixed_low, grad_branch_low))
    mid = wide_parts // 2
    up = [
        Scatter(me, [[item] for item in grad_ups[:mid] + [grad_out_weight[:, : step // 2]]], order_a),
        Scatter(me, [[item] for item in grad_ups[mid:] + [grad_out_weight[:, step // 2 :]]], order_b),
    ]
    for part in up:
        part.swap()
    result = middle + down_shift
    after_up = tie(actives[0], *[part.send for part in up])
    for k in range(wide_parts):
        result = result + product(after_up if k == 0 else actives[k], downs[k])
    result_low = result.astype(bf16)
    for part in up:
        part.advance(result_low, *grad_parts)

    before_back = [part.send for part in up]
    grad_planes = []
    grad_pair_weight, column_sum = 0.0, 0.0
    for m in range(micro_count):
        own_grad = tie(grad_parts[0], *before_back)
        grad_query, grad_pairs, grad_before, grad_after = attend_back(
            m, token_orders, info, bounds, qkv, before, after, mixed_pair, [own_grad] + grad_parts[1:], stats
        )
        from_next = shift_plane(grad_before, -1)
        from_last = shift_plane(grad_after, 1)
        for plane in grad_planes:
            plane.got = tie(plane.got, grad_before)
            plane.finish()
            plane.start()
        for part in up + down:
            part.advance(grad_before)
        sends = [part.send for part in up + down] + [plane.send for plane in grad_planes]
        grad_query = tie(grad_query, *sends)
        joined = join_grads(token_orders[m], info, grad_query, grad_pairs, from_last, from_next, tok_dev)
        grad_flat = joined.reshape(plane_rows, 3 * PAIR)
        grad_plane = product_nt(grad_flat, pair_weight).reshape(PLANE, tok_dev, model_width)
        order = [1, 2, 4] if m % 2 == 0 else [1, 4, 2]
        plane = PlaneScatter(grad_plane, token_orders[m], order)
        plane.start()
        grad_flat = tie(grad_flat, plane.send)
        rows = normed_low[m * plane_rows : (m + 1) * plane_rows]
        added = product_tn(rows, grad_flat)
        grad_pair_weight = grad_pair_weight + added
        column_sum = column_sum + jnp.sum(grad_flat.astype(f32), axis=0)
        if m < micro_count - 1:
            plane.got = tie(plane.got, added)
        plane.finish()
        plane.start()
        grad_planes.append(plane)
        before_back = [plane.send]
    grad_pair_weight = tie(grad_pair_weight, plane.send)

    wide = pair_weight.astype(f32)
    grad_shift_one = jnp.sum(wide * column_sum, axis=1)
    grad_gain_one = jnp.sum(wide * grad_pair_weight, axis=1)
    grad_gain_one = (grad_gain_one - shift_one * grad_shift_one) / gain_one

    def at_columns(part):
        return lax.dynamic_update_slice(jnp.zeros((model_width,), f32), part, (mine * PAIR,))

    small_grads = [
        grad_gain_one,
        grad_shift_one,
        at_columns(column_sum[:PAIR]),
        at_columns(column_sum[2 * PAIR :]),
        jnp.sum(grad_branch_low.astype(f32), axis=0),
        jnp.sum(grad_normed_two * normal_two, axis=0),
        jnp.sum(grad_normed_two, axis=0),
        jnp.sum(cotangent_low.astype(f32), axis=0),
        jnp.concatenate([jnp.sum(item.astype(f32), axis=0) for item in grad_hiddens]),
    ]
    small_out = jnp.concatenate([item.reshape(n, -1) for item in small_grads], axis=1).astype(bf16)
    small_out = jnp.pad(small_out, ((0, 0), (0, spare_rows * 3 * PAIR - small_len)))
    small_out = small_out.reshape(n, spare_rows, 3 * PAIR)
    leaving = jnp.concatenate(
        [grad_pair_weight.astype(bf16).reshape(n, shard_rows, 3 * PAIR), small_out], axis=1
    )
    turned = turn_blocks(info, leaving)

    turned = turned.reshape((n // PLANE, PLANE) + turned.shape[1:])
    for index, bit in enumerate(depth_bits):
        turned = turned.reshape((-1, 2) + turned.shape[1:])
        sent = turned[:, 1]
        got = swap(sent, bit)
        if index == 0:
            plane = grad_planes[-1]
            plane.got = tie(plane.got, sent)
            plane.finish()
            plane.start()
            for part in up + down:
                if part.order:
                    part.advance(sent, plane.send)
            got = tie(got, *[part.send for part in up + down])
        turned = (turned[:, 0].astype(f32) + got.astype(f32)).astype(bf16)
    turned = turned.reshape((PLANE,) + turned.shape[2:])
    for plane in grad_planes:
        plane.finish()
    grad_normed = jnp.concatenate([plane.pieces[0] for plane in grad_planes], axis=0)
    _, normal_one, inverse_one = layer_norm_parts(stream, gain_one, shift_one)
    grad_stream = grad_middle + layer_norm_back(grad_normed, normal_one, inverse_one, gain_one)
    stream_low = grad_stream.astype(bf16)
    for part in up + down:
        while part.order:
            part.advance(stream_low)
    down_sum = jnp.concatenate([part.total() for part in down], axis=0)
    up_totals = [part.total() for part in up]
    out_sum = jnp.concatenate([total[mid * step :] for total in up_totals], axis=0)
    up_sum = jnp.concatenate([total[: mid * step] for total in up_totals], axis=0)
    up_sum = jnp.concatenate([up_sum[k * step : (k + 1) * step] for k in range(wide_parts)], axis=1)
    back = exchange(tie(turned, *[plane.pieces[0] for plane in grad_planes])).astype(f32)
    qkv_sum = jnp.zeros((shard_rows, 3, model_width), f32)
    for r in range(PLANE):
        columns = back[r, :shard_rows].reshape(shard_rows, 3, PAIR)
        qkv_sum = lax.dynamic_update_slice(qkv_sum, columns, (0, 0, column(r)))
    small_sum = jnp.sum(back[:, shard_rows:], axis=0)
    qkv_sum = qkv_sum.reshape(shard_rows, 3 * model_width)
    small_sum = small_sum.reshape(-1)
    sums = []
    offset = 0
    for item in small:
        sums.append(small_sum[offset : offset + item.shape[0]])
        offset += item.shape[0]

    return (
        result_low.reshape(micro_count, tok_dev, model_width),
        stream_low.reshape(micro_count, tok_dev, model_width),
        sums[0],
        sums[1],
        qkv_sum,
        sums[2],
        sums[3],
        out_sum,
        sums[4],
        sums[5],
        sums[6],
        up_sum,
        sums[8],
        down_sum,
        sums[7],
    )


def solution(mesh):
    return jax.shard_map(
        body,
        mesh=mesh,
        in_specs=(
            P(None, "seq", None),
            P("seq"),
            P("seq"),
            P("seq", None),
            P("seq"),
            P("seq"),
            P("seq", None),
            P("seq"),
            P("seq"),
            P("seq"),
            P("seq", None),
            P("seq"),
            P("seq", None),
            P("seq"),
            P(None, "seq"),
            P(),
            P(None, "seq", None),
        ),
        out_specs=(
            P(None, "seq", None),
            P(None, "seq", None),
            P("seq"),
            P("seq"),
            P("seq", None),
            P("seq"),
            P("seq"),
            P("seq", None),
            P("seq"),
            P("seq"),
            P("seq"),
            P("seq", None),
            P("seq"),
            P("seq", None),
            P("seq"),
        ),
        check_vma=False,
    )
```

```python
import functools

import jax
import jax.numpy as jnp
from jax import lax
from jax.experimental import pallas as pl
from jax.experimental.pallas import tpu as pltpu
from jax.sharding import PartitionSpec as P

HEAD_DIM = 64
IMG_TOK = 577
PLANE = 8
PAIR = 2 * HEAD_DIM
HALO = IMG_TOK - 1
LEAD = 640
WINDOW = 640
TILE = 256
WIDE = 512

epsilon = 1e-05
negative_fill = -1e30
bf16 = jnp.bfloat16
f32 = jnp.float32


def product(left, right):
    return jnp.dot(left, right, preferred_element_type=f32)


def product_tn(left, right):
    return lax.dot_general(left, right, (((0,), (0,)), ((), ())), preferred_element_type=f32)


def product_nt(left, right):
    return lax.dot_general(left, right, (((1,), (1,)), ((), ())), preferred_element_type=f32)


def swap(block, bit):
    n = lax.axis_size("seq")
    return lax.ppermute(block, "seq", [(i, i ^ bit) for i in range(n)])


def shift_plane(block, planes):
    n = lax.axis_size("seq")
    step = planes * PLANE
    return lax.ppermute(block, "seq", [(i, i + step) for i in range(n) if 0 <= i + step < n])


def places(order):
    held = [0]
    for bit in order:
        held = held + [r ^ bit for r in held]
    return held


def gather_bits(block, order):
    current = block[None]
    for bit in order[:-1]:
        current = jnp.concatenate([current, swap(current, bit)], axis=0)
    return current, swap(current, order[-1])


def position(r, order):
    return sum(((r >> (bit.bit_length() - 1)) & 1) << k for k, bit in enumerate(order))


def tie(value, *earlier):
    return lax.optimization_barrier((value,) + earlier)[0]


def own_bit(me, bit):
    return jnp.where(jnp.bitwise_and(me, bit) != 0, 1, 0)


def pick(block, axis, index):
    return lax.dynamic_index_in_dim(block, index, axis, keepdims=False)


def exchange(blocks):
    bits = PLANE.bit_length() - 1
    cube = blocks.reshape((2,) * bits + blocks.shape[1:])
    for axis in reversed(range(bits)):
        got = swap(lax.index_in_dim(cube, 1, axis, keepdims=False), 1 << (bits - 1 - axis))
        cube = jnp.stack([lax.index_in_dim(cube, 0, axis, keepdims=False), got], axis=axis)
    return cube.reshape(blocks.shape)


class Scatter:
    def __init__(self, me, partials, order):
        self.me = me
        self.partials = partials
        depth = sum(item.shape[0] for item in partials[0]).bit_length() - 1
        self.bits = [1 << (depth - 1 - axis) for axis in range(depth)]
        self.order = list(order)
        self.split()

    def half(self, axis, index):
        if self.partials is None:
            kept = pick(self.block, axis, index).astype(f32)
            return (kept + pick(self.got, axis, index).astype(f32)).astype(bf16)
        joined = []
        for items in self.partials:
            picked = [pick(item.reshape((-1, 2) + item.shape[1:]), 1, index) for item in items]
            joined.append(picked[0] if len(picked) == 1 else jnp.concatenate(picked, axis=0))
        joined = joined[0] if len(joined) == 1 else jnp.concatenate(joined, axis=1)
        return joined.reshape((2,) * len(self.bits) + joined.shape[1:])

    def split(self):
        self.bit = self.order.pop(0)
        axis = self.bits.index(self.bit)
        self.bits.pop(axis)
        mine = own_bit(self.me, self.bit)
        self.send, keep = self.half(axis, 1 - mine), self.half(axis, mine)
        self.block, self.got, self.partials = keep, None, None

    def swap(self):
        self.got = swap(self.send, self.bit)

    def advance(self, *earlier):
        if earlier:
            self.got = tie(self.got, *earlier)
        self.split()
        self.swap()

    def total(self):
        return self.block.astype(f32) + self.got.astype(f32)


def turn_kernel(info, blocks, turned):
    for r in range(blocks.shape[0]):
        turned[r] = blocks[jnp.bitwise_xor(info[0], r)]


def turn_blocks(info, blocks):
    return pl.pallas_call(
        turn_kernel,
        grid_spec=pltpu.PrefetchScalarGridSpec(
            num_scalar_prefetch=1,
            grid=(1,),
            in_specs=[pl.BlockSpec(blocks.shape, lambda g, i: (0, 0, 0))],
            out_specs=pl.BlockSpec(blocks.shape, lambda g, i: (0, 0, 0)),
        ),
        out_shape=jax.ShapeDtypeStruct(blocks.shape, blocks.dtype),
    )(info, blocks)


def load_rows(orders, micros, place_in_plane, qkv, before, after, queries, keys, values, sem):
    blocks, rows = qkv.shape[1], qkv.shape[2]
    own = blocks * rows
    for buffer in (keys, values):
        for slot in range(len(micros)):
            buffer[slot, 0 : LEAD - HALO, :] = jnp.zeros((LEAD - HALO, PAIR), bf16)
            tail = buffer.shape[1] - (LEAD + own + HALO)
            buffer[slot, LEAD + own + HALO :, :] = jnp.zeros((tail, PAIR), bf16)
    started = []
    for slot, m in enumerate(micros):
        for p, r in enumerate(places(orders[m])):
            spot = pl.multiple_of(jnp.bitwise_xor(place_in_plane, r) * rows, rows)
            started += [
                pltpu.make_async_copy(
                    qkv.at[m, p, :, pl.ds(0, PAIR)], queries.at[slot, pl.ds(spot, rows)], sem
                ),
                pltpu.make_async_copy(
                    qkv.at[m, p, :, pl.ds(PAIR, PAIR)], keys.at[slot, pl.ds(LEAD + spot, rows)], sem
                ),
                pltpu.make_async_copy(
                    qkv.at[m, p, :, pl.ds(2 * PAIR, PAIR)], values.at[slot, pl.ds(LEAD + spot, rows)], sem
                ),
            ]
        for which, buffer in enumerate((keys, values)):
            columns = pl.ds(which * PAIR, PAIR)
            started += [
                pltpu.make_async_copy(
                    before.at[m, :, columns], buffer.at[slot, pl.ds(LEAD - HALO, HALO)], sem
                ),
                pltpu.make_async_copy(
                    after.at[m, :, columns], buffer.at[slot, pl.ds(LEAD + own, HALO)], sem
                ),
            ]
    return started


def image_span(bounds, m, image, base):
    begin = bounds[m, image] - base + LEAD
    finish = bounds[m, image + 1] - base + LEAD
    return begin, finish


def key_block(keys, m, begin, finish, key_start, key_aug):
    key_aug[:, :PAIR] = keys[m, pl.ds(key_start, WINDOW), :]
    rows = key_start + lax.broadcasted_iota(jnp.int32, (WINDOW, PAIR), 0)
    inside = (rows >= begin) & (rows < finish)
    key_aug[:, PAIR:] = jnp.where(inside, 0.0, negative_fill).astype(bf16)


def split_heads(rows_f32, lanes):
    first = jnp.where(lanes < HEAD_DIM, rows_f32, 0.0).astype(bf16)
    second = jnp.where(lanes >= HEAD_DIM, rows_f32, 0.0).astype(bf16)
    return first, second


def attend_kernel(
    orders, info, bounds, qkv, before, after, mixed, stats, queries, keys, values, result, result_low, key_aug, value_t, sem
):
    micro_count, blocks, rows, _ = qkv.shape
    own = blocks * rows
    place_in_plane, base = info[1], info[2]
    image_count = bounds.shape[1] - 1
    started = load_rows(orders, range(micro_count), place_in_plane, qkv, before, after, queries, keys, values, sem)
    for copy in started:
        copy.start()
    value_t[:, HEAD_DIM:, :] = jnp.ones((2, 16, WINDOW), bf16)
    lanes = lax.broadcasted_iota(jnp.int32, (WIDE, PAIR), 1)
    rows_iota = lax.broadcasted_iota(jnp.int32, (WIDE, PAIR), 0)
    lane_row = lax.broadcasted_iota(jnp.int32, (1, WIDE), 1)
    query_mark = jnp.where(lanes == 0, 1.0, 0.0).astype(bf16)
    for copy in started:
        copy.wait()

    for m in range(micro_count):

        def one_image(image, carry):
            begin, finish = image_span(bounds, m, image, base)

            @pl.when((finish > LEAD) & (begin < LEAD + own))
            def _():
                key_start = pl.multiple_of((begin >> 4) << 4, 16)
                key_block(keys, m, begin, finish, key_start, key_aug)
                turned = values[m, pl.ds(key_start, WINDOW), :].astype(f32).T
                value_t[0, :HEAD_DIM, :] = turned[:HEAD_DIM].astype(bf16)
                value_t[1, :HEAD_DIM, :] = turned[HEAD_DIM:].astype(bf16)
                first_tile = jnp.maximum(begin - LEAD, 0) >> (WIDE.bit_length() - 1)
                last_tile = (jnp.minimum(finish - LEAD, own) + WIDE - 1) >> (WIDE.bit_length() - 1)

                def one_tile(tile, carry):
                    spot = pl.multiple_of(tile * WIDE, WIDE)
                    scaled = queries[m, pl.ds(spot, WIDE), :].astype(f32) * (HEAD_DIM**-0.5)
                    pieces = []
                    inside_lane = (lane_row + (spot + LEAD) >= begin) & (lane_row + (spot + LEAD) < finish)
                    for h, query in enumerate(split_heads(scaled, lanes)):
                        aug = jnp.concatenate([query, query_mark], axis=1)
                        scores = product_nt(key_aug[...], aug)
                        peak = jnp.max(scores, axis=0, keepdims=True)
                        weights = jnp.exp(scores - peak).astype(bf16)
                        out = product(value_t[h], weights)
                        total = out[HEAD_DIM : HEAD_DIM + 1]
                        pieces.append(out[:HEAD_DIM] / total)
                        row = (m * 2 + h) * (own // WIDE) + tile
                        stats[pl.ds(row, 1), :] = jnp.where(
                            inside_lane, peak + jnp.log(total), stats[pl.ds(row, 1), :]
                        )
                    value = jnp.concatenate(pieces, axis=0).T
                    place_row = rows_iota + (spot + LEAD)
                    inside = (place_row >= begin) & (place_row < finish)
                    result[m, pl.ds(spot, WIDE), :] = jnp.where(
                        inside, value, result[m, pl.ds(spot, WIDE), :]
                    )
                    return carry

                lax.fori_loop(first_tile, last_tile, one_tile, 0)

            return carry

        lax.fori_loop(0, image_count, one_image, 0)

    result_low[...] = result[...].astype(bf16)
    started = []
    for m in range(micro_count):
        for r in range(blocks):
            spot = pl.multiple_of(jnp.bitwise_xor(place_in_plane, r) * rows, rows)
            started.append(pltpu.make_async_copy(result_low.at[m, pl.ds(spot, rows)], mixed.at[r, m], sem))
    for copy in started:
        copy.start()
    for copy in started:
        copy.wait()


def attend_back_kernel(m, orders, info, bounds, qkv, before, after, mixed, *refs):
    blocks, rows = qkv.shape[1], qkv.shape[2]
    own = blocks * rows
    grad_mixed, refs = refs[:blocks], refs[blocks:]
    stats, grad_query, grad_pairs, grad_before, grad_after, refs = *refs[:5], refs[5:]
    queries, keys, values, result, grads, key_aug, key_t, acc_query, acc_key, acc_value, edge, sem = refs
    place_in_plane, base = info[1], info[2]
    image_count = bounds.shape[1] - 1
    started = load_rows(orders, [m], place_in_plane, qkv, before, after, queries, keys, values, sem)
    for r in range(blocks):
        spot = pl.multiple_of(jnp.bitwise_xor(place_in_plane, r) * rows, rows)
        started += [
            pltpu.make_async_copy(mixed.at[r, m], result.at[pl.ds(spot, rows)], sem),
            pltpu.make_async_copy(grad_mixed[r].at[m], grads.at[pl.ds(spot, rows)], sem),
        ]
    for copy in started:
        copy.start()
    acc_query[...] = jnp.zeros_like(acc_query)
    acc_key[...] = jnp.zeros_like(acc_key)
    acc_value[...] = jnp.zeros_like(acc_value)
    lanes = lax.broadcasted_iota(jnp.int32, (TILE, PAIR), 1)
    lane_row = lax.broadcasted_iota(jnp.int32, (1, TILE), 1)
    query_mark = jnp.where(lanes == 0, 1.0, 0.0).astype(bf16)
    for copy in started:
        copy.wait()


    def one_image(image, carry):
        begin, finish = image_span(bounds, m, image, base)

        @pl.when((finish > LEAD) & (begin < LEAD + own))
        def _():
            key_start = pl.multiple_of((begin >> 4) << 4, 16)
            key_rows = pl.ds(key_start, WINDOW)
            key_block(keys, 0, begin, finish, key_start, key_aug)
            turned = keys[0, key_rows, :].astype(f32).T
            key_t[0] = turned[:HEAD_DIM].astype(bf16)
            key_t[1] = turned[HEAD_DIM:].astype(bf16)
            first_tile = jnp.maximum(begin - LEAD, 0) >> 8
            last_tile = (jnp.minimum(finish - LEAD, own) + TILE - 1) >> 8

            def one_tile(tile, carry):
                spot = pl.multiple_of(tile * TILE, TILE)
                here = pl.ds(spot, TILE)
                scaled = queries[0, here, :].astype(f32) * (HEAD_DIM**-0.5)
                grad = grads[ here, :].astype(f32)
                dots = (grad * result[ here, :].astype(f32)).T
                inside_lane = (lane_row + (spot + LEAD) >= begin) & (lane_row + (spot + LEAD) < finish)
                both = zip(split_heads(scaled, lanes), split_heads(grad, lanes))
                pieces = []
                add_key, add_value = None, None
                for h, (query, grad_h) in enumerate(both):
                    row = (m * 2 + h) * blocks + tile
                    level = jnp.where(inside_lane, stats[pl.ds(row, 1), :], -negative_fill)
                    row_dot = jnp.sum(
                        dots[h * HEAD_DIM : (h + 1) * HEAD_DIM], axis=0, keepdims=True
                    )
                    aug = jnp.concatenate([query, query_mark], axis=1)
                    shares = jnp.exp(product_nt(key_aug[...], aug) - level)
                    grad_share = product_nt(values[0, key_rows, :], grad_h)
                    grad_scores = (shares * (grad_share - row_dot)).astype(bf16)
                    value_part = product(shares.astype(bf16), grad_h)
                    key_part = product(grad_scores, query)
                    add_value = value_part if h == 0 else add_value + value_part
                    add_key = key_part if h == 0 else add_key + key_part
                    pieces.append(product(key_t[h], grad_scores))
                acc_value[ key_rows, :] += add_value
                acc_key[ key_rows, :] += add_key
                acc_query[ here, :] += jnp.concatenate(pieces, axis=0).T * (HEAD_DIM**-0.5)
                return carry

            lax.fori_loop(first_tile, last_tile, one_tile, 0)

        return carry

    lax.fori_loop(0, image_count, one_image, 0)

    edge_rows = grad_before.shape[0]
    edge[0, : edge_rows - HALO, :] = jnp.zeros((edge_rows - HALO, 2 * PAIR), bf16)
    edge[1, HALO:, :] = jnp.zeros((edge_rows - HALO, 2 * PAIR), bf16)
    started = [pltpu.make_async_copy(acc_query, grad_query, sem)]
    for which, acc in enumerate((acc_key, acc_value)):
        columns = pl.ds(which * PAIR, PAIR)
        edge[0, edge_rows - HALO :, which * PAIR : (which + 1) * PAIR] = acc[LEAD - HALO : LEAD, :].astype(bf16)
        edge[1, :HALO, which * PAIR : (which + 1) * PAIR] = acc[LEAD + own : LEAD + own + HALO, :].astype(bf16)
        started.append(pltpu.make_async_copy(acc.at[pl.ds(LEAD, own)], grad_pairs.at[:, columns], sem))
    started.append(pltpu.make_async_copy(edge.at[0], grad_before, sem))
    started.append(pltpu.make_async_copy(edge.at[1], grad_after, sem))
    for copy in started:
        copy.start()
    for copy in started:
        copy.wait()


def cover(rows, passes):
    scores = 2 * rows * WINDOW
    return pl.CostEstimate(
        flops=4 * scores * PAIR, transcendentals=scores, bytes_accessed=passes * scores
    )


def any_specs(count):
    return [pl.BlockSpec(memory_space=pl.ANY)] * count


def attend(orders, info, bounds, qkv, before, after):
    micro_count, blocks, rows, _ = qkv.shape
    own = blocks * rows
    span = LEAD + own + LEAD
    stat_rows = micro_count * 2 * (own // WIDE)
    return pl.pallas_call(
        functools.partial(attend_kernel, orders),
        grid_spec=pltpu.PrefetchScalarGridSpec(
            num_scalar_prefetch=2,
            grid=(1,),
            in_specs=any_specs(3),
            out_specs=any_specs(1) + [pl.BlockSpec((stat_rows, WIDE), lambda g, a, b: (0, 0))],
            scratch_shapes=[
                pltpu.VMEM((micro_count, own, PAIR), bf16),
                pltpu.VMEM((micro_count, span, PAIR), bf16),
                pltpu.VMEM((micro_count, span, PAIR), bf16),
                pltpu.VMEM((micro_count, own, PAIR), f32),
                pltpu.VMEM((micro_count, own, PAIR), bf16),
                pltpu.VMEM((WINDOW, 2 * PAIR), bf16),
                pltpu.VMEM((2, HEAD_DIM + 16, WINDOW), bf16),
                pltpu.SemaphoreType.DMA,
            ],
        ),
        out_shape=[
            jax.ShapeDtypeStruct((blocks, micro_count, rows, PAIR), bf16),
            jax.ShapeDtypeStruct((stat_rows, WIDE), f32),
        ],
        cost_estimate=cover(micro_count * own, 30),
    )(info, bounds, qkv, before, after)


def attend_back(m, orders, info, bounds, qkv, before, after, mixed, grad_mixed, stats):
    _, blocks, rows, _ = qkv.shape
    own = blocks * rows
    span = LEAD + own + LEAD
    edge_rows = -(-HALO // rows) * rows
    return pl.pallas_call(
        functools.partial(attend_back_kernel, m, orders),
        grid_spec=pltpu.PrefetchScalarGridSpec(
            num_scalar_prefetch=2,
            grid=(1,),
            in_specs=any_specs(4 + blocks) + [pl.BlockSpec(stats.shape, lambda g, a, b: (0, 0))],
            out_specs=any_specs(4),
            scratch_shapes=[
                pltpu.VMEM((1, own, PAIR), bf16),
                pltpu.VMEM((1, span, PAIR), bf16),
                pltpu.VMEM((1, span, PAIR), bf16),
                pltpu.VMEM((own, PAIR), bf16),
                pltpu.VMEM((own, PAIR), bf16),
                pltpu.VMEM((WINDOW, 2 * PAIR), bf16),
                pltpu.VMEM((2, HEAD_DIM, WINDOW), bf16),
                pltpu.VMEM((own, PAIR), f32),
                pltpu.VMEM((span, PAIR), f32),
                pltpu.VMEM((span, PAIR), f32),
                pltpu.VMEM((2, edge_rows, 2 * PAIR), bf16),
                pltpu.SemaphoreType.DMA,
            ],
        ),
        out_shape=[
            jax.ShapeDtypeStruct((own, PAIR), f32),
            jax.ShapeDtypeStruct((own, 2 * PAIR), f32),
            jax.ShapeDtypeStruct((edge_rows, 2 * PAIR), bf16),
            jax.ShapeDtypeStruct((edge_rows, 2 * PAIR), bf16),
        ],
        cost_estimate=cover(own, 35),
    )(info, bounds, qkv, before, after, mixed, *grad_mixed, stats)


def join_kernel(order, info, query, pairs, head, tail, joined):
    blocks, rows, _ = joined.shape
    edge_blocks = head.shape[0] // rows
    for tile in range(blocks):
        here = pl.ds(tile * rows, rows)
        total = pairs[here, :]
        if tile < edge_blocks:
            total = total + head[here, :].astype(f32)
        if tile >= blocks - edge_blocks:
            total = total + tail[pl.ds((tile - (blocks - edge_blocks)) * rows, rows), :].astype(f32)
        target = position(jnp.bitwise_xor(info[1], tile), order)
        joined[target, :, :PAIR] = query[here, :].astype(bf16)
        joined[target, :, PAIR:] = total.astype(bf16)


def join_grads(order, info, grad_query, grad_pairs, head, tail, rows):
    own = grad_query.shape[0]
    blocks = own // rows
    ins = (grad_query, grad_pairs, head, tail)
    return pl.pallas_call(
        functools.partial(join_kernel, order),
        grid_spec=pltpu.PrefetchScalarGridSpec(
            num_scalar_prefetch=1,
            grid=(1,),
            in_specs=[pl.BlockSpec(item.shape, lambda g, i: (0, 0)) for item in ins],
            out_specs=pl.BlockSpec((blocks, rows, 3 * PAIR), lambda g, i: (0, 0, 0)),
        ),
        out_shape=jax.ShapeDtypeStruct((blocks, rows, 3 * PAIR), bf16),
    )(info, *ins)


def layer_norm_parts(values, gain, shift):
    center = values - jnp.mean(values, axis=-1, keepdims=True)
    inverse = lax.rsqrt(jnp.mean(center * center, axis=-1, keepdims=True) + epsilon)
    normal = center * inverse
    return (normal * gain + shift, normal, inverse)


def layer_norm_back(grad_normed, normal, inverse, gain):
    scaled = grad_normed * gain
    centered = scaled - jnp.mean(scaled, axis=-1, keepdims=True)
    return inverse * (centered - normal * jnp.mean(scaled * normal, axis=-1, keepdims=True))


class PlaneScatter:
    def __init__(self, partial, held, order):
        self.pieces = [partial[position(r, held)].astype(bf16) for r in range(PLANE)]
        self.left = list(range(PLANE))
        self.order = list(order)

    def start(self, *earlier):
        self.bit = self.order.pop(0)
        self.keep = [r for r in self.left if not r & self.bit]
        self.send = jnp.stack([self.pieces[r | self.bit] for r in self.keep])
        if earlier:
            self.send = tie(self.send, *earlier)
        self.got = swap(self.send, self.bit)

    def finish(self):
        for position, r in enumerate(self.keep):
            added = self.pieces[r].astype(f32) + self.got[position].astype(f32)
            self.pieces[r] = added.astype(bf16) if self.order else added
        self.left = self.keep


def body(
    tokens,
    ln1_gain,
    ln1_bias,
    qkv_weight,
    q_bias,
    v_bias,
    out_weight,
    out_bias,
    ln2_gain,
    ln2_bias,
    fc1_weight,
    fc1_bias,
    fc2_weight,
    fc2_bias,
    image_ids,
    image_starts,
    cotangent,
):
    micro_count, tok_dev, model_width = tokens.shape
    n = lax.axis_size("seq")
    own_tokens = micro_count * tok_dev
    plane_rows = PLANE * tok_dev
    stream_len = tok_dev * n
    me = lax.axis_index("seq")
    mine = jnp.bitwise_and(me, PLANE - 1)
    base = (me - mine) * tok_dev
    info = jnp.stack([me, mine, base]).astype(jnp.int32)
    bounds = jnp.concatenate(
        [image_starts, jnp.full((micro_count, 1), stream_len, jnp.int32)], axis=1
    )
    plane_bits = [1, 2, 4]
    depth_bits = []
    bit = PLANE
    while bit < n:
        depth_bits.append(bit)
        bit *= 2

    small = [ln1_gain, ln1_bias, q_bias, v_bias, out_bias, ln2_gain, ln2_bias, fc2_bias, fc1_bias]
    shard_rows = qkv_weight.shape[0]
    small_len = sum(item.shape[0] for item in small)
    spare_rows = -(-small_len // (8 * 3 * PAIR)) * 8
    narrow = small[0].shape[0]
    small_rows = jnp.concatenate([item.reshape(-1, narrow) for item in small], axis=0)
    used = small_rows.shape[0]
    small_rows = jnp.pad(small_rows, ((0, -used % 16), (0, 3 * PAIR - narrow)))
    by_pair = qkv_weight.reshape(shard_rows, 3, PLANE, PAIR).transpose(2, 0, 1, 3)
    by_pair = by_pair.reshape(PLANE, shard_rows, 3 * PAIR)
    outgoing = jnp.concatenate(
        [by_pair, jnp.broadcast_to(small_rows[None], (PLANE,) + small_rows.shape)], axis=1
    )
    arrived = exchange(outgoing[jnp.bitwise_xor(mine, jnp.arange(PLANE))])

    token_orders = [[2, 4, 1] if m % 2 == 0 else [4, 2, 1] for m in range(micro_count)]
    gathered = [tokens[m][None] for m in range(micro_count)]
    current = arrived
    for k in range(3):
        got = [swap(item, token_orders[m][k]) for m, item in enumerate(gathered)]
        if k == 1:
            current = current[None]
            for bit in depth_bits[::-1]:
                current = jnp.stack([current, swap(current, bit)], axis=1)
                current = current.reshape((-1,) + arrived.shape)
            current = current.reshape((n,) + arrived.shape[1:])
            early = got + [current]
            got[0] = tie(got[0], current)
        gathered = [jnp.concatenate(pair, axis=0) for pair in zip(gathered, got)]

    step = out_weight.shape[0]
    wide_parts = fc1_weight.shape[1] // model_width
    shards = [out_weight]
    shards += [fc1_weight[:, k * model_width : (k + 1) * model_width] for k in range(wide_parts)]
    packed = tie(jnp.concatenate(shards + [fc2_weight], axis=0), *early)
    every = lax.all_gather(packed, "seq")
    out_full = every[:, :step].reshape(model_width, model_width)
    ups = [every[:, (1 + k) * step : (2 + k) * step].reshape(model_width, -1) for k in range(wide_parts)]
    share = n // wide_parts
    downs = [
        every[k * share : (k + 1) * share, (1 + wide_parts) * step :].reshape(-1, model_width)
        for k in range(wide_parts)
    ]

    pair_blocks = turn_blocks(info, current)
    pair_weight = pair_blocks[:, :shard_rows].reshape(n * shard_rows, 3 * PAIR)
    small_all = pair_blocks[:, shard_rows : shard_rows + used, :narrow].astype(f32)
    small_full = [small_all[:, k].reshape(-1) for k in range(len(small) - 1)]
    small_full.append(small_all[:, len(small) - 1 :].reshape(-1))
    gain_one, shift_one, q_shift, v_shift, out_shift, gain_two, shift_two, down_shift, up_shift = small_full

    plane_stream = jnp.stack(gathered)
    plane_flat = plane_stream.reshape(micro_count * plane_rows, model_width)
    normed, _, _ = layer_norm_parts(plane_flat.astype(f32), gain_one, shift_one)
    normed_low = normed.astype(bf16)
    pair_shift = jnp.concatenate(
        [
            lax.dynamic_slice_in_dim(q_shift, mine * PAIR, PAIR),
            jnp.zeros((PAIR,), f32),
            lax.dynamic_slice_in_dim(v_shift, mine * PAIR, PAIR),
        ]
    )
    qkv = (product(normed_low, pair_weight) + pair_shift).astype(bf16)
    qkv = qkv.reshape(micro_count, PLANE, tok_dev, 3 * PAIR)

    edge_blocks = -(-HALO // tok_dev)

    def plane_block(index):
        offset = jnp.bitwise_xor(mine, index)
        blocks = [pick(qkv[m], 0, position(offset, order)) for m, order in enumerate(token_orders)]
        return jnp.stack(blocks)[:, :, PAIR:]

    last_rows = jnp.concatenate([plane_block(PLANE - edge_blocks + k) for k in range(edge_blocks)], axis=1)
    first_rows = jnp.concatenate([plane_block(k) for k in range(edge_blocks)], axis=1)
    before = shift_plane(last_rows[:, edge_blocks * tok_dev - HALO :], 1)
    after = shift_plane(first_rows[:, :HALO], -1)
    mixed_pair, stats = attend(token_orders, info, bounds, qkv, before, after)
    stats = stats.reshape(-1, TILE)

    def column(r):
        return jnp.bitwise_xor(mine, r) * PAIR

    mixed_low = jnp.zeros((own_tokens, model_width), bf16)
    for r in range(PLANE):
        part = mixed_pair[r] if r == 0 else swap(mixed_pair[r], r)
        mixed_low = lax.dynamic_update_slice(mixed_low, part.reshape(own_tokens, PAIR), (0, column(r)))

    stream = tokens.reshape(own_tokens, model_width).astype(f32)
    cotangent_low = cotangent.reshape(own_tokens, model_width)
    middle = stream + product(mixed_low, out_full) + out_shift
    normed_two, normal_two, inverse_two = layer_norm_parts(middle, gain_two, shift_two)
    normed_two_low = normed_two.astype(bf16)
    up_shifts = up_shift.reshape(wide_parts, model_width)
    actives, grad_hiddens = [], []
    for k in range(wide_parts):
        hidden = product(normed_two_low, ups[k]) + up_shifts[k]
        gate = jax.nn.sigmoid(1.702 * hidden)
        actives.append((hidden * gate).astype(bf16))
        grad_active = product_nt(cotangent_low, downs[k])
        grad_hiddens.append((grad_active * (gate + 1.702 * hidden * gate * (1.0 - gate))).astype(bf16))

    def by_device(partial, devices=n):
        return partial.astype(bf16).reshape(devices, -1, model_width)

    order_a = [1, 2, 4] + depth_bits
    order_b = [1, 4, 2] + depth_bits
    grad_downs = [by_device(product_tn(active, cotangent_low), share) for active in actives]
    half = grad_downs[0].shape[1] // 2
    down = [
        Scatter(me, [[item[:, :half] for item in grad_downs]], [1] + depth_bits[:1] + [2, 4] + depth_bits[1:]),
        Scatter(me, [[item[:, half:] for item in grad_downs]], [1] + depth_bits[:1] + [4, 2] + depth_bits[1:]),
    ]
    for part in down:
        part.swap()
    grad_hiddens[0] = tie(grad_hiddens[0], *[part.send for part in down])

    grad_normed_two = product_nt(grad_hiddens[0], ups[0])
    for k in range(1, wide_parts):
        grad_normed_two = grad_normed_two + product_nt(grad_hiddens[k], ups[k])
    for part in down:
        part.advance(grad_normed_two)
    grad_normed_two = tie(grad_normed_two, *[part.send for part in down])
    grad_middle = cotangent_low.astype(f32) + layer_norm_back(
        grad_normed_two, normal_two, inverse_two, gain_two
    )
    grad_branch_low = grad_middle.astype(bf16)
    grad_mixed_low = product_nt(grad_branch_low, out_full).astype(bf16)
    grad_parts = []
    for r in range(PLANE):
        part = lax.dynamic_slice(grad_mixed_low, (0, column(r)), (own_tokens, PAIR))
        part = part.reshape(micro_count, tok_dev, PAIR)
        grad_parts.append(part if r == 0 else swap(part, r))

    later = tie(normed_two_low, grad_mixed_low)
    grad_ups = [by_device(product_tn(later, grad_hidden)) for grad_hidden in grad_hiddens]
    grad_out_weight = by_device(product_tn(mixed_low, grad_branch_low))
    mid = wide_parts // 2
    up = [
        Scatter(me, [[item] for item in grad_ups[:mid] + [grad_out_weight[:, : step // 2]]], order_a),
        Scatter(me, [[item] for item in grad_ups[mid:] + [grad_out_weight[:, step // 2 :]]], order_b),
    ]
    for part in up:
        part.swap()
    result = middle + down_shift
    after_up = tie(actives[0], *[part.send for part in up])
    for k in range(wide_parts):
        result = result + product(after_up if k == 0 else actives[k], downs[k])
    result_low = result.astype(bf16)
    for part in up:
        part.advance(result_low, *grad_parts)

    before_back = [part.send for part in up]
    grad_planes = []
    grad_pair_weight, column_sum = 0.0, 0.0
    for m in range(micro_count):
        own_grad = tie(grad_parts[0], *before_back)
        grad_query, grad_pairs, grad_before, grad_after = attend_back(
            m, token_orders, info, bounds, qkv, before, after, mixed_pair, [own_grad] + grad_parts[1:], stats
        )
        from_next = shift_plane(grad_before, -1)
        from_last = shift_plane(grad_after, 1)
        for plane in grad_planes:
            plane.got = tie(plane.got, grad_before)
            plane.finish()
            plane.start()
        for part in up + down:
            part.advance(grad_before)
        sends = [part.send for part in up + down] + [plane.send for plane in grad_planes]
        grad_query = tie(grad_query, *sends)
        joined = join_grads(token_orders[m], info, grad_query, grad_pairs, from_last, from_next, tok_dev)
        grad_flat = joined.reshape(plane_rows, 3 * PAIR)
        grad_plane = product_nt(grad_flat, pair_weight).reshape(PLANE, tok_dev, model_width)
        order = [1, 2, 4] if m % 2 == 0 else [1, 4, 2]
        plane = PlaneScatter(grad_plane, token_orders[m], order)
        plane.start()
        grad_flat = tie(grad_flat, plane.send)
        rows = normed_low[m * plane_rows : (m + 1) * plane_rows]
        added = product_tn(rows, grad_flat)
        grad_pair_weight = grad_pair_weight + added
        column_sum = column_sum + jnp.sum(grad_flat.astype(f32), axis=0)
        if m < micro_count - 1:
            plane.got = tie(plane.got, added)
        plane.finish()
        plane.start()
        grad_planes.append(plane)
        before_back = [plane.send]
    grad_pair_weight = tie(grad_pair_weight, plane.send)

    wide = pair_weight.astype(f32)
    grad_shift_one = jnp.sum(wide * column_sum, axis=1)
    grad_gain_one = jnp.sum(wide * grad_pair_weight, axis=1)
    grad_gain_one = (grad_gain_one - shift_one * grad_shift_one) / gain_one

    def at_columns(part):
        return lax.dynamic_update_slice(jnp.zeros((model_width,), f32), part, (mine * PAIR,))

    small_grads = [
        grad_gain_one,
        grad_shift_one,
        at_columns(column_sum[:PAIR]),
        at_columns(column_sum[2 * PAIR :]),
        jnp.sum(grad_branch_low.astype(f32), axis=0),
        jnp.sum(grad_normed_two * normal_two, axis=0),
        jnp.sum(grad_normed_two, axis=0),
        jnp.sum(cotangent_low.astype(f32), axis=0),
        jnp.concatenate([jnp.sum(item.astype(f32), axis=0) for item in grad_hiddens]),
    ]
    small_out = jnp.concatenate([item.reshape(n, -1) for item in small_grads], axis=1).astype(bf16)
    small_out = jnp.pad(small_out, ((0, 0), (0, spare_rows * 3 * PAIR - small_len)))
    small_out = small_out.reshape(n, spare_rows, 3 * PAIR)
    leaving = jnp.concatenate(
        [grad_pair_weight.astype(bf16).reshape(n, shard_rows, 3 * PAIR), small_out], axis=1
    )
    turned = turn_blocks(info, leaving)

    turned = turned.reshape((n // PLANE, PLANE) + turned.shape[1:])
    for index, bit in enumerate(depth_bits):
        turned = turned.reshape((-1, 2) + turned.shape[1:])
        sent = turned[:, 1]
        got = swap(sent, bit)
        if index == 0:
            plane = grad_planes[-1]
            plane.got = tie(plane.got, sent)
            plane.finish()
            plane.start()
            for part in up + down:
                if part.order:
                    part.advance(sent, plane.send)
            got = tie(got, *[part.send for part in up + down])
        turned = (turned[:, 0].astype(f32) + got.astype(f32)).astype(bf16)
    turned = turned.reshape((PLANE,) + turned.shape[2:])
    for plane in grad_planes:
        plane.finish()
    grad_normed = jnp.concatenate([plane.pieces[0] for plane in grad_planes], axis=0)
    _, normal_one, inverse_one = layer_norm_parts(stream, gain_one, shift_one)
    grad_stream = grad_middle + layer_norm_back(grad_normed, normal_one, inverse_one, gain_one)
    stream_low = grad_stream.astype(bf16)
    for part in up + down:
        while part.order:
            part.advance(stream_low)
    down_sum = jnp.concatenate([part.total() for part in down], axis=0)
    up_totals = [part.total() for part in up]
    out_sum = jnp.concatenate([total[mid * step :] for total in up_totals], axis=0)
    up_sum = jnp.concatenate([total[: mid * step] for total in up_totals], axis=0)
    up_sum = jnp.concatenate([up_sum[k * step : (k + 1) * step] for k in range(wide_parts)], axis=1)
    back = exchange(tie(turned, *[plane.pieces[0] for plane in grad_planes])).astype(f32)
    qkv_sum = jnp.zeros((shard_rows, 3, model_width), f32)
    for r in range(PLANE):
        columns = back[r, :shard_rows].reshape(shard_rows, 3, PAIR)
        qkv_sum = lax.dynamic_update_slice(qkv_sum, columns, (0, 0, column(r)))
    small_sum = jnp.sum(back[:, shard_rows:], axis=0)
    qkv_sum = qkv_sum.reshape(shard_rows, 3 * model_width)
    small_sum = small_sum.reshape(-1)
    sums = []
    offset = 0
    for item in small:
        sums.append(small_sum[offset : offset + item.shape[0]])
        offset += item.shape[0]

    return (
        result_low.reshape(micro_count, tok_dev, model_width),
        stream_low.reshape(micro_count, tok_dev, model_width),
        sums[0],
        sums[1],
        qkv_sum,
        sums[2],
        sums[3],
        out_sum,
        sums[4],
        sums[5],
        sums[6],
        up_sum,
        sums[8],
        down_sum,
        sums[7],
    )


def solution(mesh):
    return jax.shard_map(
        body,
        mesh=mesh,
        in_specs=(
            P(None, "seq", None),
            P("seq"),
            P("seq"),
            P("seq", None),
            P("seq"),
            P("seq"),
            P("seq", None),
            P("seq"),
            P("seq"),
            P("seq"),
            P("seq", None),
            P("seq"),
            P("seq", None),
            P("seq"),
            P(None, "seq"),
            P(),
            P(None, "seq", None),
        ),
        out_specs=(
            P(None, "seq", None),
            P(None, "seq", None),
            P("seq"),
            P("seq"),
            P("seq", None),
            P("seq"),
            P("seq"),
            P("seq", None),
            P("seq"),
            P("seq"),
            P("seq"),
            P("seq", None),
            P("seq"),
            P("seq", None),
            P("seq"),
        ),
        check_vma=False,
    )
```
